256 devices in a mesh: dp: 32 (over z, x), pipe: 2 (over core), tensor: 4 (over y).
Axes of the slice: x: 4, y: 4, z: 8, core: 2. Of those that a mesh axis runs over, the one named last changes fastest.
Arguments:
- tokens: bfloat16 [64, 64, 4096], P('dp', None, 'tensor'), may hold values from -8 to 8
- w_query: bfloat16 [2, 2, 4096, 4096], P(None, 'pipe', 'dp', 'tensor'), may hold values from -8 to 8
- w_key: bfloat16 [2, 2, 4096, 1024], P(None, 'pipe', 'dp', 'tensor'), may hold values from -1 to 1
- w_value: bfloat16 [2, 2, 4096, 1024], P(None, 'pipe', 'dp', 'tensor'), may hold values from -0.09375 to 0.09375
- w_out: bfloat16 [2, 2, 4096, 4096], P(None, 'pipe', 'tensor', 'dp'), may hold values from -0.09375 to 0.09375
- norm_gain: float32 [2, 2, 4096], P(None, 'pipe'), may hold values from 0.5 to 1.5
- boundary: int32 [64], P('dp'), may hold values from 1 to 63
- skip_offset: int32 [64], P('dp'), may hold values from 0 to 131008
- doc_lengths: int32 [64, 4], P('dp'), may hold values from 1 to 32, 64 in all within a row
- batch_order: int32 [32, 2], P('dp'), may hold values from 0 to 1, each once within a row
Outputs:
- final_state: bfloat16 [64, 64, 4096], P('dp', 'pipe', 'tensor')
The draws below stay inside these ranges and needn't reach their ends.
Inputs may be any that keep to these rules, and one draw needn't show every extreme that they name: `doc_lengths`: each row sums to 64. `batch_order`: each row is a permutation.
All inputs are finite; a program needn't handle non-finite values.
Results may differ from the reference program's by a relative error of at most 0.014.
Values may be sent and summed in bfloat16 or wider, within the bound.
A program may use at most 192 MiB of HBM per device.

```python
import math
from functools import partial
import jax
import jax.numpy as jnp
import numpy as np
from jax import lax

D = 4096
HEADS = 32
KV_HEADS = 8
HEAD_DIM = 128
SEQ = 64
MICRO = 2
DOCS = 4
POSITIONS = 131072
SECTIONS = 2
BATCH = 64
N_DP = 32


def draw_tokens(key, part):
    random_part = jax.random.normal(jax.random.fold_in(key, 11), (BATCH, SEQ, D), jnp.float32)
    return jnp.clip(random_part, -6.0, 6.0).astype(jnp.bfloat16)


def draw_w_query(key, part):
    raw_draw = jax.random.normal(jax.random.fold_in(key, 21), (2, SECTIONS, D, HEADS, HEAD_DIM), jnp.float32)
    values = jnp.clip(raw_draw, -6.0, 6.0) / jnp.sqrt(jnp.float32(D))
    return values.reshape(2, SECTIONS, D, HEADS * HEAD_DIM).astype(jnp.bfloat16)


def draw_w_key(key, part):
    raw_draw = jax.random.normal(jax.random.fold_in(key, 31), (2, SECTIONS, D, KV_HEADS, HEAD_DIM), jnp.float32)
    values = jnp.clip(raw_draw, -6.0, 6.0) / jnp.sqrt(jnp.float32(D))
    values = jnp.clip(values, -1.0, 1.0)
    return values.reshape(2, SECTIONS, D, KV_HEADS * HEAD_DIM).astype(jnp.bfloat16)


def with_ends(array, stream_key, low, high):
    dims = array.shape
    index_at = [jax.random.randint(jax.random.fold_in(stream_key, axis), (), 0, dims[axis]) for axis in range(len(dims))]
    array = array.at[tuple(index_at)].set(low)
    longest = dims.index(max(dims))
    index_at[longest] = (index_at[longest] + 1) % dims[longest]
    return array.at[tuple(index_at)].set(high)


def shard_levels(stream_key, shape, pieces, least, largest):
    loudness = 1.0
    for position, shards_of in pieces:
        draws = jax.random.uniform(jax.random.fold_in(jax.random.fold_in(stream_key, 6), position), (shards_of,), jnp.float32, least / len(pieces), largest / len(pieces))
        loudness = loudness * jnp.repeat(jnp.exp(draws), shape[position] // shards_of).reshape((-1,) + (1,) * (len(shape) - 1 - position))
    return loudness


def split_up(amount, total, reach, skew):
    portions = [(1 << 20) // math.isqrt(standing ** skew) + 1 for standing in range(2, amount + 1)]
    spare, counts = total - reach - (amount - 1), [1] * (amount - 1)
    while spare > 0:
        free = [i for i in range(amount - 1) if counts[i] < reach]
        mass, left = sum([portions[i] for i in free]), spare
        for i in free:
            addition = min(reach - counts[i], max(1, left * portions[i] // mass), spare)
            counts[i] = counts[i] + addition
            spare = spare - addition
    return np.array([reach] + counts)


def uneven(own_key, number_of, total, limit, slope):
    if number_of == 2:
        one = jax.random.randint(own_key, (), max(1, total - limit), min(limit, total - 1) + 1)
        return jnp.stack([one, total - one])
    tallies = jnp.asarray(split_up(number_of, total, limit, slope), jnp.int32)
    pairs = (number_of - 1) // 2
    giver, sink = tallies[1:1 + 2 * pairs:2], tallies[2:2 + 2 * pairs:2]
    slack = jnp.minimum(giver - 1, limit - sink)
    passed = jax.random.randint(jax.random.fold_in(own_key, 1), (pairs,), 0, 1 << 20) % (slack + 1)
    tallies = tallies.at[1:1 + 2 * pairs:2].set(giver - passed).at[2:2 + 2 * pairs:2].set(sink + passed)
    return tallies[jax.random.permutation(jax.random.fold_in(own_key, 2), number_of)]


def centred(stream_key, shape, width, bound, split=(), held_as=jnp.bfloat16):
    factor_of = shard_levels(stream_key, shape, split, -0.22, 0.18) if split else 1.0
    entries = jax.random.normal(stream_key, shape, jnp.float32) * width * factor_of
    return jnp.minimum(jnp.maximum(entries, -bound), bound).astype(held_as)


def setup_inputs(seed: int = 0) -> dict:
    arg_keys = jax.random.split(jax.random.key(seed), 11)
    return {
        "tokens": draw_tokens(jax.random.fold_in(arg_keys[10], 71), 0),
        "w_query": draw_w_query(jax.random.fold_in(arg_keys[10], 71), 0),
        "w_key": draw_w_key(jax.random.fold_in(arg_keys[10], 71), 0),
        "w_value": centred(arg_keys[3], (2, SECTIONS, D, KV_HEADS * HEAD_DIM), D ** -0.5, 0.09375, ((1, 2), (2, 32), (3, 4))),
        "w_out": centred(arg_keys[4], (2, SECTIONS, HEADS * HEAD_DIM, D), (HEADS * HEAD_DIM) ** -0.5, 0.09375, ((1, 2), (2, 4), (3, 32))),
        "norm_gain": jnp.clip(1.0 + 0.1 * jax.random.normal(arg_keys[5], (2, SECTIONS, D), jnp.float32), 0.5, 1.5),
        "boundary": with_ends(jax.random.randint(arg_keys[6], (BATCH,), 1, SEQ), jax.random.fold_in(arg_keys[6], 1), 1, SEQ - 1).astype(jnp.int32),
        "skip_offset": with_ends(jax.random.randint(arg_keys[7], (BATCH,), 0, POSITIONS - SEQ + 1), jax.random.fold_in(arg_keys[7], 1), 0, POSITIONS - SEQ).astype(jnp.int32),
        "doc_lengths": jax.vmap(lambda own: uneven(own, DOCS, SEQ, SEQ // 2, 1))(jax.random.split(arg_keys[8], BATCH)).reshape((BATCH, DOCS)).astype(jnp.int32),
        "batch_order": jax.vmap(lambda own: jax.random.permutation(own, MICRO))(jax.random.split(arg_keys[9], N_DP)).reshape((N_DP, MICRO)).astype(jnp.int32),
    }


ROPE_THETA = 500000.0
NORM_EPSILON = 1e-05

def rope_angles(positions, head_dim):
    half_dim = head_dim // 2
    exponent = jnp.arange(half_dim, dtype=jnp.float32) * (2.0 / head_dim)
    frequency = jnp.float32(ROPE_THETA) ** (-exponent)
    return positions.astype(jnp.float32)[..., None] * frequency

def rotate(values, angles):
    half_dim = values.shape[-1] // 2
    first_half = values[..., :half_dim]
    second = values[..., half_dim:]
    cosine = jnp.cos(angles)[:, None, :]
    sine_part = jnp.sin(angles)[:, None, :]
    return jnp.concatenate([first_half * cosine - second * sine_part, second * cosine + first_half * sine_part], axis=-1)

def sample_layout(first_cut, offset, lengths, seq_len):
    places = jnp.arange(seq_len, dtype=jnp.int32)
    positions = jnp.where(places < first_cut, places, places + offset).astype(jnp.int32)
    doc_ends = jnp.cumsum(lengths).astype(jnp.int32)
    doc_ids = lax.optimization_barrier(jnp.sum((places[:, None] >= doc_ends[None, :]).astype(jnp.int32), axis=1))
    allowed = (doc_ids[:, None] == doc_ids[None, :]) & (places[None, :] <= places[:, None])
    return (positions, allowed)

def attend(normed, q_weight, k_weight, v_weight, angles, allowed):
    seq_len = normed.shape[0]
    q_heads = q_weight.shape[1] // HEAD_DIM
    kv_heads = k_weight.shape[1] // HEAD_DIM
    group_size = q_heads // kv_heads
    queries = jnp.dot(normed, q_weight, preferred_element_type=jnp.float32)
    key_vecs = jnp.dot(normed, k_weight, preferred_element_type=jnp.float32)
    value_vecs = jnp.dot(normed, v_weight, preferred_element_type=jnp.float32).astype(jnp.bfloat16)
    value_vecs = value_vecs.reshape(seq_len, kv_heads, HEAD_DIM)
    queries = rotate(queries.reshape(seq_len, q_heads, HEAD_DIM), angles).astype(jnp.bfloat16)
    queries = queries.reshape(seq_len, kv_heads, group_size, HEAD_DIM)
    key_vecs = rotate(key_vecs.reshape(seq_len, kv_heads, HEAD_DIM), angles).astype(jnp.bfloat16)
    scores = jnp.einsum('skgd,tkd->kgst', queries.astype(jnp.float32), key_vecs.astype(jnp.float32)) * HEAD_DIM ** (-0.5)
    scores = jnp.where(allowed[None, None], scores, -jnp.inf)
    row_max = lax.optimization_barrier(jnp.max(scores, axis=-1, keepdims=True))
    exp_scores = jnp.exp(scores - row_max)
    weights = (exp_scores / lax.optimization_barrier(jnp.sum(exp_scores, axis=-1, keepdims=True))).astype(jnp.bfloat16)
    mixed = jnp.einsum('kgst,tkd->skgd', weights.astype(jnp.float32), value_vecs.astype(jnp.float32))
    return mixed.reshape(seq_len, q_heads * HEAD_DIM)

def layer_step(stream, gain_row, q_weight, k_weight, v_weight, o_weight, angles, allowed):
    widened = stream.astype(jnp.float32)
    inv_rms = lax.rsqrt(lax.optimization_barrier(jnp.mean(widened * widened, axis=-1, keepdims=True)) + NORM_EPSILON)
    normed = (widened * inv_rms * gain_row).astype(jnp.bfloat16)
    mixed = attend(normed, q_weight, k_weight, v_weight, angles, allowed).astype(jnp.bfloat16)
    projected = jnp.dot(mixed, o_weight, preferred_element_type=jnp.float32)
    return (widened + projected).astype(jnp.bfloat16)

def chained(stacked):
    return jnp.concatenate([stacked[0], stacked[1][::-1]], axis=0)

def reference(tokens, w_query, w_key, w_value, w_out, norm_gain, boundary, skip_offset, doc_lengths, batch_order):
    row_index = (jnp.arange(N_DP, dtype=jnp.int32)[:, None] * MICRO + batch_order.astype(jnp.int32)).reshape(-1).astype(jnp.int32)
    stream = jnp.take(tokens, row_index, axis=0)
    positions, allowed = jax.vmap(partial(sample_layout, seq_len=SEQ))(jnp.take(boundary, row_index), jnp.take(skip_offset, row_index), jnp.take(doc_lengths, row_index, axis=0))
    angles = rope_angles(positions, HEAD_DIM)
    layers = (chained(norm_gain), chained(w_query), chained(w_key), chained(w_value), chained(w_out))

    def advance(current, layer_weights):
        gain_row, q_weight, k_weight, v_weight, o_weight = layer_weights

        def per_sample(sample_rows, sample_angles, sample_allowed):
            return layer_step(sample_rows, gain_row, q_weight, k_weight, v_weight, o_weight, sample_angles, sample_allowed)
        return (jax.vmap(per_sample)(current, angles, allowed), None)
    stream, unused = lax.scan(advance, stream, layers)
    return stream
```

```python
from functools import partial

import jax
import jax.numpy as jnp
from jax import lax
from jax.experimental import pallas as pl
from jax.experimental.pallas import tpu as pltpu
from jax.sharding import PartitionSpec as P

HEAD_DIM = 128
ROPE_THETA = 500000.0
NORM_EPSILON = 1e-05
MESH = pl.DeviceIdType.MESH

LAYERS = 4
NZ, NX, NY = 8, 4, 4
SEQ = 64
WIDTH = 4096
CHUNK = 128
SET = NZ * CHUNK
QKV = 1536
HEADS = 1024
EXTRA = QKV + 128
TOK = NX * SEQ
PIECE = SET // NY


def rope_angles(positions, head_dim):
    half_dim = head_dim // 2
    exponent = jnp.arange(half_dim, dtype=jnp.float32) * (2.0 / head_dim)
    frequency = jnp.float32(ROPE_THETA) ** (-exponent)
    return positions.astype(jnp.float32)[..., None] * frequency


def sample_layout(first_cut, offset, lengths, seq_len):
    places = jnp.arange(seq_len, dtype=jnp.int32)
    positions = jnp.where(places < first_cut, places, places + offset)
    doc_ends = jnp.cumsum(lengths)
    doc_ids = jnp.sum((places[:, None] >= doc_ends[None, :]).astype(jnp.int32), axis=1)
    allowed = (doc_ids[:, None] == doc_ids[None, :]) & (places[None, :] <= places[:, None])
    return (positions, allowed)


def stack_kernel(
    xtok,
    cosines,
    sines,
    bias,
    gain,
    wq,
    wk,
    wv,
    wo,
    out,
    wqkv,
    wob,
    gbuf,
    tsend,
    xbuf,
    xg,
    psend,
    precv,
    abuf,
    osend,
    oown,
    orecv,
    frecv,
    lsem,
    hop_s,
    hop_r,
    own_s,
    own_r,
    par_s,
    par_r,
    g_s,
    g_r,
    t_s,
    t_r,
    x_s,
    x_r,
    p_s,
    p_r,
    a_s,
    a_r,
    o_s,
    o_r,
    f_s,
    f_r,
):
    dp = lax.axis_index("dp")
    p = lax.axis_index("pipe")
    y = lax.axis_index("tensor")
    z = dp // NX
    x = dp % NX
    step = 1 - 2 * p

    def at(zz, xx, pp, yy):
        return {"dp": zz * NX + xx, "pipe": pp, "tensor": yy}

    def zrel(k):
        return (z + step * k + NZ) % NZ

    down = at(zrel(1), x, p, y)
    up = at(zrel(-1), x, p, y)
    other = at(z, x, 1 - p, y)

    def remote(src, dst, s, r, dev):
        return pltpu.make_async_remote_copy(
            src_ref=src, dst_ref=dst, send_sem=s, recv_sem=r, device_id=dev, device_id_type=MESH
        )

    def layer_of(d):
        return p + d * (3 - 2 * p)

    def rows_of(zz):
        return pl.ds(pl.multiple_of(zz * CHUNK, CHUNK), CHUNK)

    def loads(d):
        c = layer_of(d)
        r = rows_of(z)
        return [
            pltpu.make_async_copy(wq.at[d, 0], wqkv.at[c, r, pl.ds(0, 1024)], lsem.at[d, 0]),
            pltpu.make_async_copy(wk.at[d, 0], wqkv.at[c, r, pl.ds(1024, 256)], lsem.at[d, 1]),
            pltpu.make_async_copy(wv.at[d, 0], wqkv.at[c, r, pl.ds(1280, 256)], lsem.at[d, 2]),
            pltpu.make_async_copy(wo.at[d, 0], wob.at[c, :, r], lsem.at[d, 3]),
        ]

    for d in range(2):
        for copy in loads(d):
            copy.start()

    barrier = pltpu.get_barrier_semaphore()
    peers = [down, up, other]
    for i in (1, 2, 3):
        peers.append(at(z, (x + i) % NX, p, y))
        peers.append(at(z, (x + i) % NX, 1 - p, y))
        peers.append(at(z, x, p, (y + i) % NY))
    for dev in peers:
        pl.semaphore_signal(barrier, inc=1, device_id=dev, device_id_type=MESH)
    pl.semaphore_wait(barrier, len(peers))

    def piece(c, zz, t, half):
        if t == 0:
            return wqkv.at[c, pl.ds(pl.multiple_of(zz * CHUNK + half * 64, 64), 64), :]
        return wob.at[c, pl.ds(pl.multiple_of(half * 512, 512), 512), rows_of(zz)]

    def whole(c, zz, t):
        if t == 0:
            return wqkv.at[c, rows_of(zz), :]
        return wob.at[c, :, rows_of(zz)]

    def hop_out(c, t, half, h):
        ref = piece(c, zrel(1 - h), t, half)
        return remote(ref, ref, hop_s.at[c, t, half, h - 1], hop_r.at[c, t, half, h - 1], down)

    def hop_in(c, t, half, h):
        ref = piece(c, zrel(-h), t, half)
        return remote(ref, ref, hop_s.at[c, t, half, h - 1], hop_r.at[c, t, half, h - 1], up)

    def swap_out(c, t, half, h):
        ref = piece(c, zrel(-h), t, half)
        return remote(ref, ref, par_s.at[c, t, half, h - 1], par_r.at[c, t, half, h - 1], other)

    def swap_in(c, t, half, h):
        ref = piece(c, zrel(h), t, half)
        return remote(ref, ref, par_s.at[c, t, half, h - 1], par_r.at[c, t, half, h - 1], other)

    def own_swap(c, t):
        ref = whole(c, z, t)
        return remote(ref, ref, own_s.at[c, t], own_r.at[c, t], other)

    def holder(c):
        return jnp.where((c == 0) | (c == 3), 0, 1)

    def first_hop(c):
        for t in range(2):

            @pl.when(p != holder(c))
            def _():
                own_swap(c, t).wait_recv()

            for half in range(2):
                hop_out(c, t, half, 1).start()

    def forward(c, h):
        for t in range(2):
            for half in range(2):
                hop_in(c, t, half, h).wait_recv()
                if h < 3:
                    hop_out(c, t, half, h + 1).start()
                swap_out(c, t, half, h).start()
            if h == 3:
                hop_out(c, t, p, 4).start()

    def finish(c):
        for t in range(2):
            hop_in(c, t, p, 4).wait_recv()
            swap_out(c, t, p, 4).start()

    def ready(c, t):
        for h in (1, 2, 3):
            for half in range(2):
                swap_in(c, t, half, h).wait_recv()
        swap_in(c, t, 1 - p, 4).wait_recv()

    def load_and_share(d):
        for copy in loads(d):
            copy.wait()
        for t in range(2):
            own_swap(layer_of(d), t).start()

    load_and_share(0)
    first_hop(0)

    for xx in range(NX):
        tsend[xx, :, 0:128] = xtok[:, xx * 128 : xx * 128 + 128]
        tsend[xx, :, 128:256] = xtok[:, 512 + xx * 128 : 512 + xx * 128 + 128]

    def block(ref, b, size):
        return ref.at[pl.ds(pl.multiple_of(b * size, size), size), :]

    def tok_out(i):
        xx = (x + i) % NX
        return remote(
            tsend.at[xx], block(xbuf.at[0, y], x, SEQ), t_s.at[xx], t_r.at[x], at(z, xx, p, y)
        )

    def tok_in(i):
        xx = (x + i) % NX
        return remote(
            tsend.at[xx], block(xbuf.at[0, y], xx, SEQ), t_s.at[xx], t_r.at[xx], at(z, xx, p, y)
        )

    for i in (2, 1, 3):
        tok_out(i).start()
    xbuf[0, y, pl.ds(pl.multiple_of(x * SEQ, SEQ), SEQ), :] = tsend[x]

    load_and_share(1)

    for d in range(2):
        c = layer_of(d)
        for zz in range(NZ):
            row = gain[d, :, pl.ds(pl.multiple_of((zz * NX + x) * CHUNK, CHUNK), CHUNK)]
            gbuf[c, :, zz * CHUNK : zz * CHUNK + CHUNK] = jnp.broadcast_to(row, (8, CHUNK))

    def gain_swap(d, c):
        return remote(gbuf.at[c], gbuf.at[c], g_s.at[d], g_r.at[d], other)

    for d in range(2):
        gain_swap(d, layer_of(d)).start()

    def stream_out(c, i):
        yy = (y + i) % NY
        return remote(xbuf.at[c, y], xbuf.at[c, y], x_s.at[c, yy], x_r.at[c, y], at(z, x, p, yy))

    def stream_in(c, i):
        yy = (y + i) % NY
        return remote(xbuf.at[c, yy], xbuf.at[c, yy], x_s.at[c, yy], x_r.at[c, yy], at(z, x, p, yy))

    for i in (2, 1, 3):
        tok_in(i).wait_recv()
    for i in (2, 1, 3):
        stream_out(0, i).start()

    for h in (1, 2, 3):
        forward(0, h)
    first_hop(1)
    finish(0)
    for d in range(2):
        gain_swap(d, 1 - p + d * (1 + 2 * p)).wait_recv()

    lane = lax.broadcasted_iota(jnp.int32, (SEQ, 128), 1)

    def layer(c, carry):
        for i in (2, 1, 3):
            stream_in(c, i).wait_recv()

        def scale_block(b, carry):
            rows = pl.ds(pl.multiple_of(b * SEQ, SEQ), SEQ)
            total = jnp.zeros((SEQ, 1), jnp.float32)
            for yy in range(NY):
                wide = xbuf[c, yy, rows, :].astype(jnp.float32)
                total = total + jnp.sum(wide * wide, axis=1, keepdims=True)
                row = gbuf[c, 0:1, yy * PIECE : yy * PIECE + PIECE]
                xg[yy, rows, :] = (wide * row).astype(jnp.bfloat16)
            high = total.astype(jnp.bfloat16).astype(jnp.float32)
            mixed = jnp.where(lane == 0, high, jnp.where(lane == 1, total - high, 0.0))
            psend[b, :, QKV:EXTRA] = mixed.astype(jnp.bfloat16)
            return carry

        lax.fori_loop(0, NX, scale_block, 0)
        ready(c, 0)

        def qkv_tile(n, carry):
            cols = pl.ds(pl.multiple_of(n * 256, 256), 256)
            acc = jnp.zeros((TOK, 256), jnp.float32)
            for yy in range(NY):
                acc = acc + jnp.dot(
                    xg[yy],
                    wqkv[c, yy * PIECE : yy * PIECE + PIECE, cols],
                    preferred_element_type=jnp.float32,
                )
            acc = acc.astype(jnp.bfloat16)
            for xx in range(NX):
                psend[xx, :, cols] = acc[xx * SEQ : xx * SEQ + SEQ]
            return carry

        lax.fori_loop(0, QKV // 256, qkv_tile, 0)

        def part_out(i):
            xx = (x + i) % NX
            return remote(psend.at[xx], precv.at[c, x], p_s.at[xx], p_r.at[c, x], at(z, xx, p, y))

        def part_in(i):
            xx = (x + i) % NX
            return remote(psend.at[xx], precv.at[c, xx], p_s.at[xx], p_r.at[c, xx], at(z, xx, p, y))

        for i in (2, 1, 3):
            part_out(i).start()

        @pl.when(c < LAYERS - 1)
        def _():
            forward(c + 1, 1)

        for i in (2, 1, 3):
            part_in(i).wait_recv()
        for i in (2, 1, 3):
            part_out(i).wait_send()

        def summed(b):
            cols = slice(b * 128, b * 128 + 128)
            total = psend[x, :, cols].astype(jnp.float32)
            for i in (1, 2, 3):
                total = total + precv[c, (x + i) % NX, :, cols].astype(jnp.float32)
            return total

        square = jnp.sum(summed(12), axis=1, keepdims=True)
        inv_rms = lax.rsqrt(square * (1.0 / WIDTH) + NORM_EPSILON)
        cos = cosines[...]
        sin = sines[...]

        def turned(b):
            value = summed(b) * inv_rms
            return (value * cos + pltpu.roll(value, 64, 1) * sin).astype(jnp.bfloat16)

        bias4 = jnp.concatenate([bias[...]] * 4, axis=0)
        for g in range(2):
            keys = turned(8 + g)
            vals = (summed(10 + g) * inv_rms).astype(jnp.bfloat16)
            query = jnp.concatenate([turned(g * 4 + j) for j in range(4)], axis=0)
            scores = lax.dot_general(
                query, keys, (((1,), (1,)), ((), ())), preferred_element_type=jnp.float32
            )
            scores = scores * HEAD_DIM ** (-0.5) + bias4
            top = jnp.max(scores, axis=1, keepdims=True)
            expo = jnp.exp(scores - top)
            weights = (expo / jnp.sum(expo, axis=1, keepdims=True)).astype(jnp.bfloat16)
            mixed = jnp.dot(weights, vals, preferred_element_type=jnp.float32).astype(jnp.bfloat16)
            for j in range(4):
                b = g * 4 + j
                abuf[c, x, :, b * 128 : b * 128 + 128] = mixed[j * SEQ : j * SEQ + SEQ]

        def attn_out(i):
            xx = (x + i) % NX
            return remote(abuf.at[c, x], abuf.at[c, x], a_s.at[xx], a_r.at[c, x], at(z, xx, p, y))

        def attn_in(i):
            xx = (x + i) % NX
            return remote(abuf.at[c, xx], abuf.at[c, xx], a_s.at[xx], a_r.at[c, xx], at(z, xx, p, y))

        for i in (2, 1, 3):
            attn_out(i).start()

        @pl.when(c < LAYERS - 1)
        def _():
            forward(c + 1, 2)

        ready(c, 1)
        for i in (2, 1, 3):
            attn_in(i).wait_recv()
        for i in (2, 1, 3):
            attn_out(i).wait_send()

        def proj(yy):
            cols = pl.ds(pl.multiple_of(yy * PIECE, PIECE), PIECE)
            return jnp.dot(
                abuf[c].reshape(TOK, HEADS),
                wob[c, :, cols],
                preferred_element_type=jnp.float32,
            )

        def proj_out(yy):
            return remote(osend.at[yy], orecv.at[c, y], o_s.at[yy], o_r.at[c, y], at(z, x, p, yy))

        def proj_in(yy):
            return remote(osend.at[yy], orecv.at[c, yy], o_s.at[yy], o_r.at[c, yy], at(z, x, p, yy))

        def proj_tile(i, carry):
            yy = (y + i) % NY
            osend[yy] = proj(yy).astype(jnp.bfloat16)
            proj_out(yy).start()
            return carry

        lax.fori_loop(1, NY, proj_tile, 0)
        oown[...] = proj(y)

        @pl.when(c < LAYERS - 1)
        def _():
            forward(c + 1, 3)

        @pl.when(c < LAYERS - 2)
        def _():
            first_hop(c + 2)

        for i in (1, 2, 3):
            proj_in((y + i) % NY).wait_recv()
        for i in (1, 2, 3):
            proj_out((y + i) % NY).wait_send()

        def add_block(b, carry):
            rows = pl.ds(pl.multiple_of(b * SEQ, SEQ), SEQ)
            total = oown[rows, :]
            for i in (1, 2, 3):
                total = total + orecv[c, (y + i) % NY, rows, :].astype(jnp.float32)
            total = total + xbuf[c, y, rows, :].astype(jnp.float32)
            xbuf[c + 1, y, rows, :] = total.astype(jnp.bfloat16)
            return carry

        lax.fori_loop(0, NX, add_block, 0)

        @pl.when(c < LAYERS - 1)
        def _():
            for i in (2, 1, 3):
                stream_out(c + 1, i).start()
            finish(c + 1)

        return carry

    lax.fori_loop(0, LAYERS, layer, 0)

    def done_rows(xx, q):
        return pl.ds(pl.multiple_of(xx * SEQ + q * 32, 32), 32)

    def done_out(i, j):
        xx, q = (x + i) % NX, (p + j) % 2
        return remote(
            xbuf.at[LAYERS, y, done_rows(xx, q), :],
            frecv.at[p, x],
            f_s.at[q, xx],
            f_r.at[p, x],
            at(z, xx, q, y),
        )

    def done_in(i, j):
        xx, q = (x + i) % NX, (p + j) % 2
        return remote(
            xbuf.at[LAYERS, y, done_rows(xx, q), :],
            frecv.at[q, xx],
            f_s.at[q, xx],
            f_r.at[q, xx],
            at(z, xx, q, y),
        )

    away = [(i, j) for i in (2, 1, 3, 0) for j in range(2) if (i, j) != (0, 0)]
    for i, j in away:
        done_out(i, j).start()
    frecv[p, x] = xbuf[LAYERS, y, done_rows(x, p), :]
    for i, j in away:
        done_in(i, j).wait_recv()
    for q in range(2):
        for xx in range(NX):
            out[q, :, xx * 128 : xx * 128 + 128] = frecv[q, xx, :, 0:128]
            out[q, :, 512 + xx * 128 : 512 + xx * 128 + 128] = frecv[q, xx, :, 128:256]

    for i, j in away:
        done_out(i, j).wait_send()
    for i in (1, 2, 3):
        tok_out(i).wait_send()
    for d in range(2):
        gain_swap(d, layer_of(d)).wait_send()
        for t in range(2):
            own_swap(layer_of(d), t).wait_send()

    def drain(c, carry):
        for t in range(2):
            for half in range(2):
                for h in (1, 2, 3):
                    hop_out(c, t, half, h).wait_send()
                    swap_out(c, t, half, h).wait_send()
            hop_out(c, t, p, 4).wait_send()
            swap_out(c, t, p, 4).wait_send()

        @pl.when(c < LAYERS - 1)
        def _():
            for i in (1, 2, 3):
                stream_out(c, i).wait_send()

        @pl.when(c == LAYERS - 1)
        def _():
            for i in (1, 2, 3):
                stream_out(c, i).wait_send()

        return carry

    lax.fori_loop(0, LAYERS, drain, 0)


def per_device(
    tokens,
    w_query,
    w_key,
    w_value,
    w_out,
    norm_gain,
    boundary,
    skip_offset,
    doc_lengths,
    batch_order,
):
    core = lax.axis_index("pipe")
    sample = lax.dynamic_index_in_dim(batch_order[0], core, 0, keepdims=False)

    def chosen(array):
        return lax.dynamic_index_in_dim(array, sample, 0, keepdims=False)

    positions, allowed = sample_layout(
        chosen(boundary), chosen(skip_offset), chosen(doc_lengths), SEQ
    )
    angles = rope_angles(positions, HEAD_DIM)
    cosine = jnp.cos(angles)
    sine = jnp.sin(angles)
    cosines = jnp.concatenate([cosine, cosine], axis=1)
    sines = jnp.concatenate([-sine, sine], axis=1)
    bias = jnp.where(allowed, 0.0, -jnp.inf).astype(jnp.float32)

    vmem = pl.BlockSpec(memory_space=pltpu.VMEM)
    anywhere = pl.BlockSpec(memory_space=pl.ANY)
    dma = pltpu.SemaphoreType.DMA
    bf16, f32 = jnp.bfloat16, jnp.float32
    return pl.pallas_call(
        stack_kernel,
        out_shape=jax.ShapeDtypeStruct((2, 32, 1024), bf16),
        in_specs=[vmem] * 5 + [anywhere] * 4,
        out_specs=vmem,
        scratch_shapes=[
            pltpu.VMEM((LAYERS, SET, QKV), bf16),
            pltpu.VMEM((LAYERS, HEADS, SET), bf16),
            pltpu.VMEM((LAYERS, 8, SET), f32),
            pltpu.VMEM((NX, SEQ, PIECE), bf16),
            pltpu.VMEM((LAYERS + 1, NY, TOK, PIECE), bf16),
            pltpu.VMEM((NY, TOK, PIECE), bf16),
            pltpu.VMEM((NX, SEQ, EXTRA), bf16),
            pltpu.VMEM((LAYERS, NX, SEQ, EXTRA), bf16),
            pltpu.VMEM((LAYERS, NX, SEQ, HEADS), bf16),
            pltpu.VMEM((NY, TOK, PIECE), bf16),
            pltpu.VMEM((TOK, PIECE), f32),
            pltpu.VMEM((LAYERS, NY, TOK, PIECE), bf16),
            pltpu.VMEM((2, NX, 32, PIECE), bf16),
            dma((2, 4)),
            dma((LAYERS, 2, 2, 4)),
            dma((LAYERS, 2, 2, 4)),
            dma((LAYERS, 2)),
            dma((LAYERS, 2)),
            dma((LAYERS, 2, 2, 4)),
            dma((LAYERS, 2, 2, 4)),
            dma((2,)),
            dma((2,)),
            dma((NX,)),
            dma((NX,)),
            dma((LAYERS, NY)),
            dma((LAYERS, NY)),
            dma((NX,)),
            dma((LAYERS, NX)),
            dma((NX,)),
            dma((LAYERS, NX)),
            dma((NY,)),
            dma((LAYERS, NY)),
            dma((2, NX)),
            dma((2, NX)),
        ],
        compiler_params=pltpu.CompilerParams(
            collective_id=0, has_side_effects=True, vmem_limit_bytes=60 * 1024 * 1024
        ),
    )(chosen(tokens), cosines, sines, bias, norm_gain, w_query, w_key, w_value, w_out)


def solution(mesh):
    placed = (
        P("dp", None, "tensor"),
        P(None, "pipe", "dp", "tensor"),
        P(None, "pipe", "dp", "tensor"),
        P(None, "pipe", "dp", "tensor"),
        P(None, "pipe", "tensor", "dp"),
        P(None, "pipe", None),
        P("dp"),
        P("dp"),
        P("dp", None),
        P("dp", None),
    )
    return jax.shard_map(
        per_device, mesh=mesh, in_specs=placed, out_specs=P("dp", "pipe", "tensor"), check_vma=False
    )
```

```python
import math

import jax
import jax.numpy as jnp
import numpy as np
from jax import lax
from jax.experimental import pallas as pl
from jax.experimental.pallas import tpu as pltpu
from jax.sharding import PartitionSpec as P

HEAD_DIM = 128
ROPE_THETA = 500000.0
NORM_EPSILON = 1e-05
MESH = pl.DeviceIdType.MESH

LAYERS = 4
NZ, NX, NY = 8, 4, 4
SEQ = 64
WIDTH = 4096
CHUNK = 128
SET = NZ * CHUNK
QKV = 1536
HEADS = 1024
GROUP = QKV // 2
EXTRA = GROUP + 128
HALF = HEADS // 2
TOK = NX * SEQ
PIECE = SET // NY


TWO_PI_HIGH = 6.28125
TWO_PI_MID = 0.0019340515136718750
TWO_PI_LOW = 2 * math.pi - TWO_PI_HIGH - TWO_PI_MID
SINE_TERMS = [(-1.0) ** k / math.factorial(2 * k + 1) for k in range(10)]
COSINE_TERMS = [(-1.0) ** k / math.factorial(2 * k) for k in range(11)]


def frequencies():
    half = HEAD_DIM // 2
    table = np.float64(ROPE_THETA) ** (-np.arange(half, dtype=np.float64) / half)
    return np.tile(table.astype(np.float32), 2)[None, :].repeat(8, axis=0)


def series(terms, square):
    total = jnp.full(square.shape, terms[-1], jnp.float32)
    for term in terms[-2::-1]:
        total = total * square + term
    return total


def sine_and_cosine(angle):
    turns = jnp.floor(angle * (0.5 / math.pi) + 0.5)
    rest = ((angle - turns * TWO_PI_HIGH) - turns * TWO_PI_MID) - turns * TWO_PI_LOW
    square = rest * rest
    return rest * series(SINE_TERMS, square), series(COSINE_TERMS, square)


def stack_kernel(
    order,
    boundary,
    offset,
    lengths,
    tokens,
    freq,
    gain_in,
    wq,
    wk,
    wv,
    wo,
    out,
    wqkv,
    wob,
    gbuf,
    tsend,
    xbuf,
    xg,
    psend0,
    psend1,
    precv0,
    precv1,
    abuf,
    osend,
    oown,
    orecv,
    frecv,
    tok_v,
    freq_v,
    gain,
    cosines,
    sines,
    bias,
    isem,
    lsem,
    hop_s,
    hop_r,
    own_s,
    own_r,
    par_s,
    par_r,
    g_s,
    g_r,
    t_s,
    t_r,
    x_s,
    x_r,
    p_s,
    p_r,
    a_s,
    a_r,
    o_s,
    o_r,
    f_s,
    f_r,
):
    dp = lax.axis_index("dp")
    p = lax.axis_index("pipe")
    y = lax.axis_index("tensor")
    z = dp // NX
    x = dp % NX
    step = 1 - 2 * p

    def at(zz, xx, pp, yy):
        return {"dp": zz * NX + xx, "pipe": pp, "tensor": yy}

    def zrel(k):
        return (z + step * k + NZ) % NZ

    down = at(zrel(1), x, p, y)
    up = at(zrel(-1), x, p, y)
    other = at(z, x, 1 - p, y)

    def remote(src, dst, s, r, dev):
        return pltpu.make_async_remote_copy(
            src_ref=src, dst_ref=dst, send_sem=s, recv_sem=r, device_id=dev, device_id_type=MESH
        )

    def layer_of(d):
        return p + d * (3 - 2 * p)

    def rows_of(zz):
        return pl.ds(pl.multiple_of(zz * CHUNK, CHUNK), CHUNK)

    def loads(d):
        c = layer_of(d)
        r = rows_of(z)
        copies = []
        for g in range(2):
            for k, (source, width, first) in enumerate(
                ((wq, 512, 0), (wk, 128, 512), (wv, 128, 640))
            ):
                copies.append(
                    pltpu.make_async_copy(
                        source.at[d, 0, :, pl.ds(g * width, width)],
                        wqkv.at[c, r, pl.ds(g * GROUP + first, width)],
                        lsem.at[d, g * 3 + k],
                    )
                )
        return copies, [pltpu.make_async_copy(wo.at[d, 0], wob.at[c, :, r], lsem.at[d, 6])]

    small = [
        pltpu.make_async_copy(tokens, tok_v, isem.at[0]),
        pltpu.make_async_copy(freq, freq_v, isem.at[1]),
        pltpu.make_async_copy(gain_in, gain, isem.at[2]),
    ]
    for copy in loads(0)[0] + loads(0)[1] + small + loads(1)[0] + loads(1)[1]:
        copy.start()

    barrier = pltpu.get_barrier_semaphore()
    peers = [down, up, other]
    for i in (1, 2, 3):
        peers.append(at(z, (x + i) % NX, p, y))
        peers.append(at(z, (x + i) % NX, 1 - p, y))
        peers.append(at(z, x, p, (y + i) % NY))
    for dev in peers:
        pl.semaphore_signal(barrier, inc=1, device_id=dev, device_id_type=MESH)
    pl.semaphore_wait(barrier, len(peers))

    def piece(c, zz, t, half):
        if t == 0:
            return wqkv.at[c, pl.ds(pl.multiple_of(zz * CHUNK + half * 64, 64), 64), :]
        return wob.at[c, pl.ds(pl.multiple_of(half * 512, 512), 512), rows_of(zz)]

    def whole(c, zz, t):
        if t == 0:
            return wqkv.at[c, rows_of(zz), :]
        return wob.at[c, :, rows_of(zz)]

    def hop_out(c, t, half, h):
        ref = piece(c, zrel(1 - h), t, half)
        return remote(ref, ref, hop_s.at[c, t, half, h - 1], hop_r.at[c, t, half, h - 1], down)

    def hop_in(c, t, half, h):
        ref = piece(c, zrel(-h), t, half)
        return remote(ref, ref, hop_s.at[c, t, half, h - 1], hop_r.at[c, t, half, h - 1], up)

    def swap_out(c, t, half, h):
        ref = piece(c, zrel(-h), t, half)
        return remote(ref, ref, par_s.at[c, t, half, h - 1], par_r.at[c, t, half, h - 1], other)

    def swap_in(c, t, half, h):
        ref = piece(c, zrel(h), t, half)
        return remote(ref, ref, par_s.at[c, t, half, h - 1], par_r.at[c, t, half, h - 1], other)

    def own_swap(c, t):
        ref = whole(c, z, t)
        return remote(ref, ref, own_s.at[c, t], own_r.at[c, t], other)

    def holder(c):
        return jnp.where((c == 0) | (c == 3), 0, 1)

    def first_hop(c, t):
        @pl.when(p != holder(c))
        def _():
            own_swap(c, t).wait_recv()

        for half in range(2):
            hop_out(c, t, half, 1).start()

    def forward(c, t, h):
        for half in range(2):
            hop_in(c, t, half, h).wait_recv()
            if h < 3:
                hop_out(c, t, half, h + 1).start()
            swap_out(c, t, half, h).start()
        if h == 3:
            hop_out(c, t, p, 4).start()

    def finish(c, t):
        hop_in(c, t, p, 4).wait_recv()
        swap_out(c, t, p, 4).start()

    def ready(c, t):
        for h in (1, 2, 3):
            for half in range(2):
                swap_in(c, t, half, h).wait_recv()
        swap_in(c, t, 1 - p, 4).wait_recv()

    def load_and_share(d):
        for t in range(2):
            for copy in loads(d)[t]:
                copy.wait()
            own_swap(layer_of(d), t).start()

    load_and_share(0)
    first_hop(0, 0)

    for copy in small:
        copy.wait()
    second = order[0, p] == 1

    def chosen(first, other_one):
        return jnp.where(second, other_one, first)

    for xx in range(NX):
        for k in range(2):
            cols = slice(k * 512 + xx * 128, k * 512 + xx * 128 + 128)
            tsend[xx, :, k * 128 : k * 128 + 128] = chosen(
                tok_v[0, :, cols].astype(jnp.float32), tok_v[1, :, cols].astype(jnp.float32)
            ).astype(jnp.bfloat16)

    def block(ref, b, size):
        return ref.at[pl.ds(pl.multiple_of(b * size, size), size), :]

    def tok_out(i):
        xx = (x + i) % NX
        return remote(
            tsend.at[xx], block(xbuf.at[0, y], x, SEQ), t_s.at[xx], t_r.at[x], at(z, xx, p, y)
        )

    def tok_in(i):
        xx = (x + i) % NX
        return remote(
            tsend.at[xx], block(xbuf.at[0, y], xx, SEQ), t_s.at[xx], t_r.at[xx], at(z, xx, p, y)
        )

    for i in (2, 1, 3):
        tok_out(i).start()
    xbuf[0, y, pl.ds(pl.multiple_of(x * SEQ, SEQ), SEQ), :] = tsend[x]

    forward(0, 0, 1)
    load_and_share(1)

    for d in range(2):
        c = layer_of(d)
        for zz in range(NZ):
            row = gain[d, :, pl.ds(pl.multiple_of((zz * NX + x) * CHUNK, CHUNK), CHUNK)]
            gbuf[c, :, zz * CHUNK : zz * CHUNK + CHUNK] = jnp.broadcast_to(row, (8, CHUNK))

    def gain_swap(d, c):
        return remote(gbuf.at[c], gbuf.at[c], g_s.at[d], g_r.at[d], other)

    for d in range(2):
        gain_swap(d, layer_of(d)).start()

    def stream_out(c, i):
        yy = (y + i) % NY
        return remote(xbuf.at[c, y], xbuf.at[c, y], x_s.at[c, yy], x_r.at[c, y], at(z, x, p, yy))

    def stream_in(c, i):
        yy = (y + i) % NY
        return remote(xbuf.at[c, yy], xbuf.at[c, yy], x_s.at[c, yy], x_r.at[c, yy], at(z, x, p, yy))

    for i in (2, 1, 3):
        tok_in(i).wait_recv()
    for i in (2, 1, 3):
        stream_out(0, i).start()

    forward(0, 0, 2)

    row = lax.broadcasted_iota(jnp.int32, (SEQ, 128), 0)
    lane = lax.broadcasted_iota(jnp.int32, (SEQ, 128), 1)
    cut = chosen(boundary[0], boundary[1])
    jump = chosen(offset[0], offset[1])
    places = jnp.where(row < cut, row, row + jump)
    sine, cosine = sine_and_cosine(places.astype(jnp.float32) * freq_v[0:1, :])
    cosines[...] = cosine
    sines[...] = jnp.where(lane < 64, -sine, sine)
    from_row = lax.broadcasted_iota(jnp.int32, (SEQ, SEQ), 0)
    to_row = lax.broadcasted_iota(jnp.int32, (SEQ, SEQ), 1)
    end = 0
    doc_from = jnp.zeros((SEQ, SEQ), jnp.int32)
    doc_to = jnp.zeros((SEQ, SEQ), jnp.int32)
    for k in range(4):
        end = end + chosen(lengths[0, k], lengths[1, k])
        doc_from = doc_from + jnp.where(from_row >= end, 1, 0)
        doc_to = doc_to + jnp.where(to_row >= end, 1, 0)
    allowed = (doc_from == doc_to) & (to_row <= from_row)
    mask = jnp.where(allowed, 0.0, -jnp.inf).astype(jnp.float32)
    for j in range(4):
        bias[j * SEQ : j * SEQ + SEQ, :] = mask

    forward(0, 0, 3)
    first_hop(0, 1)
    for d in range(2):
        gain_swap(d, 1 - p + d * (1 + 2 * p)).wait_recv()

    def layer(c, carry):
        last = c == LAYERS - 1

        @pl.when(c > 0)
        def _():
            forward(c, 1, 1)

        finish(c, 0)
        stream_in(c, 1).wait_recv()

        @pl.when(c > 0)
        def _():
            forward(c, 1, 2)

            @pl.when(jnp.logical_not(last))
            def _():
                first_hop(c + 1, 0)

        for i in (3, 2):
            stream_in(c, i).wait_recv()

        def scale_block(b, carry):
            rows = pl.ds(pl.multiple_of(b * SEQ, SEQ), SEQ)
            total = jnp.zeros((SEQ, 1), jnp.float32)
            for yy in range(NY):
                wide = xbuf[c, yy, rows, :].astype(jnp.float32)
                total = total + jnp.sum(wide * wide, axis=1, keepdims=True)
                row = gbuf[c, 0:1, yy * PIECE : yy * PIECE + PIECE]
                xg[yy, rows, :] = (wide * row).astype(jnp.bfloat16)
            high = total.astype(jnp.bfloat16).astype(jnp.float32)
            mixed = jnp.where(lane == 0, high, jnp.where(lane == 1, total - high, 0.0))
            psend0[b, :, GROUP:EXTRA] = mixed.astype(jnp.bfloat16)
            return carry

        lax.fori_loop(0, NX, scale_block, 0)
        ready(c, 0)

        def qkv_tile(n, g, psend):
            cols = pl.ds(pl.multiple_of(g * GROUP + n * 256, 256), 256)
            acc = jnp.zeros((TOK, 256), jnp.float32)
            for yy in range(NY):
                acc = acc + jnp.dot(
                    xg[yy],
                    wqkv[c, yy * PIECE : yy * PIECE + PIECE, cols],
                    preferred_element_type=jnp.float32,
                )
            acc = acc.astype(jnp.bfloat16)
            for xx in range(NX):
                psend[xx, :, pl.ds(pl.multiple_of(n * 256, 256), 256)] = acc[
                    xx * SEQ : xx * SEQ + SEQ
                ]
            return 0

        sends = (psend0, psend1)
        lands = (precv0, precv1)

        def part_out(g, i):
            xx = (x + i) % NX
            return remote(
                sends[g].at[xx], lands[g].at[c, x], p_s.at[g, xx], p_r.at[g, c, x], at(z, xx, p, y)
            )

        def part_in(g, i):
            xx = (x + i) % NX
            return remote(
                sends[g].at[xx], lands[g].at[c, xx], p_s.at[g, xx], p_r.at[g, c, xx], at(z, xx, p, y)
            )

        def attn_out(g, i):
            xx = (x + i) % NX
            ref = abuf.at[c, g, x]
            return remote(ref, ref, a_s.at[g, xx], a_r.at[g, c, x], at(z, xx, p, y))

        def attn_in(g, i):
            xx = (x + i) % NX
            ref = abuf.at[c, g, xx]
            return remote(ref, ref, a_s.at[g, xx], a_r.at[g, c, xx], at(z, xx, p, y))

        for g in range(2):
            lax.fori_loop(0, GROUP // 256, lambda n, _: qkv_tile(n, g, sends[g]), 0)
            for i in (2, 1, 3):
                part_out(g, i).start()

        @pl.when(c == 0)
        def _():
            forward(c, 1, 1)
            first_hop(c + 1, 0)
            forward(c, 1, 2)

        def summed(g, b):
            cols = slice(b * 128, b * 128 + 128)
            total = sends[g][x, :, cols].astype(jnp.float32)
            for i in (1, 2, 3):
                total = total + lands[g][c, (x + i) % NX, :, cols].astype(jnp.float32)
            return total

        inv_rms = None
        for g in range(2):
            for i in (1, 3, 2):
                part_in(g, i).wait_recv()
            if g == 0:
                square = jnp.sum(summed(0, 6), axis=1, keepdims=True)
                inv_rms = lax.rsqrt(square * (1.0 / WIDTH) + NORM_EPSILON)

            def turned(b):
                value = summed(g, b) * inv_rms
                return (value * cosines[...] + pltpu.roll(value, 64, 1) * sines[...]).astype(
                    jnp.bfloat16
                )

            keys = turned(4)
            vals = (summed(g, 5) * inv_rms).astype(jnp.bfloat16)
            query = jnp.concatenate([turned(j) for j in range(4)], axis=0)
            scores = lax.dot_general(
                query, keys, (((1,), (1,)), ((), ())), preferred_element_type=jnp.float32
            )
            scores = scores * HEAD_DIM ** (-0.5) + bias[...]
            top = jnp.max(scores, axis=1, keepdims=True)
            expo = jnp.exp(scores - top)
            weights = (expo / jnp.sum(expo, axis=1, keepdims=True)).astype(jnp.bfloat16)
            mixed = jnp.dot(weights, vals, preferred_element_type=jnp.float32).astype(jnp.bfloat16)
            for j in range(4):
                abuf[c, g, x, :, j * 128 : j * 128 + 128] = mixed[j * SEQ : j * SEQ + SEQ]
            for i in (2, 1, 3):
                attn_out(g, i).start()
            if g == 0:
                forward(c, 1, 3)

                @pl.when(jnp.logical_not(last))
                def _():
                    forward(c + 1, 0, 1)

        finish(c, 1)
        for i in (1, 3, 2):
            attn_in(0, i).wait_recv()

        @pl.when(jnp.logical_not(last))
        def _():
            forward(c + 1, 0, 2)

        ready(c, 1)
        for i in (1, 3, 2):
            attn_in(1, i).wait_recv()
        for g in range(2):
            for i in (1, 2, 3):
                part_out(g, i).wait_send()
                attn_out(g, i).wait_send()

        def proj(yy):
            cols = pl.ds(pl.multiple_of(yy * PIECE, PIECE), PIECE)
            total = jnp.zeros((TOK, PIECE), jnp.float32)
            for g in range(2):
                total = total + jnp.dot(
                    abuf[c, g].reshape(TOK, HALF),
                    wob[c, g * HALF : g * HALF + HALF, cols],
                    preferred_element_type=jnp.float32,
                )
            return total

        def proj_out(yy):
            return remote(osend.at[yy], orecv.at[c, y], o_s.at[yy], o_r.at[c, y], at(z, x, p, yy))

        def proj_in(yy):
            return remote(osend.at[yy], orecv.at[c, yy], o_s.at[yy], o_r.at[c, yy], at(z, x, p, yy))

        def proj_tile(i, carry):
            yy = (y + i) % NY
            osend[yy] = proj(yy).astype(jnp.bfloat16)
            proj_out(yy).start()
            return carry

        lax.fori_loop(1, NY, proj_tile, 0)
        oown[...] = proj(y)

        @pl.when(jnp.logical_not(last))
        def _():
            first_hop(c + 1, 1)

        proj_in((y + 1) % NY).wait_recv()

        @pl.when(jnp.logical_not(last))
        def _():
            forward(c + 1, 0, 3)

        for i in (3, 2):
            proj_in((y + i) % NY).wait_recv()
        for i in (1, 2, 3):
            proj_out((y + i) % NY).wait_send()

        def add_block(b, carry):
            rows = pl.ds(pl.multiple_of(b * SEQ, SEQ), SEQ)
            total = oown[rows, :]
            for i in (1, 2, 3):
                total = total + orecv[c, (y + i) % NY, rows, :].astype(jnp.float32)
            total = total + xbuf[c, y, rows, :].astype(jnp.float32)
            xbuf[c + 1, y, rows, :] = total.astype(jnp.bfloat16)
            return carry

        lax.fori_loop(0, NX, add_block, 0)

        @pl.when(c < LAYERS - 1)
        def _():
            for i in (2, 1, 3):
                stream_out(c + 1, i).start()

        return carry

    lax.fori_loop(0, LAYERS, layer, 0)

    def done_rows(xx, q):
        return pl.ds(pl.multiple_of(xx * SEQ + q * 32, 32), 32)

    def done_out(i, j):
        xx, q = (x + i) % NX, (p + j) % 2
        return remote(
            xbuf.at[LAYERS, y, done_rows(xx, q), :],
            frecv.at[p, x],
            f_s.at[q, xx],
            f_r.at[p, x],
            at(z, xx, q, y),
        )

    def done_in(i, j):
        xx, q = (x + i) % NX, (p + j) % 2
        return remote(
            xbuf.at[LAYERS, y, done_rows(xx, q), :],
            frecv.at[q, xx],
            f_s.at[q, xx],
            f_r.at[q, xx],
            at(z, xx, q, y),
        )

    away = [(i, j) for i in (2, 1, 3, 0) for j in range(2) if (i, j) != (0, 0)]
    for i, j in away:
        done_out(i, j).start()
    frecv[p, x] = xbuf[LAYERS, y, done_rows(x, p), :]
    for i, j in away:
        done_in(i, j).wait_recv()
    for q in range(2):
        for xx in range(NX):
            out[q, :, xx * 128 : xx * 128 + 128] = frecv[q, xx, :, 0:128]
            out[q, :, 512 + xx * 128 : 512 + xx * 128 + 128] = frecv[q, xx, :, 128:256]

    for i, j in away:
        done_out(i, j).wait_send()
    for i in (1, 2, 3):
        tok_out(i).wait_send()
    for d in range(2):
        gain_swap(d, layer_of(d)).wait_send()
        for t in range(2):
            own_swap(layer_of(d), t).wait_send()

    def drain(c, carry):
        for t in range(2):
            for half in range(2):
                for h in (1, 2, 3):
                    hop_out(c, t, half, h).wait_send()
                    swap_out(c, t, half, h).wait_send()
            hop_out(c, t, p, 4).wait_send()
            swap_out(c, t, p, 4).wait_send()

        @pl.when(c < LAYERS - 1)
        def _():
            for i in (1, 2, 3):
                stream_out(c, i).wait_send()

        @pl.when(c == LAYERS - 1)
        def _():
            for i in (1, 2, 3):
                stream_out(c, i).wait_send()

        return carry

    lax.fori_loop(0, LAYERS, drain, 0)


def per_device(
    tokens,
    w_query,
    w_key,
    w_value,
    w_out,
    norm_gain,
    boundary,
    skip_offset,
    doc_lengths,
    batch_order,
):
    vmem = pl.BlockSpec(memory_space=pltpu.VMEM)
    smem = pl.BlockSpec(memory_space=pltpu.SMEM)
    anywhere = pl.BlockSpec(memory_space=pl.ANY)
    dma = pltpu.SemaphoreType.DMA
    bf16, f32 = jnp.bfloat16, jnp.float32
    return pl.pallas_call(
        stack_kernel,
        out_shape=jax.ShapeDtypeStruct((2, 32, 1024), bf16),
        in_specs=[smem] * 4 + [anywhere] * 7,
        out_specs=vmem,
        scratch_shapes=[
            pltpu.VMEM((LAYERS, SET, QKV), bf16),
            pltpu.VMEM((LAYERS, HEADS, SET), bf16),
            pltpu.VMEM((LAYERS, 8, SET), f32),
            pltpu.VMEM((NX, SEQ, PIECE), bf16),
            pltpu.VMEM((LAYERS + 1, NY, TOK, PIECE), bf16),
            pltpu.VMEM((NY, TOK, PIECE), bf16),
            pltpu.VMEM((NX, SEQ, EXTRA), bf16),
            pltpu.VMEM((NX, SEQ, GROUP), bf16),
            pltpu.VMEM((LAYERS, NX, SEQ, EXTRA), bf16),
            pltpu.VMEM((LAYERS, NX, SEQ, GROUP), bf16),
            pltpu.VMEM((LAYERS, 2, NX, SEQ, HALF), bf16),
            pltpu.VMEM((NY, TOK, PIECE), bf16),
            pltpu.VMEM((TOK, PIECE), f32),
            pltpu.VMEM((LAYERS, NY, TOK, PIECE), bf16),
            pltpu.VMEM((2, NX, 32, PIECE), bf16),
            pltpu.VMEM((2, SEQ, 1024), bf16),
            pltpu.VMEM((8, HEAD_DIM), f32),
            pltpu.VMEM((2, 1, WIDTH), f32),
            pltpu.VMEM((SEQ, HEAD_DIM), f32),
            pltpu.VMEM((SEQ, HEAD_DIM), f32),
            pltpu.VMEM((4 * SEQ, SEQ), f32),
            dma((3,)),
            dma((2, 7)),
            dma((LAYERS, 2, 2, 4)),
            dma((LAYERS, 2, 2, 4)),
            dma((LAYERS, 2)),
            dma((LAYERS, 2)),
            dma((LAYERS, 2, 2, 4)),
            dma((LAYERS, 2, 2, 4)),
            dma((2,)),
            dma((2,)),
            dma((NX,)),
            dma((NX,)),
            dma((LAYERS, NY)),
            dma((LAYERS, NY)),
            dma((2, NX)),
            dma((2, LAYERS, NX)),
            dma((2, NX)),
            dma((2, LAYERS, NX)),
            dma((NY,)),
            dma((LAYERS, NY)),
            dma((2, NX)),
            dma((2, NX)),
        ],
        compiler_params=pltpu.CompilerParams(
            collective_id=0, has_side_effects=True, vmem_limit_bytes=60 * 1024 * 1024
        ),
    )(
        batch_order,
        boundary,
        skip_offset,
        doc_lengths,
        tokens,
        jnp.asarray(frequencies()),
        norm_gain,
        w_query,
        w_key,
        w_value,
        w_out,
    )


def solution(mesh):
    placed = (
        P("dp", None, "tensor"),
        P(None, "pipe", "dp", "tensor"),
        P(None, "pipe", "dp", "tensor"),
        P(None, "pipe", "dp", "tensor"),
        P(None, "pipe", "tensor", "dp"),
        P(None, "pipe", None),
        P("dp"),
        P("dp"),
        P("dp", None),
        P("dp", None),
    )
    return jax.shard_map(
        per_device, mesh=mesh, in_specs=placed, out_specs=P("dp", "pipe", "tensor"), check_vma=False
    )
```

```python
import math

import jax
import jax.numpy as jnp
import numpy as np
from jax import lax
from jax.experimental import pallas as pl
from jax.experimental.pallas import tpu as pltpu
from jax.sharding import PartitionSpec as P

HEAD_DIM = 128
ROPE_THETA = 500000.0
NORM_EPSILON = 1e-05
MESH = pl.DeviceIdType.MESH

LAYERS = 4
NZ, NX, NY = 8, 4, 4
SEQ = 64
WIDTH = 4096
CHUNK = 128
SET = NZ * CHUNK
QKV = 1536
HEADS = 1024
GROUP = QKV // 2
EXTRA = GROUP + 128
STREAM = 2 * SEQ
HALF = HEADS // 2
TOK = NX * SEQ
PIECE = SET // NY
PIECES = (4, 2)


TWO_PI_HIGH = 6.28125
TWO_PI_MID = 0.0019340515136718750
TWO_PI_LOW = 2 * math.pi - TWO_PI_HIGH - TWO_PI_MID
SINE_TERMS = [(-1.0) ** k / math.factorial(2 * k + 1) for k in range(10)]
COSINE_TERMS = [(-1.0) ** k / math.factorial(2 * k) for k in range(11)]


def frequencies():
    half = HEAD_DIM // 2
    table = np.float64(ROPE_THETA) ** (-np.arange(half, dtype=np.float64) / half)
    return np.tile(table.astype(np.float32), 2)[None, :].repeat(8, axis=0)


def series(terms, square):
    total = jnp.full(square.shape, terms[-1], jnp.float32)
    for term in terms[-2::-1]:
        total = total * square + term
    return total


def sine_and_cosine(angle):
    turns = jnp.floor(angle * (0.5 / math.pi) + 0.5)
    rest = ((angle - turns * TWO_PI_HIGH) - turns * TWO_PI_MID) - turns * TWO_PI_LOW
    square = rest * rest
    return rest * series(SINE_TERMS, square), series(COSINE_TERMS, square)


def stack_kernel(
    order,
    boundary,
    offset,
    lengths,
    tokens,
    freq,
    gain_in,
    wq,
    wk,
    wv,
    wo,
    out,
    wqkv,
    wob,
    gbuf,
    tsend,
    xbuf,
    xg,
    psend,
    precv,
    abuf,
    osend,
    oown,
    orecv,
    frecv,
    tok_v,
    freq_v,
    gain,
    tables,
    isem,
    lsem,
    hop_sq,
    hop_rq,
    hop_so,
    hop_ro,
    own_s,
    own_r,
    par_sq,
    par_rq,
    par_so,
    par_ro,
    g_s,
    g_r,
    t_s,
    t_r,
    tab_s,
    tab_r,
    x_s,
    x_r,
    p_s,
    p_r,
    a_s,
    a_r,
    o_s,
    o_r,
    f_s,
    f_r,
):
    dp = lax.axis_index("dp")
    p = lax.axis_index("pipe")
    y = lax.axis_index("tensor")
    z = dp // NX
    x = dp % NX
    step = 1 - 2 * p

    def at(zz, xx, pp, yy):
        return {"dp": zz * NX + xx, "pipe": pp, "tensor": yy}

    def zrel(k):
        return (z + step * k + NZ) % NZ

    down = at(zrel(1), x, p, y)
    up = at(zrel(-1), x, p, y)
    other = at(z, x, 1 - p, y)

    def remote(src, dst, s, r, dev):
        return pltpu.make_async_remote_copy(
            src_ref=src, dst_ref=dst, send_sem=s, recv_sem=r, device_id=dev, device_id_type=MESH
        )

    def layer_of(d):
        return p + d * (3 - 2 * p)

    def rows_of(zz):
        return pl.ds(pl.multiple_of(zz * CHUNK, CHUNK), CHUNK)

    def loads(d):
        c = layer_of(d)
        r = rows_of(z)
        copies = []
        for g in range(2):
            for k, (source, width, first) in enumerate(
                ((wq, 512, 0), (wk, 128, 512), (wv, 128, 640))
            ):
                copies.append(
                    pltpu.make_async_copy(
                        source.at[d, 0, :, pl.ds(g * width, width)],
                        wqkv.at[c, r, pl.ds(g * GROUP + first, width)],
                        lsem.at[d, g * 3 + k],
                    )
                )
        copies.append(pltpu.make_async_copy(wo.at[d, 0], wob.at[c, :, r], lsem.at[d, 6]))
        return copies

    small = [
        pltpu.make_async_copy(tokens, tok_v, isem.at[0]),
        pltpu.make_async_copy(freq, freq_v, isem.at[1]),
        pltpu.make_async_copy(gain_in, gain, isem.at[2]),
    ]
    for copy in loads(0) + small + loads(1):
        copy.start()

    barrier = pltpu.get_barrier_semaphore()
    peers = [down, up, other]
    for i in (1, 2, 3):
        peers.append(at(z, (x + i) % NX, p, y))
        peers.append(at(z, (x + i) % NX, 1 - p, y))
        peers.append(at(z, x, p, (y + i) % NY))
    for dev in peers:
        pl.semaphore_signal(barrier, inc=1, device_id=dev, device_id_type=MESH)
    pl.semaphore_wait(barrier, len(peers))

    def piece(c, zz, t, k):
        rows = (CHUNK if t == 0 else HEADS) // PIECES[t]
        if t == 0:
            return wqkv.at[c, pl.ds(pl.multiple_of(zz * CHUNK + k * rows, rows), rows), :]
        return wob.at[c, pl.ds(pl.multiple_of(k * rows, rows), rows), rows_of(zz)]

    def whole(c, zz, t):
        if t == 0:
            return wqkv.at[c, rows_of(zz), :]
        return wob.at[c, :, rows_of(zz)]

    hop_s, hop_r, par_s, par_r = (hop_sq, hop_so), (hop_rq, hop_ro), (par_sq, par_so), (par_rq, par_ro)

    def hop_out(c, t, k, h):
        ref = piece(c, zrel(1 - h), t, k)
        return remote(ref, ref, hop_s[t].at[c, k, h - 1], hop_r[t].at[c, k, h - 1], down)

    def hop_in(c, t, k, h):
        ref = piece(c, zrel(-h), t, k)
        return remote(ref, ref, hop_s[t].at[c, k, h - 1], hop_r[t].at[c, k, h - 1], up)

    def swap_out(c, t, k, h):
        ref = piece(c, zrel(-h), t, k)
        return remote(ref, ref, par_s[t].at[c, k, h - 1], par_r[t].at[c, k, h - 1], other)

    def swap_in(c, t, k, h):
        ref = piece(c, zrel(h), t, k)
        return remote(ref, ref, par_s[t].at[c, k, h - 1], par_r[t].at[c, k, h - 1], other)

    def own_swap(c, t):
        ref = whole(c, z, t)
        return remote(ref, ref, own_s.at[c, t], own_r.at[c, t], other)

    def holder(c):
        return jnp.where((c == 0) | (c == 3), 0, 1)

    def nth(t, j, core):
        return (j + core * (PIECES[t] // 2)) % PIECES[t]

    def first_hop(c, t):
        @pl.when(p != holder(c))
        def _():
            own_swap(c, t).wait_recv()

        for j in range(PIECES[t]):
            hop_out(c, t, nth(t, j, p), 1).start()

    def forward(c, t, h):
        for j in range(PIECES[t]):
            k = nth(t, j, p)
            hop_in(c, t, k, h).wait_recv()
            if h < 3 or j < PIECES[t] // 2:
                hop_out(c, t, k, h + 1).start()
            swap_out(c, t, k, h).start()

    def finish(c, t):
        for j in range(PIECES[t] // 2):
            k = nth(t, j, p)
            hop_in(c, t, k, 4).wait_recv()
            swap_out(c, t, k, 4).start()

    def ready(c, t):
        for h in (1, 2, 3):
            for k in range(PIECES[t]):
                swap_in(c, t, k, h).wait_recv()
        for j in range(PIECES[t] // 2):
            swap_in(c, t, nth(t, j, 1 - p), 4).wait_recv()

    def load_and_share(d):
        copies = loads(d)
        for t in range(2):
            for copy in (copies[:6], copies[6:])[t]:
                copy.wait()
            own_swap(layer_of(d), t).start()

    load_and_share(0)
    first_hop(0, 0)

    for copy in small:
        copy.wait()
    second = order[0, p] == 1

    def chosen(first, other_one):
        return jnp.where(second, other_one, first)

    for xx in range(NX):
        for k in range(2):
            cols = slice(k * 512 + xx * 128, k * 512 + xx * 128 + 128)
            tsend[xx, :, k * 128 : k * 128 + 128] = chosen(
                tok_v[0, :, cols].astype(jnp.float32), tok_v[1, :, cols].astype(jnp.float32)
            ).astype(jnp.bfloat16)

    def block(ref, b, size):
        return ref.at[pl.ds(pl.multiple_of(b * size, size), size), :]

    def tok_out(i):
        xx = (x + i) % NX
        return remote(
            tsend.at[xx], block(xbuf.at[0, y], x, SEQ), t_s.at[xx], t_r.at[x], at(z, xx, p, y)
        )

    def tok_in(i):
        xx = (x + i) % NX
        return remote(
            tsend.at[xx], block(xbuf.at[0, y], xx, SEQ), t_s.at[xx], t_r.at[xx], at(z, xx, p, y)
        )

    for i in (2, 1, 3):
        tok_out(i).start()
    xbuf[0, y, pl.ds(pl.multiple_of(x * SEQ, SEQ), SEQ), :] = tsend[x]

    forward(0, 0, 1)
    load_and_share(1)

    for d in range(2):
        c = layer_of(d)
        for zz in range(NZ):
            row = gain[d, :, pl.ds(pl.multiple_of((zz * NX + x) * CHUNK, CHUNK), CHUNK)]
            gbuf[c, :, zz * CHUNK : zz * CHUNK + CHUNK] = jnp.broadcast_to(row, (8, CHUNK))

    def gain_swap(d, c):
        return remote(gbuf.at[c], gbuf.at[c], g_s.at[d], g_r.at[d], other)

    for d in range(2):
        gain_swap(d, layer_of(d)).start()

    def stream_rows(st):
        return pl.ds(st * STREAM, STREAM)

    def stream_out(c, st, i):
        yy = (y + i) % NY
        ref = xbuf.at[c, y, stream_rows(st), :]
        return remote(ref, ref, x_s.at[c, st, yy], x_r.at[c, st, y], at(z, x, p, yy))

    def stream_in(c, st, i):
        yy = (y + i) % NY
        ref = xbuf.at[c, yy, stream_rows(st), :]
        return remote(ref, ref, x_s.at[c, st, yy], x_r.at[c, st, yy], at(z, x, p, yy))

    for i in (2, 1, 3):
        tok_in(i).wait_recv()
    for st in range(2):
        for i in (2, 1, 3):
            stream_out(0, st, i).start()

    row = lax.broadcasted_iota(jnp.int32, (SEQ, 128), 0)
    lane = lax.broadcasted_iota(jnp.int32, (SEQ, 128), 1)
    cut = chosen(boundary[0], boundary[1])
    jump = chosen(offset[0], offset[1])
    places = jnp.where(row < cut, row, row + jump)
    sine, cosine = sine_and_cosine(places.astype(jnp.float32) * freq_v[0:1, :])
    tables[x, 0] = cosine
    tables[x, 1] = jnp.where(lane < 64, -sine, sine)
    end = 0
    doc_from = jnp.zeros((SEQ, 128), jnp.int32)
    doc_to = jnp.zeros((SEQ, 128), jnp.int32)
    for k in range(4):
        end = end + chosen(lengths[0, k], lengths[1, k])
        doc_from = doc_from + jnp.where(row >= end, 1, 0)
        doc_to = doc_to + jnp.where(lane >= end, 1, 0)
    allowed = (doc_from == doc_to) & (lane <= row)
    tables[x, 2] = jnp.where(allowed, 0.0, -jnp.inf).astype(jnp.float32)

    def table_out(i):
        xx = (x + i) % NX
        return remote(tables.at[x], tables.at[x], tab_s.at[xx], tab_r.at[x], at(z, xx, p, y))

    def table_in(i):
        xx = (x + i) % NX
        return remote(tables.at[xx], tables.at[xx], tab_s.at[xx], tab_r.at[xx], at(z, xx, p, y))

    for i in (2, 1, 3):
        table_out(i).start()

    forward(0, 0, 2)
    forward(0, 0, 3)
    first_hop(0, 1)
    first_hop(1, 0)
    first_hop(1, 1)
    finish(0, 0)
    for d in range(2):
        gain_swap(d, 1 - p + d * (1 + 2 * p)).wait_recv()
    for i in (2, 1, 3):
        table_in(i).wait_recv()

    def part_out(c, st, xx):
        return remote(
            psend.at[st, xx],
            precv.at[c, st, x],
            p_s.at[st, xx],
            p_r.at[c, st, x],
            at(z, xx, p, y),
        )

    def part_in(c, st, i):
        xx = (x + i) % NX
        return remote(
            psend.at[st, xx],
            precv.at[c, st, xx],
            p_s.at[st, xx],
            p_r.at[c, st, xx],
            at(z, xx, p, y),
        )

    def attn_ref(c, st, xx):
        return abuf.at[c, st, xx % 2, xx // 2]

    def attn_out(c, st, i):
        xx = (x + i) % NX
        ref = attn_ref(c, st, x)
        return remote(ref, ref, a_s.at[st, xx], a_r.at[c, st, x], at(z, xx, p, y))

    def attn_in(c, st, i):
        xx = (x + i) % NX
        ref = attn_ref(c, st, xx)
        return remote(ref, ref, a_s.at[st, xx], a_r.at[c, st, xx], at(z, xx, p, y))

    def proj_out(c, st, yy):
        return remote(
            osend.at[st, yy], orecv.at[c, st, y], o_s.at[st, yy], o_r.at[c, st, y], at(z, x, p, yy)
        )

    def proj_in(c, st, yy):
        return remote(
            osend.at[st, yy], orecv.at[c, st, yy], o_s.at[st, yy], o_r.at[c, st, yy], at(z, x, p, yy)
        )

    def project_stage(c, st):
        for i in (1, 3, 2):
            attn_in(c, st, i).wait_recv()
        for xx in range(NX):

            @pl.when(xx != x)
            def _():
                part_out(c, st, xx).wait_send()

        def proj(yy):
            cols = pl.ds(pl.multiple_of(yy * PIECE, PIECE), PIECE)
            total = jnp.zeros((STREAM, PIECE), jnp.float32)
            for g in range(2):
                total = total + jnp.dot(
                    abuf[c, st, g].reshape(STREAM, HALF),
                    wob[c, g * HALF : g * HALF + HALF, cols],
                    preferred_element_type=jnp.float32,
                )
            return total

        def proj_tile(i, carry):
            yy = (y + i) % NY
            osend[st, yy] = proj(yy).astype(jnp.bfloat16)
            proj_out(c, st, yy).start()
            return carry

        lax.fori_loop(1, NY, proj_tile, 0)
        oown[st] = proj(y)

    def add_stage(c, st):
        for i in (1, 3, 2):
            proj_in(c, st, (y + i) % NY).wait_recv()
        for i in (1, 2, 3):
            proj_out(c, st, (y + i) % NY).wait_send()
            attn_out(c, st, i).wait_send()
        for b in range(2):
            rows = slice(b * SEQ, b * SEQ + SEQ)
            places = slice(st * STREAM + b * SEQ, st * STREAM + b * SEQ + SEQ)
            total = oown[st, rows, :]
            for i in (1, 2, 3):
                total = total + orecv[c, st, (y + i) % NY, rows, :].astype(jnp.float32)
            total = total + xbuf[c, y, places, :].astype(jnp.float32)
            xbuf[c + 1, y, places, :] = total.astype(jnp.bfloat16)

        @pl.when(c < LAYERS - 1)
        def _():
            for i in (2, 1, 3):
                stream_out(c + 1, st, i).start()

    def qkv_stage(c, st):
        for i in (1, 3, 2):
            stream_in(c, st, i).wait_recv()
        for b in range(2):
            rows = slice(b * SEQ, b * SEQ + SEQ)
            places = slice(st * STREAM + b * SEQ, st * STREAM + b * SEQ + SEQ)
            total = jnp.zeros((SEQ, 1), jnp.float32)
            for yy in range(NY):
                wide = xbuf[c, yy, places, :].astype(jnp.float32)
                total = total + jnp.sum(wide * wide, axis=1, keepdims=True)
                gains = gbuf[c, 0:1, yy * PIECE : yy * PIECE + PIECE]
                xg[yy, rows, :] = (wide * gains).astype(jnp.bfloat16)
            high = total.astype(jnp.bfloat16).astype(jnp.float32)
            mixed = jnp.where(lane == 0, high, jnp.where(lane == 1, total - high, 0.0))
            for g in range(2):
                psend[st, b * 2 + g, :, GROUP:EXTRA] = mixed.astype(jnp.bfloat16)
        if st == 0:
            ready(c, 0)
        for g in range(2):

            def qkv_tile(n, carry):
                cols = pl.ds(pl.multiple_of(g * GROUP + n * 256, 256), 256)
                acc = jnp.zeros((STREAM, 256), jnp.float32)
                for yy in range(NY):
                    acc = acc + jnp.dot(
                        xg[yy],
                        wqkv[c, yy * PIECE : yy * PIECE + PIECE, cols],
                        preferred_element_type=jnp.float32,
                    )
                acc = acc.astype(jnp.bfloat16)
                for b in range(2):
                    psend[st, b * 2 + g, :, pl.ds(pl.multiple_of(n * 256, 256), 256)] = acc[
                        b * SEQ : b * SEQ + SEQ
                    ]
                return carry

            lax.fori_loop(0, GROUP // 256, qkv_tile, 0)
            for b in range(2):

                @pl.when(b * 2 + g != x)
                def _():
                    part_out(c, st, b * 2 + g).start()

    def attention_stage(c, st):
        for i in (1, 3, 2):
            part_in(c, st, i).wait_recv()
        for i in (1, 2, 3):
            stream_out(c, st, i).wait_send()
        mine = st * 2 + x // 2

        def summed(b):
            cols = slice(b * 128, b * 128 + 128)
            total = psend[st, x, :, cols].astype(jnp.float32)
            for i in (1, 2, 3):
                total = total + precv[c, st, (x + i) % NX, :, cols].astype(jnp.float32)
            return total

        square = jnp.sum(summed(6), axis=1, keepdims=True)
        inv_rms = lax.rsqrt(square * (1.0 / WIDTH) + NORM_EPSILON)

        def turned(b):
            value = summed(b) * inv_rms
            return (value * tables[mine, 0] + pltpu.roll(value, 64, 1) * tables[mine, 1]).astype(
                jnp.bfloat16
            )

        keys = turned(4)
        vals = (summed(5) * inv_rms).astype(jnp.bfloat16)
        query = jnp.concatenate([turned(j) for j in range(4)], axis=0)
        scores = lax.dot_general(
            query, keys, (((1,), (1,)), ((), ())), preferred_element_type=jnp.float32
        )
        bias = jnp.concatenate([tables[mine, 2, :, 0:SEQ]] * 4, axis=0)
        scores = scores * HEAD_DIM ** (-0.5) + bias
        top = jnp.max(scores, axis=1, keepdims=True)
        expo = jnp.exp(scores - top)
        weights = (expo / jnp.sum(expo, axis=1, keepdims=True)).astype(jnp.bfloat16)
        mixed = jnp.dot(weights, vals, preferred_element_type=jnp.float32).astype(jnp.bfloat16)
        for j in range(4):
            abuf[c, st, x % 2, x // 2, :, j * 128 : j * 128 + 128] = mixed[j * SEQ : j * SEQ + SEQ]
        for i in (2, 1, 3):
            attn_out(c, st, i).start()

    def only(condition, *events):
        @pl.when(condition)
        def _():
            for event in events:
                event()

    def layer(c, carry):
        later = c > 0
        next1 = later & (c < LAYERS - 1)
        next2 = later & (c < LAYERS - 2)

        only(later, lambda: forward(c, 1, 3))
        qkv_stage(c, 0)

        only(next1, lambda: forward(c + 1, 0, 2))
        only(later, lambda: project_stage(c - 1, 1))

        only(next1, lambda: forward(c + 1, 1, 1))
        only(
            c == 0,
            lambda: forward(c, 1, 1),
            lambda: forward(c + 1, 0, 1),
            lambda: forward(c, 1, 2),
        )
        attention_stage(c, 0)

        only(later, lambda: finish(c, 1))
        only(next2, lambda: first_hop(c + 2, 0))
        only(later, lambda: add_stage(c - 1, 1))

        only(next1, lambda: forward(c + 1, 0, 3))
        only(
            c == 0,
            lambda: forward(c, 1, 3),
            lambda: forward(c + 1, 0, 2),
            lambda: finish(c, 1),
        )
        ready(c, 1)
        project_stage(c, 0)

        only(next1, lambda: forward(c + 1, 1, 2))
        only(c == 0, lambda: forward(c + 1, 1, 1), lambda: first_hop(c + 2, 0))
        qkv_stage(c, 1)

        only(next2, lambda: forward(c + 2, 0, 1))
        only(c == 0, lambda: forward(c + 1, 0, 3), lambda: forward(c + 1, 1, 2))
        add_stage(c, 0)

        only(next1, lambda: finish(c + 1, 0))
        only(next2, lambda: first_hop(c + 2, 1))
        only(
            c == 0,
            lambda: forward(c + 2, 0, 1),
            lambda: finish(c + 1, 0),
            lambda: first_hop(c + 2, 1),
        )
        attention_stage(c, 1)
        return carry

    lax.fori_loop(0, LAYERS, layer, 0)
    project_stage(LAYERS - 1, 1)
    add_stage(LAYERS - 1, 1)

    def done_rows(xx, q):
        return pl.ds(pl.multiple_of(xx * SEQ + q * 32, 32), 32)

    def done_out(i, j):
        xx, q = (x + i) % NX, (p + j) % 2
        return remote(
            xbuf.at[LAYERS, y, done_rows(xx, q), :],
            frecv.at[p, x],
            f_s.at[q, xx],
            f_r.at[p, x],
            at(z, xx, q, y),
        )

    def done_in(i, j):
        xx, q = (x + i) % NX, (p + j) % 2
        return remote(
            xbuf.at[LAYERS, y, done_rows(xx, q), :],
            frecv.at[q, xx],
            f_s.at[q, xx],
            f_r.at[q, xx],
            at(z, xx, q, y),
        )

    away = [(i, j) for i in (2, 1, 3, 0) for j in range(2) if (i, j) != (0, 0)]
    for i, j in away:
        done_out(i, j).start()
    frecv[p, x] = xbuf[LAYERS, y, done_rows(x, p), :]
    for i, j in away:
        done_in(i, j).wait_recv()
    for q in range(2):
        for xx in range(NX):
            out[q, :, xx * 128 : xx * 128 + 128] = frecv[q, xx, :, 0:128]
            out[q, :, 512 + xx * 128 : 512 + xx * 128 + 128] = frecv[q, xx, :, 128:256]

    for i, j in away:
        done_out(i, j).wait_send()
    for i in (1, 2, 3):
        tok_out(i).wait_send()
        table_out(i).wait_send()
    for d in range(2):
        gain_swap(d, layer_of(d)).wait_send()
        for t in range(2):
            own_swap(layer_of(d), t).wait_send()

    def drain(c, carry):
        for t in range(2):
            for k in range(PIECES[t]):
                for h in (1, 2, 3):
                    hop_out(c, t, k, h).wait_send()
                    swap_out(c, t, k, h).wait_send()
            for j in range(PIECES[t] // 2):
                hop_out(c, t, nth(t, j, p), 4).wait_send()
                swap_out(c, t, nth(t, j, p), 4).wait_send()

        return carry

    lax.fori_loop(0, LAYERS, drain, 0)


def per_device(
    tokens,
    w_query,
    w_key,
    w_value,
    w_out,
    norm_gain,
    boundary,
    skip_offset,
    doc_lengths,
    batch_order,
):
    vmem = pl.BlockSpec(memory_space=pltpu.VMEM)
    smem = pl.BlockSpec(memory_space=pltpu.SMEM)
    anywhere = pl.BlockSpec(memory_space=pl.ANY)
    dma = pltpu.SemaphoreType.DMA
    bf16, f32 = jnp.bfloat16, jnp.float32
    return pl.pallas_call(
        stack_kernel,
        out_shape=jax.ShapeDtypeStruct((2, 32, 1024), bf16),
        in_specs=[smem] * 4 + [anywhere] * 7,
        out_specs=vmem,
        scratch_shapes=[
            pltpu.VMEM((LAYERS, SET, QKV), bf16),
            pltpu.VMEM((LAYERS, HEADS, SET), bf16),
            pltpu.VMEM((LAYERS, 8, SET), f32),
            pltpu.VMEM((NX, SEQ, PIECE), bf16),
            pltpu.VMEM((LAYERS + 1, NY, TOK, PIECE), bf16),
            pltpu.VMEM((NY, STREAM, PIECE), bf16),
            pltpu.VMEM((2, NX, SEQ, EXTRA), bf16),
            pltpu.VMEM((LAYERS, 2, NX, SEQ, EXTRA), bf16),
            pltpu.VMEM((LAYERS, 2, 2, 2, SEQ, HALF), bf16),
            pltpu.VMEM((2, NY, STREAM, PIECE), bf16),
            pltpu.VMEM((2, STREAM, PIECE), f32),
            pltpu.VMEM((LAYERS, 2, NY, STREAM, PIECE), bf16),
            pltpu.VMEM((2, NX, 32, PIECE), bf16),
            pltpu.VMEM((2, SEQ, 1024), bf16),
            pltpu.VMEM((8, HEAD_DIM), f32),
            pltpu.VMEM((2, 1, WIDTH), f32),
            pltpu.VMEM((NX, 3, SEQ, HEAD_DIM), f32),
            dma((3,)),
            dma((2, 7)),
            dma((LAYERS, PIECES[0], 4)),
            dma((LAYERS, PIECES[0], 4)),
            dma((LAYERS, PIECES[1], 4)),
            dma((LAYERS, PIECES[1], 4)),
            dma((LAYERS, 2)),
            dma((LAYERS, 2)),
            dma((LAYERS, PIECES[0], 4)),
            dma((LAYERS, PIECES[0], 4)),
            dma((LAYERS, PIECES[1], 4)),
            dma((LAYERS, PIECES[1], 4)),
            dma((2,)),
            dma((2,)),
            dma((NX,)),
            dma((NX,)),
            dma((NX,)),
            dma((NX,)),
            dma((LAYERS, 2, NY)),
            dma((LAYERS, 2, NY)),
            dma((2, NX)),
            dma((LAYERS, 2, NX)),
            dma((2, NX)),
            dma((LAYERS, 2, NX)),
            dma((2, NY)),
            dma((LAYERS, 2, NY)),
            dma((2, NX)),
            dma((2, NX)),
        ],
        compiler_params=pltpu.CompilerParams(
            collective_id=0, has_side_effects=True, vmem_limit_bytes=60 * 1024 * 1024
        ),
    )(
        batch_order,
        boundary,
        skip_offset,
        doc_lengths,
        tokens,
        jnp.asarray(frequencies()),
        norm_gain,
        w_query,
        w_key,
        w_value,
        w_out,
    )


def solution(mesh):
    placed = (
        P("dp", None, "tensor"),
        P(None, "pipe", "dp", "tensor"),
        P(None, "pipe", "dp", "tensor"),
        P(None, "pipe", "dp", "tensor"),
        P(None, "pipe", "tensor", "dp"),
        P(None, "pipe", None),
        P("dp"),
        P("dp"),
        P("dp", None),
        P("dp", None),
    )
    return jax.shard_map(
        per_device, mesh=mesh, in_specs=placed, out_specs=P("dp", "pipe", "tensor"), check_vma=False
    )
```

```python
import math

import jax
import jax.numpy as jnp
import numpy as np
from jax import lax
from jax.experimental import pallas as pl
from jax.experimental.pallas import tpu as pltpu
from jax.sharding import PartitionSpec as P

HEAD_DIM = 128
ROPE_THETA = 500000.0
NORM_EPSILON = 1e-05
MESH = pl.DeviceIdType.MESH

LAYERS = 4
NZ, NX, NY = 8, 4, 4
SEQ = 64
WIDTH = 4096
CHUNK = 128
SET = NZ * CHUNK
QKV = 1536
HEADS = 1024
GROUP = QKV // 2
STREAM = 2 * SEQ
HALF = HEADS // 2
TOK = NX * SEQ
PIECE = SET // NY
PIECES = (4, 2)


TWO_PI_HIGH = 6.28125
TWO_PI_MID = 0.0019340515136718750
TWO_PI_LOW = 2 * math.pi - TWO_PI_HIGH - TWO_PI_MID
SINE_TERMS = [(-1.0) ** k / math.factorial(2 * k + 1) for k in range(10)]
COSINE_TERMS = [(-1.0) ** k / math.factorial(2 * k) for k in range(11)]


def frequencies():
    half = HEAD_DIM // 2
    table = np.float64(ROPE_THETA) ** (-np.arange(half, dtype=np.float64) / half)
    return np.tile(table.astype(np.float32), 2)[None, :].repeat(8, axis=0)


def series(terms, square):
    total = jnp.full(square.shape, terms[-1], jnp.float32)
    for term in terms[-2::-1]:
        total = total * square + term
    return total


def sine_and_cosine(angle):
    turns = jnp.floor(angle * (0.5 / math.pi) + 0.5)
    rest = ((angle - turns * TWO_PI_HIGH) - turns * TWO_PI_MID) - turns * TWO_PI_LOW
    square = rest * rest
    return rest * series(SINE_TERMS, square), series(COSINE_TERMS, square)


PROLOGUE = ((0, 1, 0), (0, 1, 1), (0, 0, 4), (1, 0, 0))
EVENTS = (
    (
        (),
        ((0, 1, 2),),
        ((1, 0, 1), (0, 1, 3)),
        (),
        ((1, 0, 2), (1, 1, 0), (0, 1, 4)),
        (),
        ((1, 0, 3), (1, 1, 1)),
        ((2, 0, 0), (1, 0, 4)),
    ),
    (
        ((1, 1, 2),),
        ((2, 0, 1),),
        (),
        ((1, 1, 3), (2, 1, 0)),
        ((1, 1, 4), (2, 0, 2)),
        (),
        ((2, 0, 3), (2, 1, 1)),
        ((3, 0, 0), (2, 0, 4)),
    ),
    (
        (),
        ((2, 1, 2),),
        ((3, 1, 0), (2, 1, 3), (3, 0, 1)),
        (),
        ((2, 1, 4),),
        ((3, 0, 2),),
        (),
        ((3, 0, 3), (3, 1, 1)),
    ),
    (
        ((3, 0, 4),),
        ((3, 1, 2),),
        ((3, 1, 3),),
        ((3, 1, 4),),
        (),
        (),
        (),
        (),
    ),
)


def stack_kernel(
    order,
    boundary,
    offset,
    lengths,
    tokens,
    freq,
    gain_in,
    wq,
    wk,
    wv,
    wo,
    out,
    wqkv,
    wob,
    gbuf,
    tsend,
    xbuf,
    xg,
    psend,
    precv,
    qsend,
    qrecv,
    abuf,
    osend,
    oown,
    orecv,
    frecv,
    tok_v,
    freq_v,
    gain,
    tables,
    isem,
    lsem,
    hop_sq,
    hop_rq,
    hop_so,
    hop_ro,
    own_sq,
    own_rq,
    own_so,
    own_ro,
    par_sq,
    par_rq,
    par_so,
    par_ro,
    g_s,
    g_r,
    t_s,
    t_r,
    tab_s,
    tab_r,
    x_s,
    x_r,
    p_s,
    p_r,
    q_s,
    q_r,
    a_s,
    a_r,
    o_s,
    o_r,
    f_s,
    f_r,
):
    dp = lax.axis_index("dp")
    p = lax.axis_index("pipe")
    y = lax.axis_index("tensor")
    z = dp // NX
    x = dp % NX
    step = 1 - 2 * p

    def at(zz, xx, pp, yy):
        return {"dp": zz * NX + xx, "pipe": pp, "tensor": yy}

    def zrel(k):
        return (z + step * k + NZ) % NZ

    down = at(zrel(1), x, p, y)
    up = at(zrel(-1), x, p, y)
    other = at(z, x, 1 - p, y)

    def remote(src, dst, s, r, dev):
        return pltpu.make_async_remote_copy(
            src_ref=src, dst_ref=dst, send_sem=s, recv_sem=r, device_id=dev, device_id_type=MESH
        )

    def layer_of(d):
        return p + d * (3 - 2 * p)

    def rows_of(zz):
        return pl.ds(pl.multiple_of(zz * CHUNK, CHUNK), CHUNK)

    def loads(d):
        c = layer_of(d)
        r = rows_of(z)
        copies = []
        for g in range(2):
            for k, (source, width, first) in enumerate(
                ((wq, 512, 0), (wk, 128, 512), (wv, 128, 640))
            ):
                copies.append(
                    pltpu.make_async_copy(
                        source.at[d, 0, :, pl.ds(g * width, width)],
                        wqkv.at[c, r, pl.ds(g * GROUP + first, width)],
                        lsem.at[d, g * 3 + k],
                    )
                )
        copies.append(pltpu.make_async_copy(wo.at[d, 0], wob.at[c, :, r], lsem.at[d, 6]))
        return copies

    barrier = pltpu.get_barrier_semaphore()
    peers = [down, up, other]
    for i in (1, 2, 3):
        peers.append(at(z, (x + i) % NX, p, y))
        peers.append(at(z, (x + i) % NX, 1 - p, y))
        peers.append(at(z, x, p, (y + i) % NY))
    for dev in peers:
        pl.semaphore_signal(barrier, inc=1, device_id=dev, device_id_type=MESH)

    small = [
        pltpu.make_async_copy(tokens, tok_v, isem.at[0]),
        pltpu.make_async_copy(freq, freq_v, isem.at[1]),
        pltpu.make_async_copy(gain_in, gain, isem.at[2]),
    ]
    for copy in loads(0) + small + loads(1):
        copy.start()
    pl.semaphore_wait(barrier, len(peers))

    def piece(c, zz, t, k):
        rows = (CHUNK if t == 0 else HEADS) // PIECES[t]
        if t == 0:
            return wqkv.at[c, pl.ds(pl.multiple_of(zz * CHUNK + k * rows, rows), rows), :]
        return wob.at[c, pl.ds(pl.multiple_of(k * rows, rows), rows), rows_of(zz)]

    hop_s, hop_r = (hop_sq, hop_so), (hop_rq, hop_ro)
    par_s, par_r = (par_sq, par_so), (par_rq, par_ro)
    own_s, own_r = (own_sq, own_so), (own_rq, own_ro)

    def hop_out(c, t, k, h):
        ref = piece(c, zrel(1 - h), t, k)
        return remote(ref, ref, hop_s[t].at[c, k, h - 1], hop_r[t].at[c, k, h - 1], down)

    def hop_in(c, t, k, h):
        ref = piece(c, zrel(-h), t, k)
        return remote(ref, ref, hop_s[t].at[c, k, h - 1], hop_r[t].at[c, k, h - 1], up)

    def swap_out(c, t, k, h):
        ref = piece(c, zrel(-h), t, k)
        return remote(ref, ref, par_s[t].at[c, k, h - 1], par_r[t].at[c, k, h - 1], other)

    def swap_in(c, t, k, h):
        ref = piece(c, zrel(h), t, k)
        return remote(ref, ref, par_s[t].at[c, k, h - 1], par_r[t].at[c, k, h - 1], other)

    def own_swap(c, t, k):
        ref = piece(c, z, t, k)
        return remote(ref, ref, own_s[t].at[c, k], own_r[t].at[c, k], other)

    def holder(c):
        return jnp.where((c == 0) | (c == 3), 0, 1)

    def nth(t, j, core):
        return (j + core * (PIECES[t] // 2)) % PIECES[t]

    def first_hop(c, t):
        for j in range(PIECES[t]):
            k = nth(t, j, p)

            @pl.when(p != holder(c))
            def _():
                own_swap(c, t, k).wait_recv()

            hop_out(c, t, k, 1).start()

    def forward(c, t, h):
        for j in range(PIECES[t]):
            k = nth(t, j, p)
            hop_in(c, t, k, h).wait_recv()
            if h < 3 or j < PIECES[t] // 2:
                hop_out(c, t, k, h + 1).start()
            swap_out(c, t, k, h).start()

    def finish(c, t):
        for j in range(PIECES[t] // 2):
            k = nth(t, j, p)
            hop_in(c, t, k, 4).wait_recv()
            swap_out(c, t, k, 4).start()

    def ready(c, t):
        for h in (1, 2, 3):
            for k in range(PIECES[t]):
                swap_in(c, t, k, h).wait_recv()
        for j in range(PIECES[t] // 2):
            swap_in(c, t, nth(t, j, 1 - p), 4).wait_recv()

    def load_and_share(d):
        copies = loads(d)
        for t in range(2):
            for copy in (copies[:6], copies[6:])[t]:
                copy.wait()
            for j in range(PIECES[t]):
                own_swap(layer_of(d), t, nth(t, j, 1 - p)).start()

    load_and_share(0)
    first_hop(0, 0)

    def run(event):
        c, t, h = event
        if h == 0:
            first_hop(c, t)
        elif h < 4:
            forward(c, t, h)
        else:
            finish(c, t)

    for copy in small:
        copy.wait()
    second = order[0, p] == 1

    def chosen(first, other_one):
        return jnp.where(second, other_one, first)

    for xx in range(NX):
        for k in range(2):
            cols = slice(k * 512 + xx * 128, k * 512 + xx * 128 + 128)
            tsend[xx, :, k * 128 : k * 128 + 128] = chosen(
                tok_v[0, :, cols].astype(jnp.float32), tok_v[1, :, cols].astype(jnp.float32)
            ).astype(jnp.bfloat16)

    def block(ref, b, size):
        return ref.at[pl.ds(pl.multiple_of(b * size, size), size), :]

    def tok_out(i):
        xx = (x + i) % NX
        return remote(
            tsend.at[xx], block(xbuf.at[0, y], x, SEQ), t_s.at[xx], t_r.at[x], at(z, xx, p, y)
        )

    def tok_in(i):
        xx = (x + i) % NX
        return remote(
            tsend.at[xx], block(xbuf.at[0, y], xx, SEQ), t_s.at[xx], t_r.at[xx], at(z, xx, p, y)
        )

    for i in (2, 1, 3):
        tok_out(i).start()
    xbuf[0, y, pl.ds(pl.multiple_of(x * SEQ, SEQ), SEQ), :] = tsend[x]

    forward(0, 0, 1)
    load_and_share(1)

    for d in range(2):
        c = layer_of(d)
        for zz in range(NZ):
            row = gain[d, :, pl.ds(pl.multiple_of((zz * NX + x) * CHUNK, CHUNK), CHUNK)]
            gbuf[c, :, zz * CHUNK : zz * CHUNK + CHUNK] = jnp.broadcast_to(row, (8, CHUNK))

    def gain_swap(d, c):
        return remote(gbuf.at[c], gbuf.at[c], g_s.at[d], g_r.at[d], other)

    for d in range(2):
        gain_swap(d, layer_of(d)).start()

    def stream_rows(st):
        return pl.ds(st * STREAM, STREAM)

    def stream_out(c, st, i):
        yy = (y + i) % NY
        ref = xbuf.at[c, y, stream_rows(st), :]
        return remote(ref, ref, x_s.at[c, st, yy], x_r.at[c, st, y], at(z, x, p, yy))

    def stream_in(c, st, i):
        yy = (y + i) % NY
        ref = xbuf.at[c, yy, stream_rows(st), :]
        return remote(ref, ref, x_s.at[c, st, yy], x_r.at[c, st, yy], at(z, x, p, yy))

    for i in (2, 1, 3):
        tok_in(i).wait_recv()
    for st in range(2):
        for i in (2, 1, 3):
            stream_out(0, st, i).start()

    row = lax.broadcasted_iota(jnp.int32, (SEQ, 128), 0)
    lane = lax.broadcasted_iota(jnp.int32, (SEQ, 128), 1)
    cut = chosen(boundary[0], boundary[1])
    jump = chosen(offset[0], offset[1])
    places = jnp.where(row < cut, row, row + jump)
    sine, cosine = sine_and_cosine(places.astype(jnp.float32) * freq_v[0:1, :])
    tables[x, 0] = cosine
    tables[x, 1] = jnp.where(lane < 64, -sine, sine)
    end = 0
    doc_from = jnp.zeros((SEQ, 128), jnp.int32)
    doc_to = jnp.zeros((SEQ, 128), jnp.int32)
    for k in range(4):
        end = end + chosen(lengths[0, k], lengths[1, k])
        doc_from = doc_from + jnp.where(row >= end, 1, 0)
        doc_to = doc_to + jnp.where(lane >= end, 1, 0)
    allowed = (doc_from == doc_to) & (lane <= row)
    tables[x, 2] = jnp.where(allowed, 0.0, -jnp.inf).astype(jnp.float32)

    def table_out(i):
        xx = (x + i) % NX
        return remote(tables.at[x], tables.at[x], tab_s.at[xx], tab_r.at[x], at(z, xx, p, y))

    def table_in(i):
        xx = (x + i) % NX
        return remote(tables.at[xx], tables.at[xx], tab_s.at[xx], tab_r.at[xx], at(z, xx, p, y))

    for i in (2, 1, 3):
        table_out(i).start()

    forward(0, 0, 2)
    forward(0, 0, 3)
    for event in PROLOGUE:
        run(event)
    for d in range(2):
        gain_swap(d, 1 - p + d * (1 + 2 * p)).wait_recv()
    for i in (2, 1, 3):
        table_in(i).wait_recv()

    def part_out(c, st, xx):
        return remote(
            psend.at[st, xx],
            precv.at[c, st, x],
            p_s.at[st, xx],
            p_r.at[c, st, x],
            at(z, xx, p, y),
        )

    def part_in(c, st, i):
        xx = (x + i) % NX
        return remote(
            psend.at[st, xx],
            precv.at[c, st, xx],
            p_s.at[st, xx],
            p_r.at[c, st, xx],
            at(z, xx, p, y),
        )

    def square_out(c, st, i):
        xx = (x + i) % NX
        return remote(
            qsend.at[st, xx // 2],
            qrecv.at[c, st, x],
            q_s.at[st, xx],
            q_r.at[c, st, x],
            at(z, xx, p, y),
        )

    def square_in(c, st, i):
        xx = (x + i) % NX
        return remote(
            qsend.at[st, xx // 2],
            qrecv.at[c, st, xx],
            q_s.at[st, xx],
            q_r.at[c, st, xx],
            at(z, xx, p, y),
        )

    def attn_ref(c, st, xx):
        return abuf.at[c, st, xx % 2, xx // 2]

    def attn_out(c, st, i):
        xx = (x + i) % NX
        ref = attn_ref(c, st, x)
        return remote(ref, ref, a_s.at[st, xx], a_r.at[c, st, x], at(z, xx, p, y))

    def attn_in(c, st, i):
        xx = (x + i) % NX
        ref = attn_ref(c, st, xx)
        return remote(ref, ref, a_s.at[st, xx], a_r.at[c, st, xx], at(z, xx, p, y))

    def proj_out(c, st, yy):
        return remote(
            osend.at[st, yy], orecv.at[c, st, y], o_s.at[st, yy], o_r.at[c, st, y], at(z, x, p, yy)
        )

    def proj_in(c, st, yy):
        return remote(
            osend.at[st, yy], orecv.at[c, st, yy], o_s.at[st, yy], o_r.at[c, st, yy], at(z, x, p, yy)
        )

    def project_stage(c, st):
        for i in (1, 3, 2):
            attn_in(c, st, i).wait_recv()
        for xx in range(NX):

            @pl.when(xx != x)
            def _():
                part_out(c, st, xx).wait_send()

        def proj(yy):
            cols = pl.ds(pl.multiple_of(yy * PIECE, PIECE), PIECE)
            total = jnp.zeros((STREAM, PIECE), jnp.float32)
            for g in range(2):
                total = total + jnp.dot(
                    abuf[c, st, g].reshape(STREAM, HALF),
                    wob[c, g * HALF : g * HALF + HALF, cols],
                    preferred_element_type=jnp.float32,
                )
            return total

        def proj_tile(i, carry):
            yy = (y + i) % NY
            osend[st, yy] = proj(yy).astype(jnp.bfloat16)
            proj_out(c, st, yy).start()
            return carry

        lax.fori_loop(1, NY, proj_tile, 0)
        oown[st] = proj(y)

    def add_stage(c, st):
        for i in (1, 3, 2):
            proj_in(c, st, (y + i) % NY).wait_recv()
        for i in (1, 2, 3):
            proj_out(c, st, (y + i) % NY).wait_send()
            attn_out(c, st, i).wait_send()
            square_out(c, st, i).wait_send()
        for b in range(2):
            rows = slice(b * SEQ, b * SEQ + SEQ)
            places = slice(st * STREAM + b * SEQ, st * STREAM + b * SEQ + SEQ)
            total = oown[st, rows, :]
            for i in (1, 2, 3):
                total = total + orecv[c, st, (y + i) % NY, rows, :].astype(jnp.float32)
            total = total + xbuf[c, y, places, :].astype(jnp.float32)
            xbuf[c + 1, y, places, :] = total.astype(jnp.bfloat16)

        @pl.when(c < LAYERS - 1)
        def _():
            for i in (2, 1, 3):
                stream_out(c + 1, st, i).start()

    def qkv_stage(c, st):
        for i in (1, 3, 2):
            stream_in(c, st, i).wait_recv()
        for b in range(2):
            rows = slice(b * SEQ, b * SEQ + SEQ)
            places = slice(st * STREAM + b * SEQ, st * STREAM + b * SEQ + SEQ)
            total = jnp.zeros((SEQ, 1), jnp.float32)
            for yy in range(NY):
                wide = xbuf[c, yy, places, :].astype(jnp.float32)
                total = total + jnp.sum(wide * wide, axis=1, keepdims=True)
                gains = gbuf[c, 0:1, yy * PIECE : yy * PIECE + PIECE]
                xg[yy, rows, :] = (wide * gains).astype(jnp.bfloat16)
            flat = jnp.sum(jnp.where(row == lane, total, 0.0), axis=0, keepdims=True)
            qsend[st, b] = jnp.broadcast_to(flat, (8, 128))
        for i in (2, 1, 3):
            square_out(c, st, i).start()
        if st == 0:
            ready(c, 0)
        for g in range(2):

            def qkv_tile(n, carry):
                cols = pl.ds(pl.multiple_of(g * GROUP + n * 256, 256), 256)
                acc = jnp.zeros((STREAM, 256), jnp.float32)
                for yy in range(NY):
                    acc = acc + jnp.dot(
                        xg[yy],
                        wqkv[c, yy * PIECE : yy * PIECE + PIECE, cols],
                        preferred_element_type=jnp.float32,
                    )
                acc = acc.astype(jnp.bfloat16)
                for b in range(2):
                    psend[st, b * 2 + g, :, pl.ds(pl.multiple_of(n * 256, 256), 256)] = acc[
                        b * SEQ : b * SEQ + SEQ
                    ]
                return carry

            lax.fori_loop(0, GROUP // 256, qkv_tile, 0)
            for b in range(2):

                @pl.when(b * 2 + g != x)
                def _():
                    part_out(c, st, b * 2 + g).start()

    def attention_stage(c, st):
        for i in (1, 3, 2):
            square_in(c, st, i).wait_recv()
        flat = qsend[st, x // 2]
        for i in (1, 2, 3):
            flat = flat + qrecv[c, st, (x + i) % NX]
        square = jnp.sum(jnp.where(row == lane, flat[0:1, :], 0.0), axis=1, keepdims=True)
        inv_rms = lax.rsqrt(square * (1.0 / WIDTH) + NORM_EPSILON)
        for i in (1, 3, 2):
            part_in(c, st, i).wait_recv()
        for i in (1, 2, 3):
            stream_out(c, st, i).wait_send()
        mine = st * 2 + x // 2

        def summed(b):
            cols = slice(b * 128, b * 128 + 128)
            total = psend[st, x, :, cols].astype(jnp.float32)
            for i in (1, 2, 3):
                total = total + precv[c, st, (x + i) % NX, :, cols].astype(jnp.float32)
            return total

        def turned(b):
            value = summed(b) * inv_rms
            return (value * tables[mine, 0] + pltpu.roll(value, 64, 1) * tables[mine, 1]).astype(
                jnp.bfloat16
            )

        keys = turned(4)
        vals = (summed(5) * inv_rms).astype(jnp.bfloat16)
        query = jnp.concatenate([turned(j) for j in range(4)], axis=0)
        scores = lax.dot_general(
            query, keys, (((1,), (1,)), ((), ())), preferred_element_type=jnp.float32
        )
        bias = jnp.concatenate([tables[mine, 2, :, 0:SEQ]] * 4, axis=0)
        scores = scores * HEAD_DIM ** (-0.5) + bias
        top = jnp.max(scores, axis=1, keepdims=True)
        expo = jnp.exp(scores - top)
        weights = (expo / jnp.sum(expo, axis=1, keepdims=True)).astype(jnp.bfloat16)
        mixed = jnp.dot(weights, vals, preferred_element_type=jnp.float32).astype(jnp.bfloat16)
        for j in range(4):
            abuf[c, st, x % 2, x // 2, :, j * 128 : j * 128 + 128] = mixed[j * SEQ : j * SEQ + SEQ]
        for i in (2, 1, 3):
            attn_out(c, st, i).start()

    stages = (qkv_stage, attention_stage, project_stage, add_stage)

    def layer(c, carry):
        for slot in range(8):
            for at_layer in range(LAYERS):
                if EVENTS[at_layer][slot]:

                    @pl.when(c == at_layer)
                    def _():
                        for event in EVENTS[at_layer][slot]:
                            run(event)

            if slot == 4:
                ready(c, 1)
            stages[slot // 2](c, slot % 2)
        return carry

    lax.fori_loop(0, LAYERS, layer, 0)

    def done_rows(xx, q):
        return pl.ds(pl.multiple_of(xx * SEQ + q * 32, 32), 32)

    def done_out(i, j):
        xx, q = (x + i) % NX, (p + j) % 2
        return remote(
            xbuf.at[LAYERS, y, done_rows(xx, q), :],
            frecv.at[p, x],
            f_s.at[q, xx],
            f_r.at[p, x],
            at(z, xx, q, y),
        )

    def done_in(i, j):
        xx, q = (x + i) % NX, (p + j) % 2
        return remote(
            xbuf.at[LAYERS, y, done_rows(xx, q), :],
            frecv.at[q, xx],
            f_s.at[q, xx],
            f_r.at[q, xx],
            at(z, xx, q, y),
        )

    away = [(i, j) for i in (2, 1, 3, 0) for j in range(2) if (i, j) != (0, 0)]
    for i, j in away:
        done_out(i, j).start()
    frecv[p, x] = xbuf[LAYERS, y, done_rows(x, p), :]
    for i, j in away:
        done_in(i, j).wait_recv()
    for q in range(2):
        for xx in range(NX):
            out[q, :, xx * 128 : xx * 128 + 128] = frecv[q, xx, :, 0:128]
            out[q, :, 512 + xx * 128 : 512 + xx * 128 + 128] = frecv[q, xx, :, 128:256]

    for i, j in away:
        done_out(i, j).wait_send()
    for i in (1, 2, 3):
        tok_out(i).wait_send()
        table_out(i).wait_send()
    for d in range(2):
        gain_swap(d, layer_of(d)).wait_send()
        for t in range(2):
            for k in range(PIECES[t]):
                own_swap(layer_of(d), t, k).wait_send()

    def drain(c, carry):
        for t in range(2):
            for k in range(PIECES[t]):
                for h in (1, 2, 3):
                    hop_out(c, t, k, h).wait_send()
                    swap_out(c, t, k, h).wait_send()
            for j in range(PIECES[t] // 2):
                hop_out(c, t, nth(t, j, p), 4).wait_send()
                swap_out(c, t, nth(t, j, p), 4).wait_send()

        return carry

    lax.fori_loop(0, LAYERS, drain, 0)


def per_device(
    tokens,
    w_query,
    w_key,
    w_value,
    w_out,
    norm_gain,
    boundary,
    skip_offset,
    doc_lengths,
    batch_order,
):
    vmem = pl.BlockSpec(memory_space=pltpu.VMEM)
    smem = pl.BlockSpec(memory_space=pltpu.SMEM)
    anywhere = pl.BlockSpec(memory_space=pl.ANY)
    dma = pltpu.SemaphoreType.DMA
    bf16, f32 = jnp.bfloat16, jnp.float32
    return pl.pallas_call(
        stack_kernel,
        out_shape=jax.ShapeDtypeStruct((2, 32, 1024), bf16),
        in_specs=[smem] * 4 + [anywhere] * 7,
        out_specs=vmem,
        scratch_shapes=[
            pltpu.VMEM((LAYERS, SET, QKV), bf16),
            pltpu.VMEM((LAYERS, HEADS, SET), bf16),
            pltpu.VMEM((LAYERS, 8, SET), f32),
            pltpu.VMEM((NX, SEQ, PIECE), bf16),
            pltpu.VMEM((LAYERS + 1, NY, TOK, PIECE), bf16),
            pltpu.VMEM((NY, STREAM, PIECE), bf16),
            pltpu.VMEM((2, NX, SEQ, GROUP), bf16),
            pltpu.VMEM((LAYERS, 2, NX, SEQ, GROUP), bf16),
            pltpu.VMEM((2, 2, 8, 128), f32),
            pltpu.VMEM((LAYERS, 2, NX, 8, 128), f32),
            pltpu.VMEM((LAYERS, 2, 2, 2, SEQ, HALF), bf16),
            pltpu.VMEM((2, NY, STREAM, PIECE), bf16),
            pltpu.VMEM((2, STREAM, PIECE), f32),
            pltpu.VMEM((LAYERS, 2, NY, STREAM, PIECE), bf16),
            pltpu.VMEM((2, NX, 32, PIECE), bf16),
            pltpu.VMEM((2, SEQ, 1024), bf16),
            pltpu.VMEM((8, HEAD_DIM), f32),
            pltpu.VMEM((2, 1, WIDTH), f32),
            pltpu.VMEM((NX, 3, SEQ, HEAD_DIM), f32),
            dma((3,)),
            dma((2, 7)),
            dma((LAYERS, PIECES[0], 4)),
            dma((LAYERS, PIECES[0], 4)),
            dma((LAYERS, PIECES[1], 4)),
            dma((LAYERS, PIECES[1], 4)),
            dma((LAYERS, PIECES[0])),
            dma((LAYERS, PIECES[0])),
            dma((LAYERS, PIECES[1])),
            dma((LAYERS, PIECES[1])),
            dma((LAYERS, PIECES[0], 4)),
            dma((LAYERS, PIECES[0], 4)),
            dma((LAYERS, PIECES[1], 4)),
            dma((LAYERS, PIECES[1], 4)),
            dma((2,)),
            dma((2,)),
            dma((NX,)),
            dma((NX,)),
            dma((NX,)),
            dma((NX,)),
            dma((LAYERS, 2, NY)),
            dma((LAYERS, 2, NY)),
            dma((2, NX)),
            dma((LAYERS, 2, NX)),
            dma((2, NX)),
            dma((LAYERS, 2, NX)),
            dma((2, NX)),
            dma((LAYERS, 2, NX)),
            dma((2, NY)),
            dma((LAYERS, 2, NY)),
            dma((2, NX)),
            dma((2, NX)),
        ],
        compiler_params=pltpu.CompilerParams(
            collective_id=0, has_side_effects=True, vmem_limit_bytes=60 * 1024 * 1024
        ),
    )(
        batch_order,
        boundary,
        skip_offset,
        doc_lengths,
        tokens,
        jnp.asarray(frequencies()),
        norm_gain,
        w_query,
        w_key,
        w_value,
        w_out,
    )


def solution(mesh):
    placed = (
        P("dp", None, "tensor"),
        P(None, "pipe", "dp", "tensor"),
        P(None, "pipe", "dp", "tensor"),
        P(None, "pipe", "dp", "tensor"),
        P(None, "pipe", "tensor", "dp"),
        P(None, "pipe", None),
        P("dp"),
        P("dp"),
        P("dp", None),
        P("dp", None),
    )
    return jax.shard_map(
        per_device, mesh=mesh, in_specs=placed, out_specs=P("dp", "pipe", "tensor"), check_vma=False
    )
```

```python
import math

import jax
import jax.numpy as jnp
import numpy as np
from jax import lax
from jax.experimental import pallas as pl
from jax.experimental.pallas import tpu as pltpu
from jax.sharding import PartitionSpec as P

HEAD_DIM = 128
ROPE_THETA = 500000.0
NORM_EPSILON = 1e-05
MESH = pl.DeviceIdType.MESH

LAYERS = 4
NZ, NX, NY = 8, 4, 4
SEQ = 64
WIDTH = 4096
CHUNK = 128
SET = NZ * CHUNK
QKV = 1536
HEADS = 1024
GROUP = QKV // 2
STREAM = 2 * SEQ
HALF = HEADS // 2
TOK = NX * SEQ
PIECE = SET // NY
PIECES = (4, 2)


TWO_PI_HIGH = 6.28125
TWO_PI_MID = 0.0019340515136718750
TWO_PI_LOW = 2 * math.pi - TWO_PI_HIGH - TWO_PI_MID
SINE_TERMS = [(-1.0) ** k / math.factorial(2 * k + 1) for k in range(10)]
COSINE_TERMS = [(-1.0) ** k / math.factorial(2 * k) for k in range(11)]


def frequencies():
    half = HEAD_DIM // 2
    table = np.float64(ROPE_THETA) ** (-np.arange(half, dtype=np.float64) / half)
    return np.tile(table.astype(np.float32), 2)[None, :].repeat(8, axis=0)


def series(terms, square):
    total = jnp.full(square.shape, terms[-1], jnp.float32)
    for term in terms[-2::-1]:
        total = total * square + term
    return total


def sine_and_cosine(angle):
    turns = jnp.floor(angle * (0.5 / math.pi) + 0.5)
    rest = ((angle - turns * TWO_PI_HIGH) - turns * TWO_PI_MID) - turns * TWO_PI_LOW
    square = rest * rest
    return rest * series(SINE_TERMS, square), series(COSINE_TERMS, square)


PROLOGUE = ((0, 1, 0), (0, 1, 1), (0, 0, 4), (1, 0, 0))
EVENTS = (
    (
        (),
        ((0, 1, 2),),
        ((1, 0, 1), (0, 1, 3)),
        (),
        ((1, 0, 2), (1, 1, 0), (0, 1, 4)),
        (),
        ((1, 0, 3), (1, 1, 1)),
        ((2, 0, 0), (1, 0, 4)),
    ),
    (
        ((1, 1, 2),),
        ((2, 0, 1),),
        (),
        ((1, 1, 3), (2, 1, 0)),
        ((1, 1, 4), (2, 0, 2)),
        (),
        ((2, 0, 3), (2, 1, 1)),
        ((3, 0, 0), (2, 0, 4)),
    ),
    (
        (),
        ((2, 1, 2),),
        ((3, 1, 0), (2, 1, 3), (3, 0, 1)),
        (),
        ((2, 1, 4),),
        ((3, 0, 2),),
        (),
        ((3, 0, 3), (3, 1, 1)),
    ),
    (
        ((3, 0, 4),),
        ((3, 1, 2),),
        ((3, 1, 3),),
        ((3, 1, 4),),
        (),
        (),
        (),
        (),
    ),
)


def stack_kernel(
    order,
    boundary,
    offset,
    lengths,
    tokens,
    freq,
    gain_in,
    wq,
    wk,
    wv,
    wo,
    out,
    wqkv,
    wob,
    gbuf,
    tsend,
    xbuf,
    xg,
    psend,
    precv,
    qsend,
    qrecv,
    abuf,
    osend,
    oown,
    orecv,
    frecv,
    tok_v,
    freq_v,
    gain,
    tables,
    isem,
    lsem,
    hop_s,
    hop_rq,
    hop_ro,
    own_s,
    own_rq,
    own_ro,
    par_s,
    par_r,
    g_s,
    g_r,
    t_s,
    t_r,
    tab_s,
    tab_r,
    x_s,
    x_r,
    p_s,
    p_r,
    q_s,
    q_r,
    a_s,
    a_r,
    o_s,
    o_r,
    f_s,
    f_r,
):
    dp = lax.axis_index("dp")
    p = lax.axis_index("pipe")
    y = lax.axis_index("tensor")
    z = dp // NX
    x = dp % NX
    step = 1 - 2 * p

    def at(zz, xx, pp, yy):
        return {"dp": zz * NX + xx, "pipe": pp, "tensor": yy}

    def zrel(k):
        return (z + step * k + NZ) % NZ

    down = at(zrel(1), x, p, y)
    up = at(zrel(-1), x, p, y)
    other = at(z, x, 1 - p, y)

    def remote(src, dst, s, r, dev):
        return pltpu.make_async_remote_copy(
            src_ref=src, dst_ref=dst, send_sem=s, recv_sem=r, device_id=dev, device_id_type=MESH
        )

    def layer_of(d):
        return p + d * (3 - 2 * p)

    def rows_of(zz):
        return pl.ds(pl.multiple_of(zz * CHUNK, CHUNK), CHUNK)

    def loads(d):
        c = layer_of(d)
        r = rows_of(z)
        copies = []
        for g in range(2):
            for source, width, first in ((wq, 512, 0), (wk, 128, 512), (wv, 128, 640)):
                copies.append(
                    pltpu.make_async_copy(
                        source.at[d, 0, :, pl.ds(g * width, width)],
                        wqkv.at[c, r, pl.ds(g * GROUP + first, width)],
                        lsem.at[d, 0],
                    )
                )
        copies.append(pltpu.make_async_copy(wo.at[d, 0], wob.at[c, :, r], lsem.at[d, 1]))
        return copies

    barrier = pltpu.get_barrier_semaphore()
    peers = [down, up, other]
    for i in (1, 2, 3):
        peers.append(at(z, (x + i) % NX, p, y))
        peers.append(at(z, (x + i) % NX, 1 - p, y))
        peers.append(at(z, x, p, (y + i) % NY))
    for dev in peers:
        pl.semaphore_signal(barrier, inc=1, device_id=dev, device_id_type=MESH)

    small = [
        pltpu.make_async_copy(tokens, tok_v, isem.at[0]),
        pltpu.make_async_copy(freq, freq_v, isem.at[1]),
        pltpu.make_async_copy(gain_in, gain, isem.at[2]),
    ]
    for copy in loads(0) + small + loads(1):
        copy.start()
    pl.semaphore_wait(barrier, len(peers))

    def piece(c, zz, t, k):
        rows = (CHUNK if t == 0 else HEADS) // PIECES[t]
        if t == 0:
            return wqkv.at[c, pl.ds(pl.multiple_of(zz * CHUNK + k * rows, rows), rows), :]
        return wob.at[c, pl.ds(pl.multiple_of(k * rows, rows), rows), rows_of(zz)]

    hop_r = (hop_rq, hop_ro)
    own_r = (own_rq, own_ro)

    def whole(c, zz, t):
        if t == 0:
            return wqkv.at[c, rows_of(zz), :]
        return wob.at[c, :, rows_of(zz)]

    def stretch(layers, t):
        return (wqkv, wob)[t].at[layers, pl.ds(0, 448), :]

    def hop_out(c, t, k, h):
        ref = piece(c, zrel(1 - h), t, k)
        return remote(ref, ref, hop_s.at[t], hop_r[t].at[c, k, h - 1], down)

    def hop_in(c, t, k, h):
        ref = piece(c, zrel(-h), t, k)
        return remote(ref, ref, hop_s.at[t], hop_r[t].at[c, k, h - 1], up)

    def swap_out(c, t, k, h):
        ref = piece(c, zrel(-h), t, k)
        return remote(ref, ref, par_s.at[t], par_r.at[c, t], other)

    def own_swap(c, t, k):
        ref = piece(c, z, t, k)
        return remote(ref, ref, own_s.at[t], own_r[t].at[c // 2, k], other)

    def holder(c):
        return jnp.where((c == 0) | (c == 3), 0, 1)

    def nth(t, j, core):
        return (j + core * (PIECES[t] // 2)) % PIECES[t]

    def first_hop(c, t):
        for j in range(PIECES[t]):
            k = nth(t, j, p)

            @pl.when(p != holder(c))
            def _():
                own_swap(c, t, k).wait_recv()

            hop_out(c, t, k, 1).start()

    def forward(c, t, h):
        for j in range(PIECES[t]):
            k = nth(t, j, p)
            hop_in(c, t, k, h).wait_recv()
            if h < 3 or j < PIECES[t] // 2:
                hop_out(c, t, k, h + 1).start()
            swap_out(c, t, k, h).start()

    def finish(c, t):
        for j in range(PIECES[t] // 2):
            k = nth(t, j, p)
            hop_in(c, t, k, 4).wait_recv()
            swap_out(c, t, k, 4).start()

    def ready(c, t):
        ref = stretch(c, t)
        remote(ref, ref, par_s.at[t], par_r.at[c, t], other).wait_recv()

    def load_and_share(d):
        for t in range(2):
            landed = whole(layer_of(d), z, t)
            pltpu.make_async_copy(landed, landed, lsem.at[d, t]).wait()
            for j in range(PIECES[t]):
                own_swap(layer_of(d), t, nth(t, j, 1 - p)).start()

    load_and_share(0)
    first_hop(0, 0)

    def run(event):
        c, t, h = event
        if h == 0:
            first_hop(c, t)
        elif h < 4:
            forward(c, t, h)
        else:
            finish(c, t)

    for copy in small:
        copy.wait()
    second = order[0, p] == 1

    def chosen(first, other_one):
        return jnp.where(second, other_one, first)

    for xx in range(NX):
        for k in range(2):
            cols = slice(k * 512 + xx * 128, k * 512 + xx * 128 + 128)
            tsend[xx, :, k * 128 : k * 128 + 128] = chosen(
                tok_v[0, :, cols].astype(jnp.float32), tok_v[1, :, cols].astype(jnp.float32)
            ).astype(jnp.bfloat16)

    def block(ref, b, size):
        return ref.at[pl.ds(pl.multiple_of(b * size, size), size), :]

    def tok_out(i):
        xx = (x + i) % NX
        return remote(
            tsend.at[xx], block(xbuf.at[0, y], x, SEQ), t_s.at[xx], t_r.at[x], at(z, xx, p, y)
        )

    def tok_in(i):
        xx = (x + i) % NX
        return remote(
            tsend.at[xx], block(xbuf.at[0, y], xx, SEQ), t_s.at[xx], t_r.at[xx], at(z, xx, p, y)
        )

    for i in (2, 1, 3):
        tok_out(i).start()
    xbuf[0, y, pl.ds(pl.multiple_of(x * SEQ, SEQ), SEQ), :] = tsend[x]

    forward(0, 0, 1)
    load_and_share(1)

    for d in range(2):
        c = layer_of(d)
        for zz in range(NZ):
            row = gain[d, :, pl.ds(pl.multiple_of((zz * NX + x) * CHUNK, CHUNK), CHUNK)]
            gbuf[c, :, zz * CHUNK : zz * CHUNK + CHUNK] = jnp.broadcast_to(row, (8, CHUNK))

    def gain_swap(d, c):
        return remote(gbuf.at[c], gbuf.at[c], g_s.at[d], g_r.at[d], other)

    for d in range(2):
        gain_swap(d, layer_of(d)).start()

    def stream_rows(st):
        return pl.ds(st * STREAM, STREAM)

    def stream_out(c, st, i):
        yy = (y + i) % NY
        ref = xbuf.at[c, y, stream_rows(st), :]
        return remote(ref, ref, x_s.at[st, yy], x_r.at[st, y], at(z, x, p, yy))

    def stream_in(c, st, i):
        yy = (y + i) % NY
        ref = xbuf.at[c, yy, stream_rows(st), :]
        return remote(ref, ref, x_s.at[st, yy], x_r.at[st, yy], at(z, x, p, yy))

    for i in (2, 1, 3):
        tok_in(i).wait_recv()
    for st in range(2):
        for i in (2, 1, 3):
            stream_out(0, st, i).start()

    row = lax.broadcasted_iota(jnp.int32, (SEQ, 128), 0)
    lane = lax.broadcasted_iota(jnp.int32, (SEQ, 128), 1)
    cut = chosen(boundary[0], boundary[1])
    jump = chosen(offset[0], offset[1])
    places = jnp.where(row < cut, row, row + jump)
    sine, cosine = sine_and_cosine(places.astype(jnp.float32) * freq_v[0:1, :])
    tables[x, 0] = cosine
    tables[x, 1] = jnp.where(lane < 64, -sine, sine)
    end = 0
    doc_from = jnp.zeros((SEQ, 128), jnp.int32)
    doc_to = jnp.zeros((SEQ, 128), jnp.int32)
    for k in range(4):
        end = end + chosen(lengths[0, k], lengths[1, k])
        doc_from = doc_from + jnp.where(row >= end, 1, 0)
        doc_to = doc_to + jnp.where(lane >= end, 1, 0)
    allowed = (doc_from == doc_to) & (lane <= row)
    tables[x, 2] = jnp.where(allowed, 0.0, -jnp.inf).astype(jnp.float32)

    def table_out(i):
        xx = (x + i) % NX
        return remote(tables.at[x], tables.at[x], tab_s.at[xx], tab_r.at[x], at(z, xx, p, y))

    def table_in(i):
        xx = (x + i) % NX
        return remote(tables.at[xx], tables.at[xx], tab_s.at[xx], tab_r.at[xx], at(z, xx, p, y))

    for i in (2, 1, 3):
        table_out(i).start()

    forward(0, 0, 2)
    forward(0, 0, 3)
    for event in PROLOGUE:
        run(event)
    for d in range(2):
        gain_swap(d, 1 - p + d * (1 + 2 * p)).wait_recv()
    for i in (2, 1, 3):
        table_in(i).wait_recv()

    def part_out(c, st, xx):
        return remote(
            psend.at[st, xx],
            precv.at[c, st, x],
            p_s.at[st, xx],
            p_r.at[st, x],
            at(z, xx, p, y),
        )

    def part_in(c, st, i):
        xx = (x + i) % NX
        return remote(
            psend.at[st, xx],
            precv.at[c, st, xx],
            p_s.at[st, xx],
            p_r.at[st, xx],
            at(z, xx, p, y),
        )

    def square_out(c, st, i):
        xx = (x + i) % NX
        return remote(
            qsend.at[st, xx // 2],
            qrecv.at[c, st, x],
            q_s.at[st, xx],
            q_r.at[st, x],
            at(z, xx, p, y),
        )

    def square_in(c, st, i):
        xx = (x + i) % NX
        return remote(
            qsend.at[st, xx // 2],
            qrecv.at[c, st, xx],
            q_s.at[st, xx],
            q_r.at[st, xx],
            at(z, xx, p, y),
        )

    def attn_ref(c, st, xx):
        return abuf.at[c, st, xx % 2, xx // 2]

    def attn_out(c, st, i):
        xx = (x + i) % NX
        ref = attn_ref(c, st, x)
        return remote(ref, ref, a_s.at[st, xx], a_r.at[st, x], at(z, xx, p, y))

    def attn_in(c, st, i):
        xx = (x + i) % NX
        ref = attn_ref(c, st, xx)
        return remote(ref, ref, a_s.at[st, xx], a_r.at[st, xx], at(z, xx, p, y))

    def proj_out(c, st, yy):
        return remote(
            osend.at[st, yy], orecv.at[c, st, y], o_s.at[st, yy], o_r.at[st, y], at(z, x, p, yy)
        )

    def proj_in(c, st, yy):
        return remote(
            osend.at[st, yy], orecv.at[c, st, yy], o_s.at[st, yy], o_r.at[st, yy], at(z, x, p, yy)
        )

    def project_stage(c, st):
        for i in (1, 3, 2):
            attn_in(c, st, i).wait_recv()
        for xx in range(NX):

            @pl.when(xx != x)
            def _():
                part_out(c, st, xx).wait_send()

        def proj(yy):
            cols = pl.ds(pl.multiple_of(yy * PIECE, PIECE), PIECE)
            total = jnp.zeros((STREAM, PIECE), jnp.float32)
            for g in range(2):
                total = total + jnp.dot(
                    abuf[c, st, g].reshape(STREAM, HALF),
                    wob[c, g * HALF : g * HALF + HALF, cols],
                    preferred_element_type=jnp.float32,
                )
            return total

        def proj_tile(i, carry):
            yy = (y + i) % NY
            osend[st, yy] = proj(yy).astype(jnp.bfloat16)
            proj_out(c, st, yy).start()
            return carry

        lax.fori_loop(1, NY, proj_tile, 0)
        oown[st] = proj(y)

    def add_stage(c, st):
        for i in (1, 3, 2):
            proj_in(c, st, (y + i) % NY).wait_recv()
        for i in (1, 2, 3):
            proj_out(c, st, (y + i) % NY).wait_send()
            attn_out(c, st, i).wait_send()
            square_out(c, st, i).wait_send()
        for b in range(2):
            rows = slice(b * SEQ, b * SEQ + SEQ)
            places = slice(st * STREAM + b * SEQ, st * STREAM + b * SEQ + SEQ)
            total = oown[st, rows, :]
            for i in (1, 2, 3):
                total = total + orecv[c, st, (y + i) % NY, rows, :].astype(jnp.float32)
            total = total + xbuf[c, y, places, :].astype(jnp.float32)
            xbuf[c + 1, y, places, :] = total.astype(jnp.bfloat16)

        @pl.when(c < LAYERS - 1)
        def _():
            for i in (2, 1, 3):
                stream_out(c + 1, st, i).start()

    def qkv_stage(c, st):
        for i in (1, 3, 2):
            stream_in(c, st, i).wait_recv()
        for b in range(2):
            rows = slice(b * SEQ, b * SEQ + SEQ)
            places = slice(st * STREAM + b * SEQ, st * STREAM + b * SEQ + SEQ)
            total = jnp.zeros((SEQ, 1), jnp.float32)
            for yy in range(NY):
                wide = xbuf[c, yy, places, :].astype(jnp.float32)
                total = total + jnp.sum(wide * wide, axis=1, keepdims=True)
                gains = gbuf[c, 0:1, yy * PIECE : yy * PIECE + PIECE]
                xg[yy, rows, :] = (wide * gains).astype(jnp.bfloat16)
            flat = jnp.sum(jnp.where(row == lane, total, 0.0), axis=0, keepdims=True)
            qsend[st, b] = jnp.broadcast_to(flat, (8, 128))
        for i in (2, 1, 3):
            square_out(c, st, i).start()
        if st == 0:
            ready(c, 0)
        for g in range(2):

            def qkv_tile(n, carry):
                cols = pl.ds(pl.multiple_of(g * GROUP + n * 256, 256), 256)
                acc = jnp.zeros((STREAM, 256), jnp.float32)
                for yy in range(NY):
                    acc = acc + jnp.dot(
                        xg[yy],
                        wqkv[c, yy * PIECE : yy * PIECE + PIECE, cols],
                        preferred_element_type=jnp.float32,
                    )
                acc = acc.astype(jnp.bfloat16)
                for b in range(2):
                    psend[st, b * 2 + g, :, pl.ds(pl.multiple_of(n * 256, 256), 256)] = acc[
                        b * SEQ : b * SEQ + SEQ
                    ]
                return carry

            lax.fori_loop(0, GROUP // 256, qkv_tile, 0)
            for b in range(2):

                @pl.when(b * 2 + g != x)
                def _():
                    part_out(c, st, b * 2 + g).start()

    def attention_stage(c, st):
        for i in (1, 3, 2):
            square_in(c, st, i).wait_recv()
        flat = qsend[st, x // 2]
        for i in (1, 2, 3):
            flat = flat + qrecv[c, st, (x + i) % NX]
        square = jnp.sum(jnp.where(row == lane, flat[0:1, :], 0.0), axis=1, keepdims=True)
        inv_rms = lax.rsqrt(square * (1.0 / WIDTH) + NORM_EPSILON)
        for i in (1, 3, 2):
            part_in(c, st, i).wait_recv()
        for i in (1, 2, 3):
            stream_out(c, st, i).wait_send()
        mine = st * 2 + x // 2

        def summed(b):
            cols = slice(b * 128, b * 128 + 128)
            total = psend[st, x, :, cols].astype(jnp.float32)
            for i in (1, 2, 3):
                total = total + precv[c, st, (x + i) % NX, :, cols].astype(jnp.float32)
            return total

        def turned(b):
            value = summed(b) * inv_rms
            return (value * tables[mine, 0] + pltpu.roll(value, 64, 1) * tables[mine, 1]).astype(
                jnp.bfloat16
            )

        keys = turned(4)
        vals = (summed(5) * inv_rms).astype(jnp.bfloat16)
        query = jnp.concatenate([turned(j) for j in range(4)], axis=0)
        scores = lax.dot_general(
            query, keys, (((1,), (1,)), ((), ())), preferred_element_type=jnp.float32
        )
        bias = jnp.concatenate([tables[mine, 2, :, 0:SEQ]] * 4, axis=0)
        scores = scores * HEAD_DIM ** (-0.5) + bias
        top = jnp.max(scores, axis=1, keepdims=True)
        expo = jnp.exp(scores - top)
        weights = (expo / jnp.sum(expo, axis=1, keepdims=True)).astype(jnp.bfloat16)
        mixed = jnp.dot(weights, vals, preferred_element_type=jnp.float32).astype(jnp.bfloat16)
        for j in range(4):
            abuf[c, st, x % 2, x // 2, :, j * 128 : j * 128 + 128] = mixed[j * SEQ : j * SEQ + SEQ]
        for i in (2, 1, 3):
            attn_out(c, st, i).start()

    stages = (qkv_stage, attention_stage, project_stage, add_stage)

    def layer(c, carry):
        for slot in range(8):
            for at_layer in range(LAYERS):
                if EVENTS[at_layer][slot]:

                    @pl.when(c == at_layer)
                    def _():
                        for event in EVENTS[at_layer][slot]:
                            run(event)

            if slot == 4:
                ready(c, 1)
            stages[slot // 2](c, slot % 2)
        return carry

    lax.fori_loop(0, LAYERS, layer, 0)

    def done_rows(xx, q):
        return pl.ds(pl.multiple_of(xx * SEQ + q * 32, 32), 32)

    def done_out(i, j):
        xx, q = (x + i) % NX, (p + j) % 2
        return remote(
            xbuf.at[LAYERS, y, done_rows(xx, q), :],
            frecv.at[p, x],
            f_s.at[q, xx],
            f_r.at[p, x],
            at(z, xx, q, y),
        )

    def done_in(i, j):
        xx, q = (x + i) % NX, (p + j) % 2
        return remote(
            xbuf.at[LAYERS, y, done_rows(xx, q), :],
            frecv.at[q, xx],
            f_s.at[q, xx],
            f_r.at[q, xx],
            at(z, xx, q, y),
        )

    away = [(i, j) for i in (2, 1, 3, 0) for j in range(2) if (i, j) != (0, 0)]
    for i, j in away:
        done_out(i, j).start()
    frecv[p, x] = xbuf[LAYERS, y, done_rows(x, p), :]
    for i, j in away:
        done_in(i, j).wait_recv()
    for q in range(2):
        for xx in range(NX):
            out[q, :, xx * 128 : xx * 128 + 128] = frecv[q, xx, :, 0:128]
            out[q, :, 512 + xx * 128 : 512 + xx * 128 + 128] = frecv[q, xx, :, 128:256]

    for i, j in away:
        done_out(i, j).wait_send()
    for i in (1, 2, 3):
        tok_out(i).wait_send()
        table_out(i).wait_send()
    for d in range(2):
        gain_swap(d, layer_of(d)).wait_send()

    for t in range(2):
        ref = wqkv.at[0, pl.ds(0, 256), :] if t == 0 else wob.at[0, pl.ds(0, 256), :]
        remote(ref, ref, own_s.at[t], own_r[t].at[0, 0], other).wait_send()
        ref = stretch(slice(0, LAYERS), t)
        remote(ref, ref, hop_s.at[t], hop_r[t].at[0, 0, 0], down).wait_send()
        remote(ref, ref, par_s.at[t], par_r.at[0, t], other).wait_send()


def per_device(
    tokens,
    w_query,
    w_key,
    w_value,
    w_out,
    norm_gain,
    boundary,
    skip_offset,
    doc_lengths,
    batch_order,
):
    vmem = pl.BlockSpec(memory_space=pltpu.VMEM)
    smem = pl.BlockSpec(memory_space=pltpu.SMEM)
    anywhere = pl.BlockSpec(memory_space=pl.ANY)
    dma = pltpu.SemaphoreType.DMA
    bf16, f32 = jnp.bfloat16, jnp.float32
    return pl.pallas_call(
        stack_kernel,
        out_shape=jax.ShapeDtypeStruct((2, 32, 1024), bf16),
        in_specs=[smem] * 4 + [anywhere] * 7,
        out_specs=vmem,
        scratch_shapes=[
            pltpu.VMEM((LAYERS, SET, QKV), bf16),
            pltpu.VMEM((LAYERS, HEADS, SET), bf16),
            pltpu.VMEM((LAYERS, 8, SET), f32),
            pltpu.VMEM((NX, SEQ, PIECE), bf16),
            pltpu.VMEM((LAYERS + 1, NY, TOK, PIECE), bf16),
            pltpu.VMEM((NY, STREAM, PIECE), bf16),
            pltpu.VMEM((2, NX, SEQ, GROUP), bf16),
            pltpu.VMEM((LAYERS, 2, NX, SEQ, GROUP), bf16),
            pltpu.VMEM((2, 2, 8, 128), f32),
            pltpu.VMEM((LAYERS, 2, NX, 8, 128), f32),
            pltpu.VMEM((LAYERS, 2, 2, 2, SEQ, HALF), bf16),
            pltpu.VMEM((2, NY, STREAM, PIECE), bf16),
            pltpu.VMEM((2, STREAM, PIECE), f32),
            pltpu.VMEM((LAYERS, 2, NY, STREAM, PIECE), bf16),
            pltpu.VMEM((2, NX, 32, PIECE), bf16),
            pltpu.VMEM((2, SEQ, 1024), bf16),
            pltpu.VMEM((8, HEAD_DIM), f32),
            pltpu.VMEM((2, 1, WIDTH), f32),
            pltpu.VMEM((NX, 3, SEQ, HEAD_DIM), f32),
            dma((3,)),
            dma((2, 2)),
            dma((2,)),
            dma((LAYERS, PIECES[0], 4)),
            dma((LAYERS, PIECES[1], 4)),
            dma((2,)),
            dma((2, PIECES[0])),
            dma((2, PIECES[1])),
            dma((2,)),
            dma((LAYERS, 2)),
        ]
        + [dma((2,))] * 2
        + [dma((NX,))] * 4
        + [dma((2, NX))] * 12,
        compiler_params=pltpu.CompilerParams(
            collective_id=0, has_side_effects=True, vmem_limit_bytes=60 * 1024 * 1024
        ),
    )(
        batch_order,
        boundary,
        skip_offset,
        doc_lengths,
        tokens,
        jnp.asarray(frequencies()),
        norm_gain,
        w_query,
        w_key,
        w_value,
        w_out,
    )


def solution(mesh):
    placed = (
        P("dp", None, "tensor"),
        P(None, "pipe", "dp", "tensor"),
        P(None, "pipe", "dp", "tensor"),
        P(None, "pipe", "dp", "tensor"),
        P(None, "pipe", "tensor", "dp"),
        P(None, "pipe", None),
        P("dp"),
        P("dp"),
        P("dp", None),
        P("dp", None),
    )
    return jax.shard_map(
        per_device, mesh=mesh, in_specs=placed, out_specs=P("dp", "pipe", "tensor"), check_vma=False
    )
```

```python
import math

import jax
import jax.numpy as jnp
import numpy as np
from jax import lax
from jax.experimental import pallas as pl
from jax.experimental.pallas import tpu as pltpu
from jax.sharding import PartitionSpec as P

HEAD_DIM = 128
ROPE_THETA = 500000.0
NORM_EPSILON = 1e-05
MESH = pl.DeviceIdType.MESH

LAYERS = 4
NZ, NX, NY = 8, 4, 4
SEQ = 64
WIDTH = 4096
CHUNK = 128
SET = NZ * CHUNK
QKV = 1536
HEADS = 1024
GROUP = QKV // 2
STREAM = 2 * SEQ
HALF = HEADS // 2
TOK = NX * SEQ
PIECE = SET // NY
PIECES = (4, 2)


TWO_PI_HIGH = 6.28125
TWO_PI_MID = 0.0019340515136718750
TWO_PI_LOW = 2 * math.pi - TWO_PI_HIGH - TWO_PI_MID
SINE_TERMS = [(-1.0) ** k / math.factorial(2 * k + 1) for k in range(10)]
COSINE_TERMS = [(-1.0) ** k / math.factorial(2 * k) for k in range(11)]


def frequencies():
    half = HEAD_DIM // 2
    table = np.float64(ROPE_THETA) ** (-np.arange(half, dtype=np.float64) / half)
    return np.tile(table.astype(np.float32), 2)[None, :].repeat(8, axis=0)


def series(terms, square):
    total = jnp.full(square.shape, terms[-1], jnp.float32)
    for term in terms[-2::-1]:
        total = total * square + term
    return total


def sine_and_cosine(angle):
    turns = jnp.floor(angle * (0.5 / math.pi) + 0.5)
    rest = ((angle - turns * TWO_PI_HIGH) - turns * TWO_PI_MID) - turns * TWO_PI_LOW
    square = rest * rest
    return rest * series(SINE_TERMS, square), series(COSINE_TERMS, square)


PROLOGUE = ((0, 1, 0), (0, 1, 1), (0, 0, 4), (1, 0, 0))
EVENTS = (
    (
        (),
        ((0, 1, 2),),
        ((1, 0, 1), (0, 1, 3)),
        (),
        ((1, 0, 2), (1, 1, 0), (0, 1, 4)),
        (),
        ((1, 0, 3), (1, 1, 1)),
        ((2, 0, 0), (1, 0, 4)),
    ),
    (
        ((1, 1, 2),),
        ((2, 0, 1),),
        (),
        ((1, 1, 3), (2, 1, 0)),
        ((1, 1, 4), (2, 0, 2)),
        (),
        ((2, 0, 3), (2, 1, 1)),
        ((3, 0, 0), (2, 0, 4)),
    ),
    (
        (),
        ((2, 1, 2),),
        ((3, 1, 0), (2, 1, 3), (3, 0, 1)),
        (),
        ((2, 1, 4),),
        ((3, 0, 2),),
        (),
        ((3, 0, 3), (3, 1, 1)),
    ),
    (
        ((3, 0, 4),),
        ((3, 1, 2),),
        ((3, 1, 3),),
        ((3, 1, 4),),
        (),
        (),
        (),
        (),
    ),
)


def stack_kernel(
    order,
    boundary,
    offset,
    lengths,
    tokens,
    freq,
    gain_in,
    wq,
    wk,
    wv,
    wo,
    out,
    wqkv,
    wob,
    gbuf,
    tsend,
    xbuf,
    xg,
    psend,
    precv,
    qsend,
    qrecv,
    abuf,
    osend,
    oown,
    orecv,
    frecv,
    tok_v,
    freq_v,
    gain,
    tables,
    isem,
    lsem,
    hop_s,
    hop_rq,
    hop_ro,
    own_s,
    own_rq,
    own_ro,
    par_s,
    par_r,
    g_s,
    g_r,
    t_s,
    t_r,
    tab_s,
    tab_r,
    x_s,
    x_r,
    p_s,
    p_r,
    q_s,
    q_r,
    a_s,
    a_r,
    o_s,
    o_r,
    f_s,
    f_r,
):
    dp = lax.axis_index("dp")
    p = lax.axis_index("pipe")
    y = lax.axis_index("tensor")
    z = dp // NX
    x = dp % NX
    step = 1 - 2 * p

    def at(zz, xx, pp, yy):
        return {"dp": zz * NX + xx, "pipe": pp, "tensor": yy}

    def zrel(k):
        return (z + step * k + NZ) % NZ

    down = at(zrel(1), x, p, y)
    up = at(zrel(-1), x, p, y)
    other = at(z, x, 1 - p, y)

    def remote(src, dst, s, r, dev):
        return pltpu.make_async_remote_copy(
            src_ref=src, dst_ref=dst, send_sem=s, recv_sem=r, device_id=dev, device_id_type=MESH
        )

    def layer_of(d):
        return p + d * (3 - 2 * p)

    def rows_of(zz):
        return pl.ds(pl.multiple_of(zz * CHUNK, CHUNK), CHUNK)

    def loads(d):
        c = layer_of(d)
        r = rows_of(z)
        copies = []
        for g in range(2):
            for source, width, first in ((wq, 512, 0), (wk, 128, 512), (wv, 128, 640)):
                copies.append(
                    pltpu.make_async_copy(
                        source.at[d, 0, :, pl.ds(g * width, width)],
                        wqkv.at[c, r, pl.ds(g * GROUP + first, width)],
                        lsem.at[d, 0],
                    )
                )
        copies.append(pltpu.make_async_copy(wo.at[d, 0], wob.at[c, :, r], lsem.at[d, 1]))
        return copies

    barrier = pltpu.get_barrier_semaphore()
    peers = [down, up, other]
    for i in (1, 2, 3):
        peers.append(at(z, (x + i) % NX, p, y))
        peers.append(at(z, (x + i) % NX, 1 - p, y))
        peers.append(at(z, x, p, (y + i) % NY))
    for dev in peers:
        pl.semaphore_signal(barrier, inc=1, device_id=dev, device_id_type=MESH)

    small = [
        pltpu.make_async_copy(tokens, tok_v, isem.at[0]),
        pltpu.make_async_copy(freq, freq_v, isem.at[1]),
        pltpu.make_async_copy(gain_in, gain, isem.at[2]),
    ]
    for copy in loads(0) + small + loads(1):
        copy.start()
    pl.semaphore_wait(barrier, len(peers))

    def piece(c, zz, t, k):
        rows = (CHUNK if t == 0 else HEADS) // PIECES[t]
        if t == 0:
            return wqkv.at[c, pl.ds(pl.multiple_of(zz * CHUNK + k * rows, rows), rows), :]
        return wob.at[c, pl.ds(pl.multiple_of(k * rows, rows), rows), rows_of(zz)]

    hop_r = (hop_rq, hop_ro)

    own_r = (own_rq, own_ro)

    def whole(c, zz, t):
        if t == 0:
            return wqkv.at[c, rows_of(zz), :]
        return wob.at[c, :, rows_of(zz)]

    def stretch(layers, t):
        return (wqkv, wob)[t].at[layers, pl.ds(0, 448), :]

    def hop_out(c, t, k, h):
        ref = piece(c, zrel(1 - h), t, k)
        return remote(ref, ref, hop_s.at[t], hop_r[t].at[c, k, h - 1], down)

    def hop_in(c, t, k, h):
        ref = piece(c, zrel(-h), t, k)
        return remote(ref, ref, hop_s.at[t], hop_r[t].at[c, k, h - 1], up)

    def swap_out(c, t, k, h):
        ref = piece(c, zrel(-h), t, k)
        return remote(ref, ref, par_s.at[t], par_r.at[c, t], other)

    def own_swap(c, t, k):
        ref = piece(c, z, t, k)
        return remote(ref, ref, own_s.at[t], own_r[t].at[c // 2, k], other)

    def holder(c):
        return jnp.where((c == 0) | (c == 3), 0, 1)

    def nth(t, j, core):
        return (j + core * (PIECES[t] // 2)) % PIECES[t]

    def first_hop(c, t):
        for j in range(PIECES[t]):
            k = nth(t, j, p)

            @pl.when(p != holder(c))
            def _():
                own_swap(c, t, k).wait_recv()

            hop_out(c, t, k, 1).start()

    def forward(c, t, h):
        for j in range(PIECES[t]):
            k = nth(t, j, p)
            hop_in(c, t, k, h).wait_recv()
            if h < 3 or j < PIECES[t] // 2:
                hop_out(c, t, k, h + 1).start()
            swap_out(c, t, k, h).start()

    def finish(c, t):
        for j in range(PIECES[t] // 2):
            k = nth(t, j, p)
            hop_in(c, t, k, 4).wait_recv()
            swap_out(c, t, k, 4).start()

    def ready(c, t):
        ref = stretch(c, t)
        remote(ref, ref, par_s.at[t], par_r.at[c, t], other).wait_recv()

    def loaded(d, t):
        landed = whole(layer_of(d), z, t)
        pltpu.make_async_copy(landed, landed, lsem.at[d, t]).wait()

    def share(d, t):
        for j in range(PIECES[t]):
            own_swap(layer_of(d), t, nth(t, j, 1 - p)).start()

    loaded(0, 0)
    share(0, 0)
    first_hop(0, 0)
    loaded(0, 1)
    share(0, 1)

    def run(event):
        c, t, h = event
        if h == 0:
            first_hop(c, t)
        elif h < 4:
            forward(c, t, h)
        else:
            finish(c, t)

    for copy in small:
        copy.wait()
    second = order[0, p] == 1

    def chosen(first, other_one):
        return jnp.where(second, other_one, first)

    for xx in range(NX):
        for k in range(2):
            cols = slice(k * 512 + xx * 128, k * 512 + xx * 128 + 128)
            tsend[xx, :, k * 128 : k * 128 + 128] = chosen(
                tok_v[0, :, cols].astype(jnp.float32), tok_v[1, :, cols].astype(jnp.float32)
            ).astype(jnp.bfloat16)

    def block(ref, b, size):
        return ref.at[pl.ds(pl.multiple_of(b * size, size), size), :]

    def tok_out(i):
        xx = (x + i) % NX
        return remote(
            tsend.at[xx], block(xbuf.at[0, y], x, SEQ), t_s.at[0], t_r.at[x], at(z, xx, p, y)
        )

    def tok_in(i):
        xx = (x + i) % NX
        return remote(
            tsend.at[xx], block(xbuf.at[0, y], xx, SEQ), t_s.at[0], t_r.at[xx], at(z, xx, p, y)
        )

    for i in (2, 1, 3):
        tok_out(i).start()
    xbuf[0, y, pl.ds(pl.multiple_of(x * SEQ, SEQ), SEQ), :] = tsend[x]

    forward(0, 0, 1)
    for t in range(2):
        loaded(1, t)
        share(1, t)

    for d in range(2):
        c = layer_of(d)
        for zz in range(NZ):
            row = gain[d, :, pl.ds(pl.multiple_of((zz * NX + x) * CHUNK, CHUNK), CHUNK)]
            gbuf[c, :, zz * CHUNK : zz * CHUNK + CHUNK] = jnp.broadcast_to(row, (8, CHUNK))

    def gain_swap(d, c):
        return remote(gbuf.at[c], gbuf.at[c], g_s.at[0], g_r.at[d], other)

    for d in range(2):
        gain_swap(d, layer_of(d)).start()

    def stream_rows(st):
        return pl.ds(st * STREAM, STREAM)

    def stream_out(c, st, i):
        yy = (y + i) % NY
        ref = xbuf.at[c, y, stream_rows(st), :]
        return remote(ref, ref, x_s.at[st], x_r.at[st, y], at(z, x, p, yy))

    def stream_in(c, st, i):
        yy = (y + i) % NY
        ref = xbuf.at[c, yy, stream_rows(st), :]
        return remote(ref, ref, x_s.at[st], x_r.at[st, yy], at(z, x, p, yy))

    for i in (2, 1, 3):
        tok_in(i).wait_recv()
    for st in range(2):
        for i in (2, 1, 3):
            stream_out(0, st, i).start()

    row = lax.broadcasted_iota(jnp.int32, (SEQ, 128), 0)
    lane = lax.broadcasted_iota(jnp.int32, (SEQ, 128), 1)
    cut = chosen(boundary[0], boundary[1])
    jump = chosen(offset[0], offset[1])
    places = jnp.where(row < cut, row, row + jump)
    sine, cosine = sine_and_cosine(places.astype(jnp.float32) * freq_v[0:1, :])
    tables[x, 0] = cosine
    tables[x, 1] = jnp.where(lane < 64, -sine, sine)
    end = 0
    doc_from = jnp.zeros((SEQ, 128), jnp.int32)
    doc_to = jnp.zeros((SEQ, 128), jnp.int32)
    for k in range(4):
        end = end + chosen(lengths[0, k], lengths[1, k])
        doc_from = doc_from + jnp.where(row >= end, 1, 0)
        doc_to = doc_to + jnp.where(lane >= end, 1, 0)
    allowed = (doc_from == doc_to) & (lane <= row)
    tables[x, 2] = jnp.where(allowed, 0.0, -jnp.inf).astype(jnp.float32)

    def table_out(i):
        xx = (x + i) % NX
        return remote(tables.at[x], tables.at[x], tab_s.at[0], tab_r.at[x], at(z, xx, p, y))

    def table_in(i):
        xx = (x + i) % NX
        return remote(tables.at[xx], tables.at[xx], tab_s.at[0], tab_r.at[xx], at(z, xx, p, y))

    for i in (2, 1, 3):
        table_out(i).start()

    forward(0, 0, 2)
    forward(0, 0, 3)
    for event in PROLOGUE:
        run(event)
    for d in range(2):
        gain_swap(d, 1 - p + d * (1 + 2 * p)).wait_recv()
    for i in (2, 1, 3):
        table_in(i).wait_recv()

    def part_out(c, st, xx):
        return remote(
            psend.at[st, xx],
            precv.at[c, st, x],
            p_s.at[st],
            p_r.at[st, x],
            at(z, xx, p, y),
        )

    def part_in(c, st, i):
        xx = (x + i) % NX
        return remote(
            psend.at[st, xx],
            precv.at[c, st, xx],
            p_s.at[st],
            p_r.at[st, xx],
            at(z, xx, p, y),
        )

    def square_out(c, st, i):
        xx = (x + i) % NX
        return remote(
            qsend.at[st, xx // 2],
            qrecv.at[c, st, x],
            q_s.at[st],
            q_r.at[st, x],
            at(z, xx, p, y),
        )

    def square_in(c, st, i):
        xx = (x + i) % NX
        return remote(
            qsend.at[st, xx // 2],
            qrecv.at[c, st, xx],
            q_s.at[st],
            q_r.at[st, xx],
            at(z, xx, p, y),
        )

    def sent(ref, sem):
        pltpu.make_async_copy(ref, ref, sem).wait()

    def attn_ref(c, st, xx):
        return abuf.at[c, st, xx % 2, xx // 2]

    def attn_out(c, st, i):
        xx = (x + i) % NX
        ref = attn_ref(c, st, x)
        return remote(ref, ref, a_s.at[st], a_r.at[st, x], at(z, xx, p, y))

    def attn_in(c, st, i):
        xx = (x + i) % NX
        ref = attn_ref(c, st, xx)
        return remote(ref, ref, a_s.at[st], a_r.at[st, xx], at(z, xx, p, y))

    def proj_out(c, st, yy):
        return remote(
            osend.at[st, yy], orecv.at[c, st, y], o_s.at[st], o_r.at[st, y], at(z, x, p, yy)
        )

    def proj_in(c, st, yy):
        return remote(
            osend.at[st, yy], orecv.at[c, st, yy], o_s.at[st], o_r.at[st, yy], at(z, x, p, yy)
        )

    def project_stage(c, st):
        for i in (1, 3, 2):
            attn_in(c, st, i).wait_recv()
        sent(psend.at[st, pl.ds(0, 3)], p_s.at[st])

        def proj(yy):
            cols = pl.ds(pl.multiple_of(yy * PIECE, PIECE), PIECE)
            total = jnp.zeros((STREAM, PIECE), jnp.float32)
            for g in range(2):
                total = total + jnp.dot(
                    abuf[c, st, g].reshape(STREAM, HALF),
                    wob[c, g * HALF : g * HALF + HALF, cols],
                    preferred_element_type=jnp.float32,
                )
            return total

        def proj_tile(i, carry):
            yy = (y + i) % NY
            osend[st, yy] = proj(yy).astype(jnp.bfloat16)
            proj_out(c, st, yy).start()
            return carry

        lax.fori_loop(1, NY, proj_tile, 0)
        oown[st] = proj(y)

    def add_stage(c, st):
        for i in (1, 3, 2):
            proj_in(c, st, (y + i) % NY).wait_recv()
        sent(osend.at[st, pl.ds(0, 3)], o_s.at[st])
        sent(psend.at[st, pl.ds(0, 2)], a_s.at[st])
        sent(qrecv.at[c, st, pl.ds(0, 3)], q_s.at[st])
        for b in range(2):
            rows = slice(b * SEQ, b * SEQ + SEQ)
            places = slice(st * STREAM + b * SEQ, st * STREAM + b * SEQ + SEQ)
            total = oown[st, rows, :]
            for i in (1, 2, 3):
                total = total + orecv[c, st, (y + i) % NY, rows, :].astype(jnp.float32)
            total = total + xbuf[c, y, places, :].astype(jnp.float32)
            xbuf[c + 1, y, places, :] = total.astype(jnp.bfloat16)

        @pl.when(c < LAYERS - 1)
        def _():
            for i in (2, 1, 3):
                stream_out(c + 1, st, i).start()

    def qkv_stage(c, st):
        for i in (1, 3, 2):
            stream_in(c, st, i).wait_recv()
        for b in range(2):
            rows = slice(b * SEQ, b * SEQ + SEQ)
            places = slice(st * STREAM + b * SEQ, st * STREAM + b * SEQ + SEQ)
            total = jnp.zeros((SEQ, 1), jnp.float32)
            for yy in range(NY):
                wide = xbuf[c, yy, places, :].astype(jnp.float32)
                total = total + jnp.sum(wide * wide, axis=1, keepdims=True)
                gains = gbuf[c, 0:1, yy * PIECE : yy * PIECE + PIECE]
                xg[yy, rows, :] = (wide * gains).astype(jnp.bfloat16)
            flat = jnp.sum(jnp.where(row == lane, total, 0.0), axis=0, keepdims=True)
            qsend[st, b] = jnp.broadcast_to(flat, (8, 128))
        for i in (2, 1, 3):
            square_out(c, st, i).start()
        if st == 0:
            ready(c, 0)
        for g in range(2):

            def qkv_tile(n, carry):
                cols = pl.ds(pl.multiple_of(g * GROUP + n * 256, 256), 256)
                acc = jnp.zeros((STREAM, 256), jnp.float32)
                for yy in range(NY):
                    acc = acc + jnp.dot(
                        xg[yy],
                        wqkv[c, yy * PIECE : yy * PIECE + PIECE, cols],
                        preferred_element_type=jnp.float32,
                    )
                acc = acc.astype(jnp.bfloat16)
                for b in range(2):
                    psend[st, b * 2 + g, :, pl.ds(pl.multiple_of(n * 256, 256), 256)] = acc[
                        b * SEQ : b * SEQ + SEQ
                    ]
                return carry

            lax.fori_loop(0, GROUP // 256, qkv_tile, 0)
            for b in range(2):

                @pl.when(b * 2 + g != x)
                def _():
                    part_out(c, st, b * 2 + g).start()

    def attention_stage(c, st):
        for i in (1, 3, 2):
            square_in(c, st, i).wait_recv()
        flat = qsend[st, x // 2]
        for i in (1, 2, 3):
            flat = flat + qrecv[c, st, (x + i) % NX]
        square = jnp.sum(jnp.where(row == lane, flat[0:1, :], 0.0), axis=1, keepdims=True)
        inv_rms = lax.rsqrt(square * (1.0 / WIDTH) + NORM_EPSILON)
        for i in (1, 3, 2):
            part_in(c, st, i).wait_recv()
        sent(osend.at[st, pl.ds(0, 3)], x_s.at[st])
        mine = st * 2 + x // 2

        def summed(b):
            cols = slice(b * 128, b * 128 + 128)
            total = psend[st, x, :, cols].astype(jnp.float32)
            for i in (1, 2, 3):
                total = total + precv[c, st, (x + i) % NX, :, cols].astype(jnp.float32)
            return total

        def turned(b):
            value = summed(b) * inv_rms
            return (value * tables[mine, 0] + pltpu.roll(value, 64, 1) * tables[mine, 1]).astype(
                jnp.bfloat16
            )

        keys = turned(4)
        vals = (summed(5) * inv_rms).astype(jnp.bfloat16)
        query = jnp.concatenate([turned(j) for j in range(4)], axis=0)
        scores = lax.dot_general(
            query, keys, (((1,), (1,)), ((), ())), preferred_element_type=jnp.float32
        )
        bias = jnp.concatenate([tables[mine, 2, :, 0:SEQ]] * 4, axis=0)
        scores = scores * HEAD_DIM ** (-0.5) + bias
        top = jnp.max(scores, axis=1, keepdims=True)
        expo = jnp.exp(scores - top)
        weights = (expo / jnp.sum(expo, axis=1, keepdims=True)).astype(jnp.bfloat16)
        mixed = jnp.dot(weights, vals, preferred_element_type=jnp.float32).astype(jnp.bfloat16)
        for j in range(4):
            abuf[c, st, x % 2, x // 2, :, j * 128 : j * 128 + 128] = mixed[j * SEQ : j * SEQ + SEQ]
        for i in (2, 1, 3):
            attn_out(c, st, i).start()

    def done_rows(xx, q):
        return pl.ds(pl.multiple_of(xx * SEQ + q * 32, 32), 32)

    def hand_over(st):
        for xx in (2 * st, 2 * st + 1):
            for q in range(2):
                here = (xx == x) & (q == p)

                @pl.when(jnp.logical_not(here))
                def _():
                    remote(
                        xbuf.at[LAYERS, y, done_rows(xx, q), :],
                        frecv.at[p, x],
                        f_s.at[0],
                        f_r.at[p, x],
                        at(z, xx, q, y),
                    ).start()

                @pl.when(here)
                def _():
                    frecv[p, x] = xbuf[LAYERS, y, done_rows(xx, q), :]

    stages = (qkv_stage, attention_stage, project_stage, add_stage)

    def layer(c, carry):
        for slot in range(8):
            for at_layer in range(LAYERS):
                if EVENTS[at_layer][slot]:

                    @pl.when(c == at_layer)
                    def _():
                        for event in EVENTS[at_layer][slot]:
                            run(event)

            if slot == 4:
                ready(c, 1)
            stages[slot // 2](c, slot % 2)
            if slot >= 6:

                @pl.when(c == LAYERS - 1)
                def _():
                    hand_over(slot - 6)

        return carry

    lax.fori_loop(0, LAYERS, layer, 0)

    def done_in(i, j):
        xx, q = (x + i) % NX, (p + j) % 2
        return remote(
            xbuf.at[LAYERS, y, done_rows(xx, q), :],
            frecv.at[q, xx],
            f_s.at[0],
            f_r.at[q, xx],
            at(z, xx, q, y),
        )

    away = [(i, j) for i in (2, 1, 3, 0) for j in range(2) if (i, j) != (0, 0)]
    for i, j in away:
        done_in(i, j).wait_recv()
    for q in range(2):
        for xx in range(NX):
            out[q, :, xx * 128 : xx * 128 + 128] = frecv[q, xx, :, 0:128]
            out[q, :, 512 + xx * 128 : 512 + xx * 128 + 128] = frecv[q, xx, :, 128:256]

    sent(xbuf.at[LAYERS, 0, pl.ds(0, 224), :], f_s.at[0])
    sent(tsend.at[pl.ds(0, 3)], t_s.at[0])
    sent(tables.at[pl.ds(0, 3)], tab_s.at[0])
    sent(gbuf.at[pl.ds(0, 2)], g_s.at[0])
    for t in range(2):
        ref = wqkv.at[0, pl.ds(0, 256), :] if t == 0 else wob.at[0, pl.ds(0, 256), :]
        remote(ref, ref, own_s.at[t], own_r[t].at[0, 0], other).wait_send()
        ref = stretch(slice(0, LAYERS), t)
        remote(ref, ref, hop_s.at[t], hop_r[t].at[0, 0, 0], down).wait_send()
        remote(ref, ref, par_s.at[t], par_r.at[0, t], other).wait_send()


def per_device(
    tokens,
    w_query,
    w_key,
    w_value,
    w_out,
    norm_gain,
    boundary,
    skip_offset,
    doc_lengths,
    batch_order,
):
    vmem = pl.BlockSpec(memory_space=pltpu.VMEM)
    smem = pl.BlockSpec(memory_space=pltpu.SMEM)
    anywhere = pl.BlockSpec(memory_space=pl.ANY)
    dma = pltpu.SemaphoreType.DMA
    bf16, f32 = jnp.bfloat16, jnp.float32
    return pl.pallas_call(
        stack_kernel,
        out_shape=jax.ShapeDtypeStruct((2, 32, 1024), bf16),
        in_specs=[smem] * 4 + [anywhere] * 7,
        out_specs=vmem,
        scratch_shapes=[
            pltpu.VMEM((LAYERS, SET, QKV), bf16),
            pltpu.VMEM((LAYERS, HEADS, SET), bf16),
            pltpu.VMEM((LAYERS, 8, SET), f32),
            pltpu.VMEM((NX, SEQ, PIECE), bf16),
            pltpu.VMEM((LAYERS + 1, NY, TOK, PIECE), bf16),
            pltpu.VMEM((NY, STREAM, PIECE), bf16),
            pltpu.VMEM((2, NX, SEQ, GROUP), bf16),
            pltpu.VMEM((LAYERS, 2, NX, SEQ, GROUP), bf16),
            pltpu.VMEM((2, 2, 8, 128), f32),
            pltpu.VMEM((LAYERS, 2, NX, 8, 128), f32),
            pltpu.VMEM((LAYERS, 2, 2, 2, SEQ, HALF), bf16),
            pltpu.VMEM((2, NY, STREAM, PIECE), bf16),
            pltpu.VMEM((2, STREAM, PIECE), f32),
            pltpu.VMEM((LAYERS, 2, NY, STREAM, PIECE), bf16),
            pltpu.VMEM((2, NX, 32, PIECE), bf16),
            pltpu.VMEM((2, SEQ, 1024), bf16),
            pltpu.VMEM((8, HEAD_DIM), f32),
            pltpu.VMEM((2, 1, WIDTH), f32),
            pltpu.VMEM((NX, 3, SEQ, HEAD_DIM), f32),
            dma((3,)),
            dma((2, 2)),
            dma((2,)),
            dma((LAYERS, PIECES[0], 4)),
            dma((LAYERS, PIECES[1], 4)),
            dma((2,)),
            dma((2, PIECES[0])),
            dma((2, PIECES[1])),
            dma((2,)),
            dma((LAYERS, 2)),
        ]
        + [dma((1,)), dma((2,))]
        + [dma((1,)), dma((NX,))] * 2
        + [dma((2,)), dma((2, NX))] * 5
        + [dma((1,)), dma((2, NX))],
        compiler_params=pltpu.CompilerParams(
            collective_id=0, has_side_effects=True, vmem_limit_bytes=60 * 1024 * 1024
        ),
    )(
        batch_order,
        boundary,
        skip_offset,
        doc_lengths,
        tokens,
        jnp.asarray(frequencies()),
        norm_gain,
        w_query,
        w_key,
        w_value,
        w_out,
    )


def solution(mesh):
    placed = (
        P("dp", None, "tensor"),
        P(None, "pipe", "dp", "tensor"),
        P(None, "pipe", "dp", "tensor"),
        P(None, "pipe", "dp", "tensor"),
        P(None, "pipe", "tensor", "dp"),
        P(None, "pipe", None),
        P("dp"),
        P("dp"),
        P("dp", None),
        P("dp", None),
    )
    return jax.shard_map(
        per_device, mesh=mesh, in_specs=placed, out_specs=P("dp", "pipe", "tensor"), check_vma=False
    )
```

```python
import math

import jax
import jax.numpy as jnp
import numpy as np
from jax import lax
from jax.experimental import pallas as pl
from jax.experimental.pallas import tpu as pltpu
from jax.sharding import PartitionSpec as P

HEAD_DIM = 128
ROPE_THETA = 500000.0
NORM_EPSILON = 1e-05
MESH = pl.DeviceIdType.MESH

LAYERS = 4
NZ, NX, NY = 8, 4, 4
SEQ = 64
WIDTH = 4096
CHUNK = 128
SET = NZ * CHUNK
QKV = 1536
HEADS = 1024
GROUP = QKV // 2
STREAM = 2 * SEQ
HALF = HEADS // 2
TOK = NX * SEQ
PIECE = SET // NY
PIECES = (4, 2)


TWO_PI_HIGH = 6.28125
TWO_PI_MID = 0.0019340515136718750
TWO_PI_LOW = 2 * math.pi - TWO_PI_HIGH - TWO_PI_MID
SINE_TERMS = [(-1.0) ** k / math.factorial(2 * k + 1) for k in range(10)]
COSINE_TERMS = [(-1.0) ** k / math.factorial(2 * k) for k in range(11)]


def frequencies():
    half = HEAD_DIM // 2
    table = np.float64(ROPE_THETA) ** (-np.arange(half, dtype=np.float64) / half)
    return np.tile(table.astype(np.float32), 2)[None, :].repeat(8, axis=0)


def series(terms, square):
    total = jnp.full(square.shape, terms[-1], jnp.float32)
    for term in terms[-2::-1]:
        total = total * square + term
    return total


def sine_and_cosine(angle):
    turns = jnp.floor(angle * (0.5 / math.pi) + 0.5)
    rest = ((angle - turns * TWO_PI_HIGH) - turns * TWO_PI_MID) - turns * TWO_PI_LOW
    square = rest * rest
    return rest * series(SINE_TERMS, square), series(COSINE_TERMS, square)


PROLOGUE = ((0, 0, 2), (0, 1, 0), (0, 0, 3), (0, 1, 1), (1, 0, 0), (0, 0, 4))
EVENTS = (
    (
        (),
        ((0, 1, 2),),
        ((1, 0, 1),),
        ((0, 1, 3), (1, 1, 0)),
        ((1, 0, 2), (0, 1, 4)),
        ((1, 1, 1),),
        ((1, 0, 3), (2, 1, 0)),
        (),
    ),
    (
        ((1, 0, 4), (1, 1, 2), (2, 0, 0)),
        (),
        ((1, 1, 3), (2, 0, 1)),
        (),
        ((1, 1, 4), (2, 0, 2), (2, 1, 1)),
        (),
        ((2, 0, 3),),
        ((2, 1, 2),),
    ),
    (
        ((3, 0, 0), (2, 0, 4)),
        ((2, 1, 3),),
        ((2, 1, 4), (3, 0, 1), (3, 1, 0)),
        (),
        ((3, 0, 2),),
        ((3, 1, 1),),
        ((3, 0, 3),),
        ((3, 1, 2),),
    ),
    (
        ((3, 0, 4),),
        (),
        ((3, 1, 3),),
        (),
        ((3, 1, 4),),
        (),
        (),
        (),
    ),
)


def stack_kernel(
    order,
    boundary,
    offset,
    lengths,
    tokens,
    freq,
    gain_in,
    wq,
    wk,
    wv,
    wo,
    out,
    wqkv,
    wob,
    gbuf,
    tsend,
    xbuf,
    xg,
    psend,
    precv,
    qsend,
    qrecv,
    abuf,
    osend,
    oown,
    orecv,
    tok_v,
    freq_v,
    gain,
    tables,
    isem,
    lsem,
    hop_s,
    hop_rq,
    hop_ro,
    own_s,
    own_rq,
    own_ro,
    par_s,
    par_r,
    g_s,
    g_r,
    t_s,
    t_r,
    tab_s,
    tab_r,
    x_s,
    x_r,
    p_s,
    p_r,
    q_s,
    q_r,
    a_s,
    a_r,
    o_s,
    o_r,
    f_s,
    f_r,
):
    dp = lax.axis_index("dp")
    p = lax.axis_index("pipe")
    y = lax.axis_index("tensor")
    z = dp // NX
    x = dp % NX
    step = 1 - 2 * p

    def at(zz, xx, pp, yy):
        return {"dp": zz * NX + xx, "pipe": pp, "tensor": yy}

    def zrel(k):
        return (z + step * k + NZ) % NZ

    down = at(zrel(1), x, p, y)
    up = at(zrel(-1), x, p, y)
    other = at(z, x, 1 - p, y)

    def remote(src, dst, s, r, dev):
        return pltpu.make_async_remote_copy(
            src_ref=src, dst_ref=dst, send_sem=s, recv_sem=r, device_id=dev, device_id_type=MESH
        )

    def layer_of(d):
        return p + d * (3 - 2 * p)

    def rows_of(zz):
        return pl.ds(pl.multiple_of(zz * CHUNK, CHUNK), CHUNK)

    def loads(d):
        c = layer_of(d)
        r = rows_of(z)
        copies = []
        for g in range(2):
            for source, width, first in ((wq, 512, 0), (wk, 128, 512), (wv, 128, 640)):
                copies.append(
                    pltpu.make_async_copy(
                        source.at[d, 0, :, pl.ds(g * width, width)],
                        wqkv.at[c, r, pl.ds(g * GROUP + first, width)],
                        lsem.at[d, 0],
                    )
                )
        copies.append(pltpu.make_async_copy(wo.at[d, 0], wob.at[c, :, r], lsem.at[d, 1]))
        return copies

    barrier = pltpu.get_barrier_semaphore()
    peers = [down, up, other]
    for i in (1, 2, 3):
        peers.append(at(z, (x + i) % NX, p, y))
        peers.append(at(z, (x + i) % NX, 1 - p, y))
        peers.append(at(z, x, p, (y + i) % NY))
    for dev in peers:
        pl.semaphore_signal(barrier, inc=1, device_id=dev, device_id_type=MESH)

    small = [
        pltpu.make_async_copy(tokens, tok_v, isem.at[0]),
        pltpu.make_async_copy(freq, freq_v, isem.at[1]),
        pltpu.make_async_copy(gain_in, gain, isem.at[2]),
    ]
    for copy in loads(0) + small + loads(1):
        copy.start()
    pl.semaphore_wait(barrier, len(peers))

    def piece(c, zz, t, k):
        rows = (CHUNK if t == 0 else HEADS) // PIECES[t]
        if t == 0:
            return wqkv.at[c, pl.ds(pl.multiple_of(zz * CHUNK + k * rows, rows), rows), :]
        return wob.at[c, pl.ds(pl.multiple_of(k * rows, rows), rows), rows_of(zz)]

    hop_r = (hop_rq, hop_ro)

    own_r = (own_rq, own_ro)

    def whole(c, zz, t):
        if t == 0:
            return wqkv.at[c, rows_of(zz), :]
        return wob.at[c, :, rows_of(zz)]

    def stretch(layers, t):
        return (wqkv, wob)[t].at[layers, pl.ds(0, 448), :]

    def hop_out(c, t, k, h):
        ref = piece(c, zrel(1 - h), t, k)
        return remote(ref, ref, hop_s.at[t], hop_r[t].at[c, k, h - 1], down)

    def hop_in(c, t, k, h):
        ref = piece(c, zrel(-h), t, k)
        return remote(ref, ref, hop_s.at[t], hop_r[t].at[c, k, h - 1], up)

    def swap_out(c, t, k, h):
        ref = piece(c, zrel(-h), t, k)
        return remote(ref, ref, par_s.at[t], par_r.at[c, t], other)

    def own_swap(c, t, k):
        ref = piece(c, z, t, k)
        return remote(ref, ref, own_s.at[t], own_r[t].at[c // 2, k], other)

    def holder(c):
        return jnp.where((c == 0) | (c == 3), 0, 1)

    def nth(t, j, core):
        return (j + core * (PIECES[t] // 2)) % PIECES[t]

    def first_hop(c, t):
        for j in range(PIECES[t]):
            k = nth(t, j, p)

            @pl.when(p != holder(c))
            def _():
                own_swap(c, t, k).wait_recv()

            hop_out(c, t, k, 1).start()

    def forward(c, t, h):
        for j in range(PIECES[t]):
            k = nth(t, j, p)
            hop_in(c, t, k, h).wait_recv()
            if h < 3 or j < PIECES[t] // 2:
                hop_out(c, t, k, h + 1).start()
            swap_out(c, t, k, h).start()

    def finish(c, t):
        for j in range(PIECES[t] // 2):
            k = nth(t, j, p)
            hop_in(c, t, k, 4).wait_recv()
            swap_out(c, t, k, 4).start()

    def ready(c, t):
        ref = stretch(c, t)
        remote(ref, ref, par_s.at[t], par_r.at[c, t], other).wait_recv()

    def loaded(d, t):
        landed = whole(layer_of(d), z, t)
        pltpu.make_async_copy(landed, landed, lsem.at[d, t]).wait()

    def share(d, t):
        for j in range(PIECES[t]):
            own_swap(layer_of(d), t, nth(t, j, 1 - p)).start()

    loaded(0, 0)
    share(0, 0)
    first_hop(0, 0)
    loaded(0, 1)
    share(0, 1)

    def run(event):
        c, t, h = event
        if h == 0:
            first_hop(c, t)
        elif h < 4:
            forward(c, t, h)
        else:
            finish(c, t)

    for copy in small:
        copy.wait()
    second = order[0, p] == 1

    def chosen(first, other_one):
        return jnp.where(second, other_one, first)

    for xx in range(NX):
        for k in range(2):
            cols = slice(k * 512 + xx * 128, k * 512 + xx * 128 + 128)
            tsend[xx, :, k * 128 : k * 128 + 128] = chosen(
                tok_v[0, :, cols].astype(jnp.float32), tok_v[1, :, cols].astype(jnp.float32)
            ).astype(jnp.bfloat16)

    def block(ref, b, size):
        return ref.at[pl.ds(pl.multiple_of(b * size, size), size), :]

    def tok_out(i):
        xx = (x + i) % NX
        return remote(
            tsend.at[xx], block(xbuf.at[0, y], x, SEQ), t_s.at[0], t_r.at[x], at(z, xx, p, y)
        )

    def tok_in(i):
        xx = (x + i) % NX
        return remote(
            tsend.at[xx], block(xbuf.at[0, y], xx, SEQ), t_s.at[0], t_r.at[xx], at(z, xx, p, y)
        )

    for i in (2, 1, 3):
        tok_out(i).start()
    xbuf[0, y, pl.ds(pl.multiple_of(x * SEQ, SEQ), SEQ), :] = tsend[x]

    forward(0, 0, 1)
    for t in range(2):
        loaded(1, t)
        share(1, t)

    for d in range(2):
        c = layer_of(d)
        for zz in range(NZ):
            row = gain[d, :, pl.ds(pl.multiple_of((zz * NX + x) * CHUNK, CHUNK), CHUNK)]
            gbuf[c, :, zz * CHUNK : zz * CHUNK + CHUNK] = jnp.broadcast_to(row, (8, CHUNK))

    def gain_swap(d, c):
        return remote(gbuf.at[c], gbuf.at[c], g_s.at[0], g_r.at[d], other)

    for d in range(2):
        gain_swap(d, layer_of(d)).start()

    def stream_rows(st):
        return pl.ds(st * STREAM, STREAM)

    def stream_out(c, st, i):
        yy = (y + i) % NY
        ref = xbuf.at[c, y, stream_rows(st), :]
        return remote(ref, ref, x_s.at[st], x_r.at[st, y], at(z, x, p, yy))

    def stream_in(c, st, i):
        yy = (y + i) % NY
        ref = xbuf.at[c, yy, stream_rows(st), :]
        return remote(ref, ref, x_s.at[st], x_r.at[st, yy], at(z, x, p, yy))

    for i in (2, 1, 3):
        tok_in(i).wait_recv()
    for st in range(2):
        for i in (2, 1, 3):
            stream_out(0, st, i).start()

    row = lax.broadcasted_iota(jnp.int32, (SEQ, 128), 0)
    lane = lax.broadcasted_iota(jnp.int32, (SEQ, 128), 1)
    cut = chosen(boundary[0], boundary[1])
    jump = chosen(offset[0], offset[1])
    places = jnp.where(row < cut, row, row + jump)
    sine, cosine = sine_and_cosine(places.astype(jnp.float32) * freq_v[0:1, :])
    tables[x, 0] = cosine
    tables[x, 1] = jnp.where(lane < 64, -sine, sine)
    end = 0
    doc_from = jnp.zeros((SEQ, 128), jnp.int32)
    doc_to = jnp.zeros((SEQ, 128), jnp.int32)
    for k in range(4):
        end = end + chosen(lengths[0, k], lengths[1, k])
        doc_from = doc_from + jnp.where(row >= end, 1, 0)
        doc_to = doc_to + jnp.where(lane >= end, 1, 0)
    allowed = (doc_from == doc_to) & (lane <= row)
    tables[x, 2] = jnp.where(allowed, 0.0, -jnp.inf).astype(jnp.float32)

    def table_out(i):
        xx = (x + i) % NX
        return remote(tables.at[x], tables.at[x], tab_s.at[0], tab_r.at[x], at(z, xx, p, y))

    def table_in(i):
        xx = (x + i) % NX
        return remote(tables.at[xx], tables.at[xx], tab_s.at[0], tab_r.at[xx], at(z, xx, p, y))

    for i in (2, 1, 3):
        table_out(i).start()

    for event in PROLOGUE:
        run(event)
    for d in range(2):
        gain_swap(d, 1 - p + d * (1 + 2 * p)).wait_recv()
    for i in (2, 1, 3):
        table_in(i).wait_recv()

    def part_out(c, st, xx):
        return remote(
            psend.at[st, xx],
            precv.at[c, st, x],
            p_s.at[st],
            p_r.at[st, x],
            at(z, xx, p, y),
        )

    def part_in(c, st, i):
        xx = (x + i) % NX
        return remote(
            psend.at[st, xx],
            precv.at[c, st, xx],
            p_s.at[st],
            p_r.at[st, xx],
            at(z, xx, p, y),
        )

    def square_out(c, st, i):
        xx = (x + i) % NX
        return remote(
            qsend.at[st, xx // 2],
            qrecv.at[c, st, x],
            q_s.at[st],
            q_r.at[st, x],
            at(z, xx, p, y),
        )

    def square_in(c, st, i):
        xx = (x + i) % NX
        return remote(
            qsend.at[st, xx // 2],
            qrecv.at[c, st, xx],
            q_s.at[st],
            q_r.at[st, xx],
            at(z, xx, p, y),
        )

    def sent(ref, sem):
        pltpu.make_async_copy(ref, ref, sem).wait()

    def attn_ref(c, st, xx):
        return abuf.at[c, st, xx % 2, xx // 2]

    def attn_out(c, st, i):
        xx = (x + i) % NX
        ref = attn_ref(c, st, x)
        return remote(ref, ref, a_s.at[st], a_r.at[st, x], at(z, xx, p, y))

    def attn_in(c, st, i):
        xx = (x + i) % NX
        ref = attn_ref(c, st, xx)
        return remote(ref, ref, a_s.at[st], a_r.at[st, xx], at(z, xx, p, y))

    def proj_out(c, st, yy):
        return remote(
            osend.at[st, yy], orecv.at[c, st, y], o_s.at[st], o_r.at[st, y], at(z, x, p, yy)
        )

    def proj_in(c, st, yy):
        return remote(
            osend.at[st, yy], orecv.at[c, st, yy], o_s.at[st], o_r.at[st, yy], at(z, x, p, yy)
        )

    def project_stage(c, st):
        for i in (1, 3, 2):
            attn_in(c, st, i).wait_recv()
        sent(psend.at[st, pl.ds(0, 3)], p_s.at[st])

        def proj(yy):
            cols = pl.ds(pl.multiple_of(yy * PIECE, PIECE), PIECE)
            total = jnp.zeros((STREAM, PIECE), jnp.float32)
            for g in range(2):
                total = total + jnp.dot(
                    abuf[c, st, g].reshape(STREAM, HALF),
                    wob[c, g * HALF : g * HALF + HALF, cols],
                    preferred_element_type=jnp.float32,
                )
            return total

        def proj_tile(i, carry):
            yy = (y + i) % NY
            osend[st, yy] = proj(yy).astype(jnp.bfloat16)
            proj_out(c, st, yy).start()
            return carry

        lax.fori_loop(1, NY, proj_tile, 0)
        oown[st] = proj(y)

    def add_stage(c, st):
        for i in (1, 3, 2):
            proj_in(c, st, (y + i) % NY).wait_recv()
        sent(osend.at[st, pl.ds(0, 3)], o_s.at[st])
        sent(psend.at[st, pl.ds(0, 2)], a_s.at[st])
        sent(qrecv.at[c, st, pl.ds(0, 3)], q_s.at[st])
        for b in range(2):
            rows = slice(b * SEQ, b * SEQ + SEQ)
            places = slice(st * STREAM + b * SEQ, st * STREAM + b * SEQ + SEQ)
            total = oown[st, rows, :]
            for i in (1, 2, 3):
                total = total + orecv[c, st, (y + i) % NY, rows, :].astype(jnp.float32)
            total = total + xbuf[c, y, places, :].astype(jnp.float32)
            xbuf[c + 1, y, places, :] = total.astype(jnp.bfloat16)

        @pl.when(c < LAYERS - 1)
        def _():
            for i in (2, 1, 3):
                stream_out(c + 1, st, i).start()

    def qkv_stage(c, st):
        for i in (1, 3, 2):
            stream_in(c, st, i).wait_recv()
        for b in range(2):
            rows = slice(b * SEQ, b * SEQ + SEQ)
            places = slice(st * STREAM + b * SEQ, st * STREAM + b * SEQ + SEQ)
            total = jnp.zeros((SEQ, 1), jnp.float32)
            for yy in range(NY):
                wide = xbuf[c, yy, places, :].astype(jnp.float32)
                total = total + jnp.sum(wide * wide, axis=1, keepdims=True)
                gains = gbuf[c, 0:1, yy * PIECE : yy * PIECE + PIECE]
                xg[yy, rows, :] = (wide * gains).astype(jnp.bfloat16)
            flat = jnp.sum(jnp.where(row == lane, total, 0.0), axis=0, keepdims=True)
            qsend[st, b] = jnp.broadcast_to(flat, (8, 128))
        for i in (2, 1, 3):
            square_out(c, st, i).start()
        if st == 0:
            ready(c, 0)
        for g in range(2):

            def qkv_tile(n, carry):
                cols = pl.ds(pl.multiple_of(g * GROUP + n * 256, 256), 256)
                acc = jnp.zeros((STREAM, 256), jnp.float32)
                for yy in range(NY):
                    acc = acc + jnp.dot(
                        xg[yy],
                        wqkv[c, yy * PIECE : yy * PIECE + PIECE, cols],
                        preferred_element_type=jnp.float32,
                    )
                acc = acc.astype(jnp.bfloat16)
                for b in range(2):
                    psend[st, b * 2 + g, :, pl.ds(pl.multiple_of(n * 256, 256), 256)] = acc[
                        b * SEQ : b * SEQ + SEQ
                    ]
                return carry

            lax.fori_loop(0, GROUP // 256, qkv_tile, 0)
            for b in range(2):

                @pl.when(b * 2 + g != x)
                def _():
                    part_out(c, st, b * 2 + g).start()

    def attention_stage(c, st):
        for i in (1, 3, 2):
            square_in(c, st, i).wait_recv()
        flat = qsend[st, x // 2]
        for i in (1, 2, 3):
            flat = flat + qrecv[c, st, (x + i) % NX]
        square = jnp.sum(jnp.where(row == lane, flat[0:1, :], 0.0), axis=1, keepdims=True)
        inv_rms = lax.rsqrt(square * (1.0 / WIDTH) + NORM_EPSILON)
        for i in (1, 3, 2):
            part_in(c, st, i).wait_recv()
        sent(osend.at[st, pl.ds(0, 3)], x_s.at[st])
        mine = st * 2 + x // 2

        def summed(b):
            cols = slice(b * 128, b * 128 + 128)
            total = psend[st, x, :, cols].astype(jnp.float32)
            for i in (1, 2, 3):
                total = total + precv[c, st, (x + i) % NX, :, cols].astype(jnp.float32)
            return total

        def turned(b):
            value = summed(b) * inv_rms
            return (value * tables[mine, 0] + pltpu.roll(value, 64, 1) * tables[mine, 1]).astype(
                jnp.bfloat16
            )

        keys = turned(4)
        vals = (summed(5) * inv_rms).astype(jnp.bfloat16)
        query = jnp.concatenate([turned(j) for j in range(4)], axis=0)
        scores = lax.dot_general(
            query, keys, (((1,), (1,)), ((), ())), preferred_element_type=jnp.float32
        )
        bias = jnp.concatenate([tables[mine, 2, :, 0:SEQ]] * 4, axis=0)
        scores = scores * HEAD_DIM ** (-0.5) + bias
        top = jnp.max(scores, axis=1, keepdims=True)
        expo = jnp.exp(scores - top)
        weights = (expo / jnp.sum(expo, axis=1, keepdims=True)).astype(jnp.bfloat16)
        mixed = jnp.dot(weights, vals, preferred_element_type=jnp.float32).astype(jnp.bfloat16)
        for j in range(4):
            abuf[c, st, x % 2, x // 2, :, j * 128 : j * 128 + 128] = mixed[j * SEQ : j * SEQ + SEQ]
        for i in (2, 1, 3):
            attn_out(c, st, i).start()

    def done_rows(xx, q):
        return pl.ds(pl.multiple_of(xx * SEQ + q * 32, 32), 32)

    def hand_over(st):
        for xx in (2 * st, 2 * st + 1):
            for q in range(2):
                here = (xx == x) & (q == p)

                for half in range(2):
                    rows = xbuf.at[LAYERS, y, done_rows(xx, q), pl.ds(half * 128, 128)]
                    first = pl.multiple_of(half * 512 + x * 128, 128)
                    place = out.at[p, :, pl.ds(first, 128)]

                    @pl.when(jnp.logical_not(here))
                    def _():
                        remote(rows, place, f_s.at[0], f_r.at[p, x], at(z, xx, q, y)).start()

                    @pl.when(here)
                    def _():
                        pltpu.make_async_copy(rows, place, isem.at[0]).start()

    stages = (qkv_stage, attention_stage, project_stage, add_stage)

    def layer(c, carry):
        for slot in range(8):
            for at_layer in range(LAYERS):
                if EVENTS[at_layer][slot]:

                    @pl.when(c == at_layer)
                    def _():
                        for event in EVENTS[at_layer][slot]:
                            run(event)

            if slot == 4:
                ready(c, 1)
            stages[slot // 2](c, slot % 2)
            if slot >= 6:

                @pl.when(c == LAYERS - 1)
                def _():
                    hand_over(slot - 6)

        return carry

    lax.fori_loop(0, LAYERS, layer, 0)

    away = [(i, j) for i in (2, 1, 3, 0) for j in range(2) if (i, j) != (0, 0)]
    landed = xbuf.at[LAYERS, y, done_rows(0, 0), :]
    for i, j in away:
        sent(landed, f_r.at[(p + j) % 2, (x + i) % NX])
    sent(landed, isem.at[0])

    sent(xbuf.at[LAYERS, 0, pl.ds(0, 224), :], f_s.at[0])
    sent(tsend.at[pl.ds(0, 3)], t_s.at[0])
    sent(tables.at[pl.ds(0, 3)], tab_s.at[0])
    sent(gbuf.at[pl.ds(0, 2)], g_s.at[0])
    for t in range(2):
        ref = wqkv.at[0, pl.ds(0, 256), :] if t == 0 else wob.at[0, pl.ds(0, 256), :]
        remote(ref, ref, own_s.at[t], own_r[t].at[0, 0], other).wait_send()
        ref = stretch(slice(0, LAYERS), t)
        remote(ref, ref, hop_s.at[t], hop_r[t].at[0, 0, 0], down).wait_send()
        remote(ref, ref, par_s.at[t], par_r.at[0, t], other).wait_send()


def per_device(
    tokens,
    w_query,
    w_key,
    w_value,
    w_out,
    norm_gain,
    boundary,
    skip_offset,
    doc_lengths,
    batch_order,
):
    smem = pl.BlockSpec(memory_space=pltpu.SMEM)
    anywhere = pl.BlockSpec(memory_space=pl.ANY)
    dma = pltpu.SemaphoreType.DMA
    bf16, f32 = jnp.bfloat16, jnp.float32
    return pl.pallas_call(
        stack_kernel,
        out_shape=jax.ShapeDtypeStruct((2, 32, 1024), bf16),
        in_specs=[smem] * 4 + [anywhere] * 7,
        out_specs=anywhere,
        scratch_shapes=[
            pltpu.VMEM((LAYERS, SET, QKV), bf16),
            pltpu.VMEM((LAYERS, HEADS, SET), bf16),
            pltpu.VMEM((LAYERS, 8, SET), f32),
            pltpu.VMEM((NX, SEQ, PIECE), bf16),
            pltpu.VMEM((LAYERS + 1, NY, TOK, PIECE), bf16),
            pltpu.VMEM((NY, STREAM, PIECE), bf16),
            pltpu.VMEM((2, NX, SEQ, GROUP), bf16),
            pltpu.VMEM((LAYERS, 2, NX, SEQ, GROUP), bf16),
            pltpu.VMEM((2, 2, 8, 128), f32),
            pltpu.VMEM((LAYERS, 2, NX, 8, 128), f32),
            pltpu.VMEM((LAYERS, 2, 2, 2, SEQ, HALF), bf16),
            pltpu.VMEM((2, NY, STREAM, PIECE), bf16),
            pltpu.VMEM((2, STREAM, PIECE), f32),
            pltpu.VMEM((LAYERS, 2, NY, STREAM, PIECE), bf16),
            pltpu.VMEM((2, SEQ, 1024), bf16),
            pltpu.VMEM((8, HEAD_DIM), f32),
            pltpu.VMEM((2, 1, WIDTH), f32),
            pltpu.VMEM((NX, 3, SEQ, HEAD_DIM), f32),
            dma((3,)),
            dma((2, 2)),
            dma((2,)),
            dma((LAYERS, PIECES[0], 4)),
            dma((LAYERS, PIECES[1], 4)),
            dma((2,)),
            dma((2, PIECES[0])),
            dma((2, PIECES[1])),
            dma((2,)),
            dma((LAYERS, 2)),
        ]
        + [dma((1,)), dma((2,))]
        + [dma((1,)), dma((NX,))] * 2
        + [dma((2,)), dma((2, NX))] * 5
        + [dma((1,)), dma((2, NX))],
        compiler_params=pltpu.CompilerParams(
            collective_id=0, has_side_effects=True, vmem_limit_bytes=60 * 1024 * 1024
        ),
    )(
        batch_order,
        boundary,
        skip_offset,
        doc_lengths,
        tokens,
        jnp.asarray(frequencies()),
        norm_gain,
        w_query,
        w_key,
        w_value,
        w_out,
    )


def solution(mesh):
    placed = (
        P("dp", None, "tensor"),
        P(None, "pipe", "dp", "tensor"),
        P(None, "pipe", "dp", "tensor"),
        P(None, "pipe", "dp", "tensor"),
        P(None, "pipe", "tensor", "dp"),
        P(None, "pipe", None),
        P("dp"),
        P("dp"),
        P("dp", None),
        P("dp", None),
    )
    return jax.shard_map(
        per_device, mesh=mesh, in_specs=placed, out_specs=P("dp", "pipe", "tensor"), check_vma=False
    )
```

```python
import math

import jax
import jax.numpy as jnp
import numpy as np
from jax import lax
from jax.experimental import pallas as pl
from jax.experimental.pallas import tpu as pltpu
from jax.sharding import PartitionSpec as P

HEAD_DIM = 128
ROPE_THETA = 500000.0
NORM_EPSILON = 1e-05
MESH = pl.DeviceIdType.MESH

LAYERS = 4
NZ, NX, NY = 8, 4, 4
SEQ = 64
WIDTH = 4096
CHUNK = 128
SET = NZ * CHUNK
QKV = 1536
HEADS = 1024
GROUP = QKV // 2
STREAM = 2 * SEQ
HALF = HEADS // 2
TOK = NX * SEQ
PIECE = SET // NY
PIECES = (4, 2)


TWO_PI_HIGH = 6.28125
TWO_PI_MID = 0.0019340515136718750
TWO_PI_LOW = 2 * math.pi - TWO_PI_HIGH - TWO_PI_MID
SINE_TERMS = [(-1.0) ** k / math.factorial(2 * k + 1) for k in range(10)]
COSINE_TERMS = [(-1.0) ** k / math.factorial(2 * k) for k in range(11)]


def frequencies():
    half = HEAD_DIM // 2
    table = np.float64(ROPE_THETA) ** (-np.arange(half, dtype=np.float64) / half)
    return np.tile(table.astype(np.float32), 2)[None, :].repeat(8, axis=0)


def series(terms, square):
    total = jnp.full(square.shape, terms[-1], jnp.float32)
    for term in terms[-2::-1]:
        total = total * square + term
    return total


def sine_and_cosine(angle):
    turns = jnp.floor(angle * (0.5 / math.pi) + 0.5)
    rest = ((angle - turns * TWO_PI_HIGH) - turns * TWO_PI_MID) - turns * TWO_PI_LOW
    square = rest * rest
    return rest * series(SINE_TERMS, square), series(COSINE_TERMS, square)


PROLOGUE = ((0, 0, 2), (0, 1, 0), (0, 0, 3), (0, 1, 1), (1, 0, 0), (0, 0, 4))
EVENTS = (
    (
        (),
        ((0, 1, 2),),
        ((1, 0, 1),),
        ((0, 1, 3), (1, 1, 0)),
        ((1, 0, 2), (0, 1, 4)),
        ((1, 1, 1),),
        ((1, 0, 3), (2, 1, 0)),
        (),
    ),
    (
        ((1, 0, 4), (1, 1, 2), (2, 0, 0)),
        (),
        ((1, 1, 3), (2, 0, 1)),
        (),
        ((1, 1, 4), (2, 0, 2), (2, 1, 1)),
        (),
        ((2, 0, 3),),
        ((2, 1, 2),),
    ),
    (
        ((3, 0, 0), (2, 0, 4)),
        ((2, 1, 3),),
        ((2, 1, 4), (3, 0, 1), (3, 1, 0)),
        (),
        ((3, 0, 2),),
        ((3, 1, 1),),
        ((3, 0, 3),),
        ((3, 1, 2),),
    ),
    (
        ((3, 0, 4),),
        (),
        ((3, 1, 3),),
        (),
        ((3, 1, 4),),
        (),
        (),
        (),
    ),
)


def stack_kernel(
    order,
    boundary,
    offset,
    lengths,
    tokens,
    freq,
    gain_in,
    wq,
    wk,
    wv,
    wo,
    out,
    wqkv,
    wob,
    gbuf,
    tsend,
    xbuf,
    xg,
    psend,
    precv,
    qsend,
    qrecv,
    abuf,
    osend,
    oown,
    orecv,
    tok_v,
    freq_v,
    gain,
    tables,
    isem,
    lsem,
    hop_s,
    hop_rq,
    hop_ro,
    own_s,
    own_rq,
    own_ro,
    par_s,
    par_r,
    g_s,
    g_r,
    t_s,
    t_r,
    tab_s,
    tab_r,
    x_s,
    x_r,
    p_s,
    p_r,
    q_s,
    q_r,
    a_s,
    a_r,
    o_s,
    o_r,
    f_s,
    f_r,
):
    dp = lax.axis_index("dp")
    p = lax.axis_index("pipe")
    y = lax.axis_index("tensor")
    z = dp // NX
    x = dp % NX
    step = 1 - 2 * p

    def at(zz, xx, pp, yy):
        return {"dp": zz * NX + xx, "pipe": pp, "tensor": yy}

    def zrel(k):
        return (z + step * k + NZ) % NZ

    down = at(zrel(1), x, p, y)
    up = at(zrel(-1), x, p, y)
    other = at(z, x, 1 - p, y)

    def remote(src, dst, s, r, dev):
        return pltpu.make_async_remote_copy(
            src_ref=src, dst_ref=dst, send_sem=s, recv_sem=r, device_id=dev, device_id_type=MESH
        )

    def layer_of(d):
        return p + d * (3 - 2 * p)

    def rows_of(zz):
        return pl.ds(pl.multiple_of(zz * CHUNK, CHUNK), CHUNK)

    def loads(d):
        c = layer_of(d)
        r = rows_of(z)
        copies = []
        for g in range(2):
            for source, width, first in ((wq, 512, 0), (wk, 128, 512), (wv, 128, 640)):
                copies.append(
                    pltpu.make_async_copy(
                        source.at[d, 0, :, pl.ds(g * width, width)],
                        wqkv.at[c, r, pl.ds(g * GROUP + first, width)],
                        lsem.at[d, 0],
                    )
                )
        copies.append(pltpu.make_async_copy(wo.at[d, 0], wob.at[c, :, r], lsem.at[d, 1]))
        return copies

    barrier = pltpu.get_barrier_semaphore()
    peers = [down, up, other]
    for i in (1, 2, 3):
        peers.append(at(z, (x + i) % NX, p, y))
        peers.append(at(z, (x + i) % NX, 1 - p, y))
        peers.append(at(z, x, p, (y + i) % NY))
    for dev in peers:
        pl.semaphore_signal(barrier, inc=1, device_id=dev, device_id_type=MESH)

    small = [
        pltpu.make_async_copy(tokens, tok_v, isem.at[0]),
        pltpu.make_async_copy(freq, freq_v, isem.at[1]),
        pltpu.make_async_copy(gain_in, gain, isem.at[2]),
    ]
    for copy in loads(0) + small + loads(1):
        copy.start()
    pl.semaphore_wait(barrier, len(peers))

    def piece(c, zz, t, k):
        rows = (CHUNK if t == 0 else HEADS) // PIECES[t]
        if t == 0:
            return wqkv.at[c, pl.ds(pl.multiple_of(zz * CHUNK + k * rows, rows), rows), :]
        return wob.at[c, pl.ds(pl.multiple_of(k * rows, rows), rows), rows_of(zz)]

    hop_r = (hop_rq, hop_ro)

    own_r = (own_rq, own_ro)

    def whole(c, zz, t):
        if t == 0:
            return wqkv.at[c, rows_of(zz), :]
        return wob.at[c, :, rows_of(zz)]

    def stretch(layers, t):
        return (wqkv, wob)[t].at[layers, pl.ds(0, 448), :]

    def hop_out(c, t, k, h):
        ref = piece(c, zrel(1 - h), t, k)
        return remote(ref, ref, hop_s.at[t], hop_r[t].at[c, k, h - 1], down)

    def hop_in(c, t, k, h):
        ref = piece(c, zrel(-h), t, k)
        return remote(ref, ref, hop_s.at[t], hop_r[t].at[c, k, h - 1], up)

    def swap_out(c, t, k, h):
        ref = piece(c, zrel(-h), t, k)
        return remote(ref, ref, par_s.at[t], par_r.at[c, t], other)

    def own_swap(c, t, k):
        ref = piece(c, z, t, k)
        return remote(ref, ref, own_s.at[t], own_r[t].at[c // 2, k], other)

    def holder(c):
        return jnp.where((c == 0) | (c == 3), 0, 1)

    def nth(t, j, core):
        return (j + core * (PIECES[t] // 2)) % PIECES[t]

    def first_hop(c, t):
        for j in range(PIECES[t]):
            k = nth(t, j, p)

            @pl.when(p != holder(c))
            def _():
                own_swap(c, t, k).wait_recv()

            hop_out(c, t, k, 1).start()

    def forward(c, t, h):
        for j in range(PIECES[t]):
            k = nth(t, j, p)
            hop_in(c, t, k, h).wait_recv()
            if h < 3 or j < PIECES[t] // 2:
                hop_out(c, t, k, h + 1).start()
            swap_out(c, t, k, h).start()

    def finish(c, t):
        for j in range(PIECES[t] // 2):
            k = nth(t, j, p)
            hop_in(c, t, k, 4).wait_recv()
            swap_out(c, t, k, 4).start()

    def ready(c, t):
        ref = stretch(c, t)
        remote(ref, ref, par_s.at[t], par_r.at[c, t], other).wait_recv()

    def loaded(d, t):
        landed = whole(layer_of(d), z, t)
        pltpu.make_async_copy(landed, landed, lsem.at[d, t]).wait()

    def share(d, t):
        for j in range(PIECES[t]):
            own_swap(layer_of(d), t, nth(t, j, 1 - p)).start()

    loaded(0, 0)
    share(0, 0)
    first_hop(0, 0)
    loaded(0, 1)
    share(0, 1)

    def run(event):
        c, t, h = event
        if h == 0:
            first_hop(c, t)
        elif h < 4:
            forward(c, t, h)
        else:
            finish(c, t)

    for copy in small:
        copy.wait()
    second = order[0, p] == 1

    def chosen(first, other_one):
        return jnp.where(second, other_one, first)

    for xx in range(NX):
        for k in range(2):
            cols = slice(k * 512 + xx * 128, k * 512 + xx * 128 + 128)
            tsend[xx, :, k * 128 : k * 128 + 128] = chosen(
                tok_v[0, :, cols].astype(jnp.float32), tok_v[1, :, cols].astype(jnp.float32)
            ).astype(jnp.bfloat16)

    def block(ref, b, size):
        return ref.at[pl.ds(pl.multiple_of(b * size, size), size), :]

    def tok_out(i):
        xx = (x + i) % NX
        return remote(
            tsend.at[xx], block(xbuf.at[0, y], x, SEQ), t_s.at[0], t_r.at[x], at(z, xx, p, y)
        )

    def tok_in(i):
        xx = (x + i) % NX
        return remote(
            tsend.at[xx], block(xbuf.at[0, y], xx, SEQ), t_s.at[0], t_r.at[xx], at(z, xx, p, y)
        )

    for i in (1, 3, 2):
        tok_out(i).start()
    xbuf[0, y, pl.ds(pl.multiple_of(x * SEQ, SEQ), SEQ), :] = tsend[x]

    forward(0, 0, 1)
    for t in range(2):
        loaded(1, t)
        share(1, t)

    for d in range(2):
        c = layer_of(d)
        for zz in range(NZ):
            row = gain[d, :, pl.ds(pl.multiple_of((zz * NX + x) * CHUNK, CHUNK), CHUNK)]
            gbuf[c, :, zz * CHUNK : zz * CHUNK + CHUNK] = jnp.broadcast_to(row, (8, CHUNK))

    def gain_swap(d, c):
        return remote(gbuf.at[c], gbuf.at[c], g_s.at[0], g_r.at[d], other)

    for d in range(2):
        gain_swap(d, layer_of(d)).start()

    def stream_rows(st):
        return pl.ds(st * STREAM, STREAM)

    def stream_out(c, st, i):
        yy = (y + i) % NY
        ref = xbuf.at[c, y, stream_rows(st), :]
        return remote(ref, ref, x_s.at[st], x_r.at[st, y], at(z, x, p, yy))

    def stream_in(c, st, i):
        yy = (y + i) % NY
        ref = xbuf.at[c, yy, stream_rows(st), :]
        return remote(ref, ref, x_s.at[st], x_r.at[st, yy], at(z, x, p, yy))

    for i in (1, 3, 2):
        tok_in(i).wait_recv()
    for st in range(2):
        for i in (1, 3, 2):
            stream_out(0, st, i).start()

    row = lax.broadcasted_iota(jnp.int32, (SEQ, 128), 0)
    lane = lax.broadcasted_iota(jnp.int32, (SEQ, 128), 1)
    cut = chosen(boundary[0], boundary[1])
    jump = chosen(offset[0], offset[1])
    places = jnp.where(row < cut, row, row + jump)
    sine, cosine = sine_and_cosine(places.astype(jnp.float32) * freq_v[0:1, :])
    tables[x, 0] = cosine
    tables[x, 1] = jnp.where(lane < 64, -sine, sine)
    end = 0
    doc_from = jnp.zeros((SEQ, 128), jnp.int32)
    doc_to = jnp.zeros((SEQ, 128), jnp.int32)
    for k in range(4):
        end = end + chosen(lengths[0, k], lengths[1, k])
        doc_from = doc_from + jnp.where(row >= end, 1, 0)
        doc_to = doc_to + jnp.where(lane >= end, 1, 0)
    allowed = (doc_from == doc_to) & (lane <= row)
    tables[x, 2] = jnp.where(allowed, 0.0, -jnp.inf).astype(jnp.float32)

    def table_out(i):
        xx = (x + i) % NX
        return remote(tables.at[x], tables.at[x], tab_s.at[0], tab_r.at[x], at(z, xx, p, y))

    def table_in(i):
        xx = (x + i) % NX
        return remote(tables.at[xx], tables.at[xx], tab_s.at[0], tab_r.at[xx], at(z, xx, p, y))

    for i in (1, 3, 2):
        table_out(i).start()

    for event in PROLOGUE:
        run(event)
    for d in range(2):
        gain_swap(d, 1 - p + d * (1 + 2 * p)).wait_recv()
    for i in (1, 3, 2):
        table_in(i).wait_recv()

    def part_out(c, st, xx):
        return remote(
            psend.at[st, xx],
            precv.at[c, st, x],
            p_s.at[st],
            p_r.at[st, x],
            at(z, xx, p, y),
        )

    def part_in(c, st, i):
        xx = (x + i) % NX
        return remote(
            psend.at[st, xx],
            precv.at[c, st, xx],
            p_s.at[st],
            p_r.at[st, xx],
            at(z, xx, p, y),
        )

    def square_out(c, st, i):
        xx = (x + i) % NX
        return remote(
            qsend.at[st, xx // 2],
            qrecv.at[c, st, x],
            q_s.at[st],
            q_r.at[st, x],
            at(z, xx, p, y),
        )

    def square_in(c, st, i):
        xx = (x + i) % NX
        return remote(
            qsend.at[st, xx // 2],
            qrecv.at[c, st, xx],
            q_s.at[st],
            q_r.at[st, xx],
            at(z, xx, p, y),
        )

    def sent(ref, sem):
        pltpu.make_async_copy(ref, ref, sem).wait()

    def attn_ref(c, st, xx):
        return abuf.at[c, st, xx % 2, xx // 2]

    def attn_out(c, st, i):
        xx = (x + i) % NX
        ref = attn_ref(c, st, x)
        return remote(ref, ref, a_s.at[st], a_r.at[st, x], at(z, xx, p, y))

    def attn_in(c, st, i):
        xx = (x + i) % NX
        ref = attn_ref(c, st, xx)
        return remote(ref, ref, a_s.at[st], a_r.at[st, xx], at(z, xx, p, y))

    def proj_out(c, st, yy):
        return remote(
            osend.at[st, yy], orecv.at[c, st, y], o_s.at[st], o_r.at[st, y], at(z, x, p, yy)
        )

    def proj_in(c, st, yy):
        return remote(
            osend.at[st, yy], orecv.at[c, st, yy], o_s.at[st], o_r.at[st, yy], at(z, x, p, yy)
        )

    def project_stage(c, st):
        for i in (1, 3, 2):
            attn_in(c, st, i).wait_recv()
        sent(psend.at[st, pl.ds(0, 3)], p_s.at[st])

        def proj(yy):
            cols = pl.ds(pl.multiple_of(yy * PIECE, PIECE), PIECE)
            total = jnp.zeros((STREAM, PIECE), jnp.float32)
            for g in range(2):
                total = total + jnp.dot(
                    abuf[c, st, g].reshape(STREAM, HALF),
                    wob[c, g * HALF : g * HALF + HALF, cols],
                    preferred_element_type=jnp.float32,
                )
            return total

        def proj_tile(i, carry):
            yy = (y + i) % NY
            osend[st, yy] = proj(yy).astype(jnp.bfloat16)
            proj_out(c, st, yy).start()
            return carry

        lax.fori_loop(1, NY, proj_tile, 0)
        oown[st] = proj(y)

    def add_stage(c, st):
        for i in (1, 3, 2):
            proj_in(c, st, (y + i) % NY).wait_recv()
        sent(osend.at[st, pl.ds(0, 3)], o_s.at[st])
        sent(psend.at[st, pl.ds(0, 2)], a_s.at[st])
        sent(qrecv.at[c, st, pl.ds(0, 3)], q_s.at[st])
        for b in range(2):
            rows = slice(b * SEQ, b * SEQ + SEQ)
            places = slice(st * STREAM + b * SEQ, st * STREAM + b * SEQ + SEQ)
            total = oown[st, rows, :]
            for i in (1, 2, 3):
                total = total + orecv[c, st, (y + i) % NY, rows, :].astype(jnp.float32)
            total = total + xbuf[c, y, places, :].astype(jnp.float32)
            xbuf[c + 1, y, places, :] = total.astype(jnp.bfloat16)

        @pl.when(c < LAYERS - 1)
        def _():
            for i in (1, 3, 2):
                stream_out(c + 1, st, i).start()

    def qkv_stage(c, st):
        for i in (1, 3, 2):
            stream_in(c, st, i).wait_recv()
        for b in range(2):
            rows = slice(b * SEQ, b * SEQ + SEQ)
            places = slice(st * STREAM + b * SEQ, st * STREAM + b * SEQ + SEQ)
            total = jnp.zeros((SEQ, 1), jnp.float32)
            for yy in range(NY):
                wide = xbuf[c, yy, places, :].astype(jnp.float32)
                total = total + jnp.sum(wide * wide, axis=1, keepdims=True)
                gains = gbuf[c, 0:1, yy * PIECE : yy * PIECE + PIECE]
                xg[yy, rows, :] = (wide * gains).astype(jnp.bfloat16)
            flat = jnp.sum(jnp.where(row == lane, total, 0.0), axis=0, keepdims=True)
            qsend[st, b] = jnp.broadcast_to(flat, (8, 128))
        for i in (1, 3, 2):
            square_out(c, st, i).start()
        if st == 0:
            ready(c, 0)
        for turn in range(2):
            g = (x + 1 + turn) % 2

            def qkv_tile(n, carry):
                cols = pl.ds(pl.multiple_of(g * GROUP + n * 256, 256), 256)
                acc = jnp.zeros((STREAM, 256), jnp.float32)
                for yy in range(NY):
                    acc = acc + jnp.dot(
                        xg[yy],
                        wqkv[c, yy * PIECE : yy * PIECE + PIECE, cols],
                        preferred_element_type=jnp.float32,
                    )
                acc = acc.astype(jnp.bfloat16)
                for b in range(2):
                    psend[st, b * 2 + g, :, pl.ds(pl.multiple_of(n * 256, 256), 256)] = acc[
                        b * SEQ : b * SEQ + SEQ
                    ]
                return carry

            lax.fori_loop(0, GROUP // 256, qkv_tile, 0)
            for b in range(2):

                @pl.when(b * 2 + g != x)
                def _():
                    part_out(c, st, b * 2 + g).start()

    def attention_stage(c, st):
        for i in (1, 3, 2):
            square_in(c, st, i).wait_recv()
        flat = qsend[st, x // 2]
        for i in (1, 2, 3):
            flat = flat + qrecv[c, st, (x + i) % NX]
        square = jnp.sum(jnp.where(row == lane, flat[0:1, :], 0.0), axis=1, keepdims=True)
        inv_rms = lax.rsqrt(square * (1.0 / WIDTH) + NORM_EPSILON)
        for i in (1, 3, 2):
            part_in(c, st, i).wait_recv()
        sent(osend.at[st, pl.ds(0, 3)], x_s.at[st])
        mine = st * 2 + x // 2

        def summed(b):
            cols = slice(b * 128, b * 128 + 128)
            total = psend[st, x, :, cols].astype(jnp.float32)
            for i in (1, 2, 3):
                total = total + precv[c, st, (x + i) % NX, :, cols].astype(jnp.float32)
            return total

        def turned(b):
            value = summed(b) * inv_rms
            return (value * tables[mine, 0] + pltpu.roll(value, 64, 1) * tables[mine, 1]).astype(
                jnp.bfloat16
            )

        keys = turned(4)
        vals = (summed(5) * inv_rms).astype(jnp.bfloat16)
        query = jnp.concatenate([turned(j) for j in range(4)], axis=0)
        scores = lax.dot_general(
            query, keys, (((1,), (1,)), ((), ())), preferred_element_type=jnp.float32
        )
        bias = jnp.concatenate([tables[mine, 2, :, 0:SEQ]] * 4, axis=0)
        scores = scores * HEAD_DIM ** (-0.5) + bias
        top = jnp.max(scores, axis=1, keepdims=True)
        expo = jnp.exp(scores - top)
        weights = (expo / jnp.sum(expo, axis=1, keepdims=True)).astype(jnp.bfloat16)
        mixed = jnp.dot(weights, vals, preferred_element_type=jnp.float32).astype(jnp.bfloat16)
        for j in range(4):
            abuf[c, st, x % 2, x // 2, :, j * 128 : j * 128 + 128] = mixed[j * SEQ : j * SEQ + SEQ]
        for i in (1, 3, 2):
            attn_out(c, st, i).start()

    def done_rows(xx, q):
        return pl.ds(pl.multiple_of(xx * SEQ + q * 32, 32), 32)

    def hand_over(st):
        for xx in (2 * st, 2 * st + 1):
            for q in range(2):
                here = (xx == x) & (q == p)

                for half in range(2):
                    rows = xbuf.at[LAYERS, y, done_rows(xx, q), pl.ds(half * 128, 128)]
                    first = pl.multiple_of(half * 512 + x * 128, 128)
                    place = out.at[p, :, pl.ds(first, 128)]

                    @pl.when(jnp.logical_not(here))
                    def _():
                        remote(rows, place, f_s.at[0], f_r.at[p, x], at(z, xx, q, y)).start()

                    @pl.when(here)
                    def _():
                        pltpu.make_async_copy(rows, place, isem.at[0]).start()

    stages = (qkv_stage, attention_stage, project_stage, add_stage)

    def layer(c, carry):
        for slot in range(8):
            for at_layer in range(LAYERS):
                if EVENTS[at_layer][slot]:

                    @pl.when(c == at_layer)
                    def _():
                        for event in EVENTS[at_layer][slot]:
                            run(event)

            if slot == 4:
                ready(c, 1)
            stages[slot // 2](c, slot % 2)
            if slot >= 6:

                @pl.when(c == LAYERS - 1)
                def _():
                    hand_over(slot - 6)

        return carry

    lax.fori_loop(0, LAYERS, layer, 0)

    away = [(i, j) for i in (2, 1, 3, 0) for j in range(2) if (i, j) != (0, 0)]
    landed = xbuf.at[LAYERS, y, done_rows(0, 0), :]
    for i, j in away:
        sent(landed, f_r.at[(p + j) % 2, (x + i) % NX])
    sent(landed, isem.at[0])

    sent(xbuf.at[LAYERS, 0, pl.ds(0, 224), :], f_s.at[0])
    sent(tsend.at[pl.ds(0, 3)], t_s.at[0])
    sent(tables.at[pl.ds(0, 3)], tab_s.at[0])
    sent(gbuf.at[pl.ds(0, 2)], g_s.at[0])
    for t in range(2):
        ref = wqkv.at[0, pl.ds(0, 256), :] if t == 0 else wob.at[0, pl.ds(0, 256), :]
        remote(ref, ref, own_s.at[t], own_r[t].at[0, 0], other).wait_send()
        ref = stretch(slice(0, LAYERS), t)
        remote(ref, ref, hop_s.at[t], hop_r[t].at[0, 0, 0], down).wait_send()
        remote(ref, ref, par_s.at[t], par_r.at[0, t], other).wait_send()


def per_device(
    tokens,
    w_query,
    w_key,
    w_value,
    w_out,
    norm_gain,
    boundary,
    skip_offset,
    doc_lengths,
    batch_order,
):
    smem = pl.BlockSpec(memory_space=pltpu.SMEM)
    anywhere = pl.BlockSpec(memory_space=pl.ANY)
    dma = pltpu.SemaphoreType.DMA
    bf16, f32 = jnp.bfloat16, jnp.float32
    return pl.pallas_call(
        stack_kernel,
        out_shape=jax.ShapeDtypeStruct((2, 32, 1024), bf16),
        in_specs=[smem] * 4 + [anywhere] * 7,
        out_specs=anywhere,
        scratch_shapes=[
            pltpu.VMEM((LAYERS, SET, QKV), bf16),
            pltpu.VMEM((LAYERS, HEADS, SET), bf16),
            pltpu.VMEM((LAYERS, 8, SET), f32),
            pltpu.VMEM((NX, SEQ, PIECE), bf16),
            pltpu.VMEM((LAYERS + 1, NY, TOK, PIECE), bf16),
            pltpu.VMEM((NY, STREAM, PIECE), bf16),
            pltpu.VMEM((2, NX, SEQ, GROUP), bf16),
            pltpu.VMEM((LAYERS, 2, NX, SEQ, GROUP), bf16),
            pltpu.VMEM((2, 2, 8, 128), f32),
            pltpu.VMEM((LAYERS, 2, NX, 8, 128), f32),
            pltpu.VMEM((LAYERS, 2, 2, 2, SEQ, HALF), bf16),
            pltpu.VMEM((2, NY, STREAM, PIECE), bf16),
            pltpu.VMEM((2, STREAM, PIECE), f32),
            pltpu.VMEM((LAYERS, 2, NY, STREAM, PIECE), bf16),
            pltpu.VMEM((2, SEQ, 1024), bf16),
            pltpu.VMEM((8, HEAD_DIM), f32),
            pltpu.VMEM((2, 1, WIDTH), f32),
            pltpu.VMEM((NX, 3, SEQ, HEAD_DIM), f32),
            dma((3,)),
            dma((2, 2)),
            dma((2,)),
            dma((LAYERS, PIECES[0], 4)),
            dma((LAYERS, PIECES[1], 4)),
            dma((2,)),
            dma((2, PIECES[0])),
            dma((2, PIECES[1])),
            dma((2,)),
            dma((LAYERS, 2)),
        ]
        + [dma((1,)), dma((2,))]
        + [dma((1,)), dma((NX,))] * 2
        + [dma((2,)), dma((2, NX))] * 5
        + [dma((1,)), dma((2, NX))],
        compiler_params=pltpu.CompilerParams(
            collective_id=0, has_side_effects=True, vmem_limit_bytes=60 * 1024 * 1024
        ),
    )(
        batch_order,
        boundary,
        skip_offset,
        doc_lengths,
        tokens,
        jnp.asarray(frequencies()),
        norm_gain,
        w_query,
        w_key,
        w_value,
        w_out,
    )


def solution(mesh):
    placed = (
        P("dp", None, "tensor"),
        P(None, "pipe", "dp", "tensor"),
        P(None, "pipe", "dp", "tensor"),
        P(None, "pipe", "dp", "tensor"),
        P(None, "pipe", "tensor", "dp"),
        P(None, "pipe", None),
        P("dp"),
        P("dp"),
        P("dp", None),
        P("dp", None),
    )
    return jax.shard_map(
        per_device, mesh=mesh, in_specs=placed, out_specs=P("dp", "pipe", "tensor"), check_vma=False
    )
```

```python
import math

import jax
import jax.numpy as jnp
import numpy as np
from jax import lax
from jax.experimental import pallas as pl
from jax.experimental.pallas import tpu as pltpu
from jax.sharding import PartitionSpec as P

HEAD_DIM = 128
ROPE_THETA = 500000.0
NORM_EPSILON = 1e-05
MESH = pl.DeviceIdType.MESH

LAYERS = 4
NZ, NX, NY = 8, 4, 4
SEQ = 64
WIDTH = 4096
CHUNK = 128
SET = NZ * CHUNK
QKV = 1536
HEADS = 1024
GROUP = QKV // 2
STREAM = 2 * SEQ
HALF = HEADS // 2
TOK = NX * SEQ
PIECE = SET // NY
PIECES = (4, 2)


TWO_PI_HIGH = 6.28125
TWO_PI_MID = 0.0019340515136718750
TWO_PI_LOW = 2 * math.pi - TWO_PI_HIGH - TWO_PI_MID
SINE_TERMS = [(-1.0) ** k / math.factorial(2 * k + 1) for k in range(10)]
COSINE_TERMS = [(-1.0) ** k / math.factorial(2 * k) for k in range(11)]


def frequencies():
    half = HEAD_DIM // 2
    table = np.float64(ROPE_THETA) ** (-np.arange(half, dtype=np.float64) / half)
    return np.tile(table.astype(np.float32), 2)[None, :].repeat(8, axis=0)


def series(terms, square):
    total = jnp.full(square.shape, terms[-1], jnp.float32)
    for term in terms[-2::-1]:
        total = total * square + term
    return total


def sine_and_cosine(angle):
    turns = jnp.floor(angle * (0.5 / math.pi) + 0.5)
    rest = ((angle - turns * TWO_PI_HIGH) - turns * TWO_PI_MID) - turns * TWO_PI_LOW
    square = rest * rest
    return rest * series(SINE_TERMS, square), series(COSINE_TERMS, square)


PROLOGUE = ((0, 0, 2), (0, 1, 0), (0, 0, 3), (0, 1, 1), (1, 0, 0), (0, 0, 4))
EVENTS = (
    (
        (),
        ((0, 1, 2),),
        ((1, 0, 1),),
        ((0, 1, 3), (1, 1, 0)),
        ((1, 0, 2), (0, 1, 4)),
        ((1, 1, 1),),
        ((1, 0, 3), (2, 1, 0)),
        (),
    ),
    (
        ((1, 0, 4), (1, 1, 2), (2, 0, 0)),
        (),
        ((1, 1, 3), (2, 0, 1)),
        (),
        ((1, 1, 4), (2, 0, 2), (2, 1, 1)),
        (),
        ((2, 0, 3),),
        ((2, 1, 2),),
    ),
    (
        ((3, 0, 0), (2, 0, 4)),
        ((2, 1, 3),),
        ((2, 1, 4), (3, 0, 1), (3, 1, 0)),
        (),
        ((3, 0, 2),),
        ((3, 1, 1),),
        ((3, 0, 3),),
        ((3, 1, 2),),
    ),
    (
        ((3, 0, 4),),
        (),
        ((3, 1, 3),),
        (),
        ((3, 1, 4),),
        (),
        (),
        (),
    ),
)


def stack_kernel(
    order,
    boundary,
    offset,
    lengths,
    tokens,
    freq,
    gain_in,
    wq,
    wk,
    wv,
    wo,
    out,
    wqkv,
    wob,
    gbuf,
    tsend,
    xbuf,
    xg,
    psend,
    precv,
    qsend,
    qrecv,
    abuf,
    osend,
    oown,
    orecv,
    tok_v,
    freq_v,
    gain,
    tables,
    isem,
    lsem,
    hop_s,
    hop_rq,
    hop_ro,
    own_s,
    own_rq,
    own_ro,
    par_s,
    par_r,
    g_s,
    g_r,
    t_s,
    t_r,
    tab_s,
    tab_r,
    x_s,
    x_r,
    p_s,
    p_r,
    q_s,
    q_r,
    a_s,
    a_r,
    o_s,
    o_r,
    f_s,
    f_r,
):
    dp = lax.axis_index("dp")
    p = lax.axis_index("pipe")
    y = lax.axis_index("tensor")
    z = dp // NX
    x = dp % NX
    step = 1 - 2 * p

    def at(zz, xx, pp, yy):
        return {"dp": zz * NX + xx, "pipe": pp, "tensor": yy}

    def zrel(k):
        return (z + step * k + NZ) % NZ

    down = at(zrel(1), x, p, y)
    up = at(zrel(-1), x, p, y)
    other = at(z, x, 1 - p, y)

    def remote(src, dst, s, r, dev):
        return pltpu.make_async_remote_copy(
            src_ref=src, dst_ref=dst, send_sem=s, recv_sem=r, device_id=dev, device_id_type=MESH
        )

    def layer_of(d):
        return p + d * (3 - 2 * p)

    def rows_of(zz):
        return pl.ds(pl.multiple_of(zz * CHUNK, CHUNK), CHUNK)

    def loads(d):
        c = layer_of(d)
        r = rows_of(z)
        copies = []
        for g in range(2):
            for source, width, first in ((wq, 512, 0), (wk, 128, 512), (wv, 128, 640)):
                copies.append(
                    pltpu.make_async_copy(
                        source.at[d, 0, :, pl.ds(g * width, width)],
                        wqkv.at[c, r, pl.ds(g * GROUP + first, width)],
                        lsem.at[d, 0],
                    )
                )
        copies.append(pltpu.make_async_copy(wo.at[d, 0], wob.at[c, :, r], lsem.at[d, 1]))
        return copies

    barrier = pltpu.get_barrier_semaphore()
    peers = [down, up, other]
    for i in (1, 2, 3):
        peers.append(at(z, (x + i) % NX, p, y))
        peers.append(at(z, (x + i) % NX, 1 - p, y))
        peers.append(at(z, x, p, (y + i) % NY))
    for dev in peers:
        pl.semaphore_signal(barrier, inc=1, device_id=dev, device_id_type=MESH)

    small = [
        pltpu.make_async_copy(tokens, tok_v, isem.at[0]),
        pltpu.make_async_copy(freq, freq_v, isem.at[1]),
        pltpu.make_async_copy(gain_in, gain, isem.at[2]),
    ]
    for copy in loads(0) + small + loads(1):
        copy.start()
    pl.semaphore_wait(barrier, len(peers))

    def piece(c, zz, t, k):
        rows = (CHUNK if t == 0 else HEADS) // PIECES[t]
        if t == 0:
            return wqkv.at[c, pl.ds(pl.multiple_of(zz * CHUNK + k * rows, rows), rows), :]
        return wob.at[c, pl.ds(pl.multiple_of(k * rows, rows), rows), rows_of(zz)]

    hop_r = (hop_rq, hop_ro)

    own_r = (own_rq, own_ro)

    def whole(c, zz, t):
        if t == 0:
            return wqkv.at[c, rows_of(zz), :]
        return wob.at[c, :, rows_of(zz)]

    def stretch(layers, t):
        return (wqkv, wob)[t].at[layers, pl.ds(0, 448), :]

    def hop_out(c, t, k, h):
        ref = piece(c, zrel(1 - h), t, k)
        return remote(ref, ref, hop_s.at[t], hop_r[t].at[c, k, h - 1], down)

    def hop_in(c, t, k, h):
        ref = piece(c, zrel(-h), t, k)
        return remote(ref, ref, hop_s.at[t], hop_r[t].at[c, k, h - 1], up)

    def swap_out(c, t, k, h):
        ref = piece(c, zrel(-h), t, k)
        return remote(ref, ref, par_s.at[t], par_r.at[c, t], other)

    def own_swap(c, t, k):
        ref = piece(c, z, t, k)
        return remote(ref, ref, own_s.at[t], own_r[t].at[c // 2, k], other)

    def holder(c):
        return jnp.where((c == 0) | (c == 3), 0, 1)

    def nth(t, j, core):
        return (j + core * (PIECES[t] // 2)) % PIECES[t]

    def first_hop(c, t):
        for j in range(PIECES[t]):
            k = nth(t, j, p)

            @pl.when(p != holder(c))
            def _():
                own_swap(c, t, k).wait_recv()

            hop_out(c, t, k, 1).start()

    def forward(c, t, h):
        for j in range(PIECES[t]):
            k = nth(t, j, p)
            hop_in(c, t, k, h).wait_recv()
            if h < 3 or j < PIECES[t] // 2:
                hop_out(c, t, k, h + 1).start()
            swap_out(c, t, k, h).start()

    def finish(c, t):
        for j in range(PIECES[t] // 2):
            k = nth(t, j, p)
            hop_in(c, t, k, 4).wait_recv()
            swap_out(c, t, k, 4).start()

    def ready(c, t):
        ref = stretch(c, t)
        remote(ref, ref, par_s.at[t], par_r.at[c, t], other).wait_recv()

    def loaded(d, t):
        landed = whole(layer_of(d), z, t)
        pltpu.make_async_copy(landed, landed, lsem.at[d, t]).wait()

    def share(d, t):
        for j in range(PIECES[t]):
            own_swap(layer_of(d), t, nth(t, j, 1 - p)).start()

    loaded(0, 0)
    share(0, 0)
    first_hop(0, 0)
    loaded(0, 1)
    share(0, 1)

    def run(event):
        c, t, h = event
        if h == 0:
            first_hop(c, t)
        elif h < 4:
            forward(c, t, h)
        else:
            finish(c, t)

    for copy in small:
        copy.wait()
    second = order[0, p] == 1

    def chosen(first, other_one):
        return jnp.where(second, other_one, first)

    for xx in range(NX):
        for k in range(2):
            cols = slice(k * 512 + xx * 128, k * 512 + xx * 128 + 128)
            tsend[xx, :, k * 128 : k * 128 + 128] = chosen(
                tok_v[0, :, cols].astype(jnp.float32), tok_v[1, :, cols].astype(jnp.float32)
            ).astype(jnp.bfloat16)

    def block(ref, b, size):
        return ref.at[pl.ds(pl.multiple_of(b * size, size), size), :]

    def tok_out(i):
        xx = (x + i) % NX
        return remote(
            tsend.at[xx], block(xbuf.at[0, y], x, SEQ), t_s.at[0], t_r.at[x], at(z, xx, p, y)
        )

    def tok_in(i):
        xx = (x + i) % NX
        return remote(
            tsend.at[xx], block(xbuf.at[0, y], xx, SEQ), t_s.at[0], t_r.at[xx], at(z, xx, p, y)
        )

    for i in (1, 3, 2):
        tok_out(i).start()
    xbuf[0, y, pl.ds(pl.multiple_of(x * SEQ, SEQ), SEQ), :] = tsend[x]

    forward(0, 0, 1)
    for t in range(2):
        loaded(1, t)
        share(1, t)

    for d in range(2):
        c = layer_of(d)
        for zz in range(NZ):
            row = gain[d, :, pl.ds(pl.multiple_of((zz * NX + x) * CHUNK, CHUNK), CHUNK)]
            gbuf[c, :, zz * CHUNK : zz * CHUNK + CHUNK] = jnp.broadcast_to(row, (8, CHUNK))

    def gain_swap(d, c):
        return remote(gbuf.at[c], gbuf.at[c], g_s.at[0], g_r.at[d], other)

    for d in range(2):
        gain_swap(d, layer_of(d)).start()

    def stream_rows(st):
        return pl.ds(st * STREAM, STREAM)

    def stream_out(c, st, i):
        yy = (y + i) % NY
        ref = xbuf.at[c, y, stream_rows(st), :]
        return remote(ref, ref, x_s.at[st], x_r.at[st, y], at(z, x, p, yy))

    def stream_in(c, st, i):
        yy = (y + i) % NY
        ref = xbuf.at[c, yy, stream_rows(st), :]
        return remote(ref, ref, x_s.at[st], x_r.at[st, yy], at(z, x, p, yy))

    for i in (1, 3, 2):
        tok_in(i).wait_recv()
    for st in range(2):
        for i in (1, 3, 2):
            stream_out(0, st, i).start()

    row = lax.broadcasted_iota(jnp.int32, (SEQ, 128), 0)
    lane = lax.broadcasted_iota(jnp.int32, (SEQ, 128), 1)
    cut = chosen(boundary[0], boundary[1])
    jump = chosen(offset[0], offset[1])
    places = jnp.where(row < cut, row, row + jump)
    sine, cosine = sine_and_cosine(places.astype(jnp.float32) * freq_v[0:1, :])
    tables[x, 0] = cosine
    tables[x, 1] = jnp.where(lane < 64, -sine, sine)
    end = 0
    doc_from = jnp.zeros((SEQ, 128), jnp.int32)
    doc_to = jnp.zeros((SEQ, 128), jnp.int32)
    for k in range(4):
        end = end + chosen(lengths[0, k], lengths[1, k])
        doc_from = doc_from + jnp.where(row >= end, 1, 0)
        doc_to = doc_to + jnp.where(lane >= end, 1, 0)
    allowed = (doc_from == doc_to) & (lane <= row)
    tables[x, 2] = jnp.where(allowed, 0.0, -jnp.inf).astype(jnp.float32)

    def table_out(i):
        xx = (x + i) % NX
        return remote(tables.at[x], tables.at[x], tab_s.at[0], tab_r.at[x], at(z, xx, p, y))

    def table_in(i):
        xx = (x + i) % NX
        return remote(tables.at[xx], tables.at[xx], tab_s.at[0], tab_r.at[xx], at(z, xx, p, y))

    for i in (1, 3, 2):
        table_out(i).start()

    for event in PROLOGUE:
        run(event)
    for d in range(2):
        gain_swap(d, 1 - p + d * (1 + 2 * p)).wait_recv()
    for i in (1, 3, 2):
        table_in(i).wait_recv()

    def part_out(c, st, xx):
        return remote(
            psend.at[st, xx],
            precv.at[c, st, x],
            p_s.at[st],
            p_r.at[st, x],
            at(z, xx, p, y),
        )

    def part_in(c, st, i):
        xx = (x + i) % NX
        return remote(
            psend.at[st, xx],
            precv.at[c, st, xx],
            p_s.at[st],
            p_r.at[st, xx],
            at(z, xx, p, y),
        )

    def square_out(c, st, i):
        xx = (x + i) % NX
        return remote(
            qsend.at[st, xx // 2],
            qrecv.at[c, st, x],
            q_s.at[st],
            q_r.at[st, x],
            at(z, xx, p, y),
        )

    def square_in(c, st, i):
        xx = (x + i) % NX
        return remote(
            qsend.at[st, xx // 2],
            qrecv.at[c, st, xx],
            q_s.at[st],
            q_r.at[st, xx],
            at(z, xx, p, y),
        )

    def sent(ref, sem):
        pltpu.make_async_copy(ref, ref, sem).wait()

    def attn_ref(c, st, xx):
        return abuf.at[c, st, xx % 2, xx // 2]

    def attn_out(c, st, i):
        xx = (x + i) % NX
        ref = attn_ref(c, st, x)
        return remote(ref, ref, a_s.at[st], a_r.at[st, x], at(z, xx, p, y))

    def attn_in(c, st, i):
        xx = (x + i) % NX
        ref = attn_ref(c, st, xx)
        return remote(ref, ref, a_s.at[st], a_r.at[st, xx], at(z, xx, p, y))

    def proj_out(c, st, yy):
        return remote(
            osend.at[st, yy], orecv.at[c, st, y], o_s.at[st], o_r.at[st, y], at(z, x, p, yy)
        )

    def proj_in(c, st, yy):
        return remote(
            osend.at[st, yy], orecv.at[c, st, yy], o_s.at[st], o_r.at[st, yy], at(z, x, p, yy)
        )

    def project_stage(c, st):
        for i in (1, 3, 2):
            attn_in(c, st, i).wait_recv()
        sent(psend.at[st, pl.ds(0, 3)], p_s.at[st])

        def proj(yy):
            cols = pl.ds(pl.multiple_of(yy * PIECE, PIECE), PIECE)
            total = jnp.zeros((STREAM, PIECE), jnp.float32)
            for g in range(2):
                total = total + jnp.dot(
                    abuf[c, st, g].reshape(STREAM, HALF),
                    wob[c, g * HALF : g * HALF + HALF, cols],
                    preferred_element_type=jnp.float32,
                )
            return total

        def proj_tile(i, carry):
            yy = (y + 1 + (2 * i) % 3) % NY
            osend[st, yy] = proj(yy).astype(jnp.bfloat16)
            proj_out(c, st, yy).start()
            return carry

        lax.fori_loop(0, NY - 1, proj_tile, 0)
        oown[st] = proj(y)

    def add_stage(c, st):
        for i in (1, 3, 2):
            proj_in(c, st, (y + i) % NY).wait_recv()
        sent(osend.at[st, pl.ds(0, 3)], o_s.at[st])
        sent(psend.at[st, pl.ds(0, 2)], a_s.at[st])
        sent(qrecv.at[c, st, pl.ds(0, 3)], q_s.at[st])
        for b in range(2):
            rows = slice(b * SEQ, b * SEQ + SEQ)
            places = slice(st * STREAM + b * SEQ, st * STREAM + b * SEQ + SEQ)
            total = oown[st, rows, :]
            for i in (1, 2, 3):
                total = total + orecv[c, st, (y + i) % NY, rows, :].astype(jnp.float32)
            total = total + xbuf[c, y, places, :].astype(jnp.float32)
            xbuf[c + 1, y, places, :] = total.astype(jnp.bfloat16)

        @pl.when(c < LAYERS - 1)
        def _():
            for i in (1, 3, 2):
                stream_out(c + 1, st, i).start()

    def qkv_stage(c, st):
        for i in (1, 3, 2):
            stream_in(c, st, i).wait_recv()
        for b in range(2):
            rows = slice(b * SEQ, b * SEQ + SEQ)
            places = slice(st * STREAM + b * SEQ, st * STREAM + b * SEQ + SEQ)
            total = jnp.zeros((SEQ, 1), jnp.float32)
            for yy in range(NY):
                wide = xbuf[c, yy, places, :].astype(jnp.float32)
                total = total + jnp.sum(wide * wide, axis=1, keepdims=True)
                gains = gbuf[c, 0:1, yy * PIECE : yy * PIECE + PIECE]
                xg[yy, rows, :] = (wide * gains).astype(jnp.bfloat16)
            flat = jnp.sum(jnp.where(row == lane, total, 0.0), axis=0, keepdims=True)
            qsend[st, b] = jnp.broadcast_to(flat, (8, 128))
        for i in (1, 3, 2):
            square_out(c, st, i).start()
        if st == 0:
            ready(c, 0)
        for turn in range(2):
            g = (x + 1 + turn) % 2

            def qkv_tile(n, carry):
                cols = pl.ds(pl.multiple_of(g * GROUP + n * 256, 256), 256)
                acc = jnp.zeros((STREAM, 256), jnp.float32)
                for yy in range(NY):
                    acc = acc + jnp.dot(
                        xg[yy],
                        wqkv[c, yy * PIECE : yy * PIECE + PIECE, cols],
                        preferred_element_type=jnp.float32,
                    )
                acc = acc.astype(jnp.bfloat16)
                for b in range(2):
                    psend[st, b * 2 + g, :, pl.ds(pl.multiple_of(n * 256, 256), 256)] = acc[
                        b * SEQ : b * SEQ + SEQ
                    ]
                return carry

            lax.fori_loop(0, GROUP // 256, qkv_tile, 0)
            for b in range(2):

                @pl.when(b * 2 + g != x)
                def _():
                    part_out(c, st, b * 2 + g).start()

    def attention_stage(c, st):
        for i in (1, 3, 2):
            square_in(c, st, i).wait_recv()
        flat = qsend[st, x // 2]
        for i in (1, 2, 3):
            flat = flat + qrecv[c, st, (x + i) % NX]
        square = jnp.sum(jnp.where(row == lane, flat[0:1, :], 0.0), axis=1, keepdims=True)
        inv_rms = lax.rsqrt(square * (1.0 / WIDTH) + NORM_EPSILON)
        for i in (1, 3, 2):
            part_in(c, st, i).wait_recv()
        sent(osend.at[st, pl.ds(0, 3)], x_s.at[st])
        mine = st * 2 + x // 2

        def summed(b):
            cols = slice(b * 128, b * 128 + 128)
            total = psend[st, x, :, cols].astype(jnp.float32)
            for i in (1, 2, 3):
                total = total + precv[c, st, (x + i) % NX, :, cols].astype(jnp.float32)
            return total

        def turned(b):
            value = summed(b) * inv_rms
            return (value * tables[mine, 0] + pltpu.roll(value, 64, 1) * tables[mine, 1]).astype(
                jnp.bfloat16
            )

        keys = turned(4)
        vals = (summed(5) * inv_rms).astype(jnp.bfloat16)
        query = jnp.concatenate([turned(j) for j in range(4)], axis=0)
        scores = lax.dot_general(
            query, keys, (((1,), (1,)), ((), ())), preferred_element_type=jnp.float32
        )
        bias = jnp.concatenate([tables[mine, 2, :, 0:SEQ]] * 4, axis=0)
        scores = scores * HEAD_DIM ** (-0.5) + bias
        top = jnp.max(scores, axis=1, keepdims=True)
        expo = jnp.exp(scores - top)
        weights = (expo / jnp.sum(expo, axis=1, keepdims=True)).astype(jnp.bfloat16)
        mixed = jnp.dot(weights, vals, preferred_element_type=jnp.float32).astype(jnp.bfloat16)
        for j in range(4):
            abuf[c, st, x % 2, x // 2, :, j * 128 : j * 128 + 128] = mixed[j * SEQ : j * SEQ + SEQ]
        for i in (1, 3, 2):
            attn_out(c, st, i).start()

    def done_rows(xx, q):
        return pl.ds(pl.multiple_of(xx * SEQ + q * 32, 32), 32)

    def hand_over(st):
        for xx in (2 * st, 2 * st + 1):
            for q in range(2):
                here = (xx == x) & (q == p)

                for half in range(2):
                    rows = xbuf.at[LAYERS, y, done_rows(xx, q), pl.ds(half * 128, 128)]
                    first = pl.multiple_of(half * 512 + x * 128, 128)
                    place = out.at[p, :, pl.ds(first, 128)]

                    @pl.when(jnp.logical_not(here))
                    def _():
                        remote(rows, place, f_s.at[0], f_r.at[p, x], at(z, xx, q, y)).start()

                    @pl.when(here)
                    def _():
                        pltpu.make_async_copy(rows, place, isem.at[0]).start()

    stages = (qkv_stage, attention_stage, project_stage, add_stage)

    def layer(c, carry):
        for slot in range(8):
            for at_layer in range(LAYERS):
                if EVENTS[at_layer][slot]:

                    @pl.when(c == at_layer)
                    def _():
                        for event in EVENTS[at_layer][slot]:
                            run(event)

            if slot == 4:
                ready(c, 1)
            stages[slot // 2](c, slot % 2)
            if slot >= 6:

                @pl.when(c == LAYERS - 1)
                def _():
                    hand_over(slot - 6)

        return carry

    lax.fori_loop(0, LAYERS, layer, 0)

    away = [(i, j) for i in (2, 1, 3, 0) for j in range(2) if (i, j) != (0, 0)]
    landed = xbuf.at[LAYERS, y, done_rows(0, 0), :]
    for i, j in away:
        sent(landed, f_r.at[(p + j) % 2, (x + i) % NX])
    sent(landed, isem.at[0])

    sent(xbuf.at[LAYERS, 0, pl.ds(0, 224), :], f_s.at[0])
    sent(tsend.at[pl.ds(0, 3)], t_s.at[0])
    sent(tables.at[pl.ds(0, 3)], tab_s.at[0])
    sent(gbuf.at[pl.ds(0, 2)], g_s.at[0])
    for t in range(2):
        ref = wqkv.at[0, pl.ds(0, 256), :] if t == 0 else wob.at[0, pl.ds(0, 256), :]
        remote(ref, ref, own_s.at[t], own_r[t].at[0, 0], other).wait_send()
        ref = stretch(slice(0, LAYERS), t)
        remote(ref, ref, hop_s.at[t], hop_r[t].at[0, 0, 0], down).wait_send()
        remote(ref, ref, par_s.at[t], par_r.at[0, t], other).wait_send()


def per_device(
    tokens,
    w_query,
    w_key,
    w_value,
    w_out,
    norm_gain,
    boundary,
    skip_offset,
    doc_lengths,
    batch_order,
):
    smem = pl.BlockSpec(memory_space=pltpu.SMEM)
    anywhere = pl.BlockSpec(memory_space=pl.ANY)
    dma = pltpu.SemaphoreType.DMA
    bf16, f32 = jnp.bfloat16, jnp.float32
    return pl.pallas_call(
        stack_kernel,
        out_shape=jax.ShapeDtypeStruct((2, 32, 1024), bf16),
        in_specs=[smem] * 4 + [anywhere] * 7,
        out_specs=anywhere,
        scratch_shapes=[
            pltpu.VMEM((LAYERS, SET, QKV), bf16),
            pltpu.VMEM((LAYERS, HEADS, SET), bf16),
            pltpu.VMEM((LAYERS, 8, SET), f32),
            pltpu.VMEM((NX, SEQ, PIECE), bf16),
            pltpu.VMEM((LAYERS + 1, NY, TOK, PIECE), bf16),
            pltpu.VMEM((NY, STREAM, PIECE), bf16),
            pltpu.VMEM((2, NX, SEQ, GROUP), bf16),
            pltpu.VMEM((LAYERS, 2, NX, SEQ, GROUP), bf16),
            pltpu.VMEM((2, 2, 8, 128), f32),
            pltpu.VMEM((LAYERS, 2, NX, 8, 128), f32),
            pltpu.VMEM((LAYERS, 2, 2, 2, SEQ, HALF), bf16),
            pltpu.VMEM((2, NY, STREAM, PIECE), bf16),
            pltpu.VMEM((2, STREAM, PIECE), f32),
            pltpu.VMEM((LAYERS, 2, NY, STREAM, PIECE), bf16),
            pltpu.VMEM((2, SEQ, 1024), bf16),
            pltpu.VMEM((8, HEAD_DIM), f32),
            pltpu.VMEM((2, 1, WIDTH), f32),
            pltpu.VMEM((NX, 3, SEQ, HEAD_DIM), f32),
            dma((3,)),
            dma((2, 2)),
            dma((2,)),
            dma((LAYERS, PIECES[0], 4)),
            dma((LAYERS, PIECES[1], 4)),
            dma((2,)),
            dma((2, PIECES[0])),
            dma((2, PIECES[1])),
            dma((2,)),
            dma((LAYERS, 2)),
        ]
        + [dma((1,)), dma((2,))]
        + [dma((1,)), dma((NX,))] * 2
        + [dma((2,)), dma((2, NX))] * 5
        + [dma((1,)), dma((2, NX))],
        compiler_params=pltpu.CompilerParams(
            collective_id=0, has_side_effects=True, vmem_limit_bytes=60 * 1024 * 1024
        ),
    )(
        batch_order,
        boundary,
        skip_offset,
        doc_lengths,
        tokens,
        jnp.asarray(frequencies()),
        norm_gain,
        w_query,
        w_key,
        w_value,
        w_out,
    )


def solution(mesh):
    placed = (
        P("dp", None, "tensor"),
        P(None, "pipe", "dp", "tensor"),
        P(None, "pipe", "dp", "tensor"),
        P(None, "pipe", "dp", "tensor"),
        P(None, "pipe", "tensor", "dp"),
        P(None, "pipe", None),
        P("dp"),
        P("dp"),
        P("dp", None),
        P("dp", None),
    )
    return jax.shard_map(
        per_device, mesh=mesh, in_specs=placed, out_specs=P("dp", "pipe", "tensor"), check_vma=False
    )
```
